32 devices in a mesh: seq: 8 (over y, x, core), mp: 4 (over z).
Axes of the slice: x: 2, y: 2, z: 4, core: 2. Of those that a mesh axis runs over, the one named last changes fastest.
Arguments:
- stream: float32 [4096, 2048], P('seq', 'mp'), may hold values from -6 to 6
- doc_starts: int32 [4096], P('seq'), may hold values 0 or 1
- gain_first: float32 [2048], replicated, may hold values from 0.5 to 1.5
- proj_inner: bfloat16 [2048, 2560], P(None, 'mp'), may hold values from -0.125 to 0.125
- proj_gate: bfloat16 [2048, 2560], P(None, 'mp'), may hold values from -0.125 to 0.125
- conv_weight: float32 [4, 2560], P(None, 'mp'), may hold values from -3 to 3
- conv_bias: float32 [2560], P('mp'), may hold values from -3 to 3
- gate_recur: bfloat16 [16, 160, 160], P('mp'), may hold values from -0.5 to 0.5
- gate_input: bfloat16 [16, 160, 160], P('mp'), may hold values from -0.5 to 0.5
- bias_recur: float32 [2560], P('mp'), may hold values from -3 to 3
- bias_input: float32 [2560], P('mp'), may hold values from -3 to 3
- decay_param: float32 [2560], P('mp'), may hold values from 3.4 to 15, as said below
- proj_out: bfloat16 [2560, 2048], P('mp'), may hold values from -0.25 to 0.25
- gain_second: float32 [2048], replicated, may hold values from 0.5 to 1.5
- mlp_gate: bfloat16 [2048, 6144], P(None, 'mp'), may hold values from -0.125 to 0.125
- mlp_up: bfloat16 [2048, 6144], P(None, 'mp'), may hold values from -0.125 to 0.125
- mlp_down: bfloat16 [6144, 2048], P('mp'), may hold values from -0.15625 to 0.15625
- cotangent: float32 [4096, 2048], P('seq', 'mp'), may hold values from -6 to 6
Outputs:
- output: float32 [4096, 2048], P('seq', 'mp')
- grad_stream: float32 [4096, 2048], P('seq', 'mp')
- grad_gain_first: float32 [2048], replicated
- grad_proj_inner: float32 [2048, 2560], P('seq', 'mp')
- grad_proj_gate: float32 [2048, 2560], P('seq', 'mp')
- grad_conv_weight: float32 [4, 2560], P(None, 'mp')
- grad_conv_bias: float32 [2560], P('mp')
- grad_gate_recur: float32 [16, 160, 160], P('mp')
- grad_gate_input: float32 [16, 160, 160], P('mp')
- grad_bias_recur: float32 [2560], P('mp')
- grad_bias_input: float32 [2560], P('mp')
- grad_decay: float32 [2560], P('mp')
- grad_proj_out: float32 [2560, 2048], P(('mp', 'seq'))
- grad_gain_second: float32 [2048], replicated
- grad_mlp_gate: float32 [2048, 6144], P('seq', 'mp')
- grad_mlp_up: float32 [2048, 6144], P('seq', 'mp')
- grad_mlp_down: float32 [6144, 2048], P(('mp', 'seq'))
The draws below stay inside these ranges and needn't reach their ends.
Inputs may be any that keep to these rules, and one draw needn't show every extreme that they name: decay_param is -log(exp(q) - 1) for a per-channel rate q between 0.05 / 4096 and 0.03. `doc_starts`: a 1 marks the first token of a document.
All inputs are finite; a program needn't handle non-finite values. No bound on the sum of `doc_starts` on one device may be relied on, other than what follows from the above.
Results may differ from the reference program's by a relative error of at most 0.0089.
Values sent between devices are 32-bit elements; how exact they have to be, the bound alone decides.
No kernel may reach another device: no remote copies, remote signals or barrier semaphores. Data moves between devices by JAX's collectives and lax.ppermute only.
A program may use at most 256 MiB of HBM per device.

```python
from functools import partial
import jax
import jax.numpy as jnp
from jax import lax

D = 2048
R = 2560
FF = 6144
BLOCKS = 16
CONV = 4
BW = 160
TOK = 512
TOKENS = 4096


def draw_decay_param(key, part):
    key_pick, key_slow, key_fast = jax.random.split(jax.random.fold_in(key, 17), 3)
    share = 0.5
    slow = jax.random.uniform(key_pick, (R,), jnp.float32) < share
    bottom = jnp.log(0.05 / TOKENS)
    middle = jnp.log(0.5 / TOKENS)
    top = jnp.log(0.03)
    slow_rate = jax.random.uniform(key_slow, (R,), jnp.float32, minval=bottom, maxval=middle)
    fast_rate = jax.random.uniform(key_fast, (R,), jnp.float32, minval=middle, maxval=top)
    rate = jnp.exp(jnp.where(slow, slow_rate, fast_rate))
    return (-jnp.log(jnp.expm1(rate))).astype(jnp.float32)


def touch_ends(entries, key, smallest, largest):
    dims = entries.shape
    place = [jax.random.randint(jax.random.fold_in(key, axis), (), 0, dims[axis]) for axis in range(len(dims))]
    entries = entries.at[tuple(place)].set(smallest)
    longest = dims.index(max(dims))
    place[longest] = (place[longest] + 1) % dims[longest]
    return entries.at[tuple(place)].set(largest)


def block_scale(stream_key, extent, shards, low, top_value):
    loudness = 1.0
    for dim, shards_of in shards:
        draws = jax.random.uniform(jax.random.fold_in(jax.random.fold_in(stream_key, 6), dim), (shards_of,), jnp.float32, low / len(shards), top_value / len(shards))
        loudness = loudness * jnp.repeat(jnp.exp(draws), extent[dim] // shards_of).reshape((-1,) + (1,) * (len(extent) - 1 - dim))
    return loudness


def noise(key, dims, deviation, limit, cuts=(), held_as=jnp.bfloat16):
    entries = jax.random.normal(key, dims, jnp.float32) * deviation
    if len(cuts) > 0:
        entries = block_scale(key, dims, cuts, -0.22, 0.18) * entries
    return jnp.clip(entries, min=-limit, max=limit).astype(held_as)


def setup_inputs(seed: int = 0) -> dict:
    key_of = jax.random.split(jax.random.key(seed), 19)
    stream = noise(key_of[0], (TOKENS, D), 1.0, 6.0, ((0, 8), (1, 4)), jnp.float32)
    doc_starts = touch_ends((jax.random.randint(key_of[1], (TOKENS,), 0, 4 * TOK) < 1).astype(jnp.int32), jax.random.fold_in(key_of[1], 1), 0, 1)
    gain_first = jnp.clip(1.0 + 0.1 * jax.random.normal(key_of[2], (D,), jnp.float32), 0.5, 1.5)
    proj_inner = noise(key_of[3], (D, R), D ** -0.5, 0.125, ((1, 4),))
    proj_gate = noise(key_of[4], (D, R), D ** -0.5, 0.125, ((1, 4),))
    conv_weight = noise(key_of[5], (CONV, R), CONV ** -0.5, 3.0, ((1, 4),), jnp.float32)
    conv_bias = noise(key_of[6], (R,), 0.5, 3.0, ((0, 4),), jnp.float32)
    gate_recur = noise(key_of[7], (BLOCKS, BW, BW), BW ** -0.5, 0.5, ((0, 4),))
    gate_input = noise(key_of[8], (BLOCKS, BW, BW), BW ** -0.5, 0.5, ((0, 4),))
    bias_recur = noise(key_of[9], (R,), 0.5, 3.0, ((0, 4),), jnp.float32)
    bias_input = noise(key_of[10], (R,), 0.5, 3.0, ((0, 4),), jnp.float32)
    decay_param = draw_decay_param(jax.random.fold_in(key_of[18], 71), 0)
    proj_out = noise(key_of[12], (R, D), (R // 4) ** -0.5, 0.25, ((0, 4),))
    gain_second = jnp.clip(1.0 + 0.1 * jax.random.normal(key_of[13], (D,), jnp.float32), 0.5, 1.5)
    mlp_gate = noise(key_of[14], (D, FF), D ** -0.5, 0.125, ((1, 4),))
    mlp_up = noise(key_of[15], (D, FF), D ** -0.5, 0.125, ((1, 4),))
    mlp_down = noise(key_of[16], (FF, D), (FF // 4) ** -0.5, 0.15625, ((0, 4),))
    cotangent = noise(key_of[17], (TOKENS, D), 1.0, 6.0, ((0, 8), (1, 4)), jnp.float32)
    return dict(stream=stream, doc_starts=doc_starts, gain_first=gain_first, proj_inner=proj_inner, proj_gate=proj_gate, conv_weight=conv_weight, conv_bias=conv_bias, gate_recur=gate_recur, gate_input=gate_input, bias_recur=bias_recur, bias_input=bias_input, decay_param=decay_param, proj_out=proj_out, gain_second=gain_second, mlp_gate=mlp_gate, mlp_up=mlp_up, mlp_down=mlp_down, cotangent=cotangent)


@jax.custom_vjp
def low(v):
    return lax.optimization_barrier(v.astype(jnp.bfloat16)).astype(jnp.float32)

@jax.custom_vjp
def low_back(v):
    return v

def low_keep(v):
    return (low(v), None)

def low_pass(kept, grad):
    return (grad,)

def back_keep(v):
    return (v, None)

def back_low(kept, grad):
    return (low(grad),)
low.defvjp(low_keep, low_pass)
low_back.defvjp(back_keep, back_low)
recur_scale = 8.0
norm_eps = 1e-06

def norm_rows(rows, gain):
    return rows * lax.rsqrt(lax.optimization_barrier(jnp.mean(rows * rows, axis=-1, keepdims=True)) + norm_eps) * gain

def matmul(left, right):
    return jnp.dot(left, right, precision=lax.Precision.HIGHEST, preferred_element_type=jnp.float32)

def block_apply(values, weights):
    count = values.shape[0]
    groups = weights.shape[0]
    width = weights.shape[1]
    split = values.reshape(count, groups, width)
    mixed = jnp.einsum('tbi,bio->tbo', split, weights, precision=lax.Precision.HIGHEST)
    return mixed.reshape(count, groups * width)

def link(earlier, later):
    return (later[0] * earlier[0], later[0] * earlier[1] + later[1])

def local_scan(starts, conv_out, recur_pre, input_pre, decay):
    recur = jax.nn.sigmoid(recur_pre)
    entry = jax.nn.sigmoid(input_pre)
    log_decay = -recur_scale * recur * jax.nn.softplus(-decay)
    factor = starts + (1.0 - starts) * jnp.sqrt(-jnp.expm1(2.0 * log_decay))
    carry = jnp.exp(log_decay) * (1.0 - starts)
    fresh = factor * entry * conv_out
    return lax.associative_scan(link, (carry, fresh), axis=0)

def shifted(values, lag, fill):
    head = jnp.full((lag,) + values.shape[1:], fill, values.dtype)
    return jnp.concatenate([head, values[:values.shape[0] - lag]], 0)

def forward(starts, stream, gain_first, proj_inner, proj_gate, conv_weight, conv_bias, gate_recur, gate_input, bias_recur, bias_input, decay_param, proj_out, gain_second, mlp_gate, mlp_up, mlp_down):
    first_low = low(norm_rows(stream, gain_first))
    inner = low_back(matmul(first_low, proj_inner))
    gate_pre = low_back(matmul(first_low, proj_gate))
    keep = 1.0 - starts
    conv_out = conv_weight[0] * inner
    valid = jnp.ones_like(keep)
    for k in range(1, CONV):
        valid = valid * shifted(keep, k - 1, 1.0)
        conv_out = conv_out + conv_weight[k] * shifted(inner, k, 0.0) * valid
    conv_out = conv_out + conv_bias
    conv_low = low(conv_out)
    recur_pre = low_back(block_apply(conv_low, gate_recur) + bias_recur)
    input_pre = low_back(block_apply(conv_low, gate_input) + bias_input)
    spans, states = local_scan(starts, conv_out, recur_pre, input_pre, decay_param)
    mixed = low(jax.nn.gelu(gate_pre) * states)
    resid = stream + low_back(matmul(mixed, proj_out))
    second_low = low(norm_rows(resid, gain_second))
    ffn_gate = low_back(matmul(second_low, mlp_gate))
    ffn_up = low_back(matmul(second_low, mlp_up))
    hidden = low(jax.nn.gelu(ffn_gate) * ffn_up)
    return resid + low_back(matmul(hidden, mlp_down))

def reference(stream, doc_starts, gain_first, proj_inner, proj_gate, conv_weight, conv_bias, gate_recur, gate_input, bias_recur, bias_input, decay_param, proj_out, gain_second, mlp_gate, mlp_up, mlp_down, cotangent):
    starts = doc_starts.astype(jnp.float32)[:, None]
    primals = (stream, gain_first, proj_inner.astype(jnp.float32), proj_gate.astype(jnp.float32), conv_weight, conv_bias, gate_recur.astype(jnp.float32), gate_input.astype(jnp.float32), bias_recur, bias_input, decay_param, proj_out.astype(jnp.float32), gain_second, mlp_gate.astype(jnp.float32), mlp_up.astype(jnp.float32), mlp_down.astype(jnp.float32))
    output, backward = jax.vjp(partial(forward, starts), *primals)
    grads = backward(cotangent)
    return (output, grads[0], grads[1], grads[2], grads[3], grads[4], grads[5], grads[6], grads[7], grads[8], grads[9], grads[10], grads[11], grads[12], grads[13], grads[14], grads[15])
```

```python
from functools import partial

import jax
import jax.numpy as jnp
from jax import lax
from jax.experimental import pallas as pl
from jax.experimental.pallas import tpu as pltpu
from jax.sharding import PartitionSpec as P

recur_scale = 8.0
norm_eps = 1e-06
bf16 = jnp.bfloat16
f32 = jnp.float32
LANES = 128
SUB = 8
ROWS = 32
VMEM_LIMIT = 50 * 1024 * 1024


def matmul(left, right):
    return jnp.dot(left, right, preferred_element_type=f32)


def matmul_nt(left, right):
    return lax.dot_general(left, right, (((1,), (1,)), ((), ())), preferred_element_type=f32)


def matmul_tn(left, right):
    return lax.dot_general(left, right, (((0,), (0,)), ((), ())), preferred_element_type=f32)


PAIRS = ((0, 1), (1, 0), (2, 3), (3, 2))
MIDDLE = ((1, 2), (2, 1))
OUTWARD = ((1, 0), (2, 3))
INWARD = ((0, 1), (3, 2))
CROSS = ((0, 2), (2, 0), (1, 3), (3, 1))


def over_mp(value, pairs):
    return lax.ppermute(value, "mp", list(pairs))


def line_places():
    mine = lax.axis_index("mp")
    half = mine >> 1
    return mine, mine ^ 1, 2 - half, 3 - 3 * half


def line_gather(own):
    beside = over_mp(own, PAIRS)
    near_in = over_mp(own, MIDDLE)
    near_out = over_mp(near_in, OUTWARD)
    far_in = over_mp(beside, MIDDLE)
    far_out = over_mp(far_in, OUTWARD)
    return own, beside, near_in + near_out, far_in + far_out


def line_scatter(piece):
    mine, beside, near, far = line_places()
    far_part = piece(far)
    far_one = over_mp(far_part, INWARD)
    far_two = over_mp(far_part + far_one, MIDDLE)
    near_part = piece(near)
    near_one = over_mp(near_part, INWARD)
    near_two = over_mp(near_part + near_one, MIDDLE)
    last = over_mp(piece(beside) + far_two, PAIRS)
    return piece(mine) + near_two + last


def line_sum(value):
    value = value + over_mp(value, PAIRS)
    return value + over_mp(value, CROSS)


def assemble(pieces, width, turn):
    rows, own_width = pieces[0].shape
    whole = jnp.zeros((rows, width), bf16)
    for piece, place in zip(pieces, line_places()):
        start = place * own_width
        whole = lax.dynamic_update_slice(whole, turn(piece, start).astype(bf16), (0, start))
    return whole


def wide(value, width):
    return jnp.concatenate([value] * (width // LANES), axis=-1)


def neg_expm1(x, e):
    poly = 1.0 / 40320.0
    for term in (5040.0, 720.0, 120.0, 24.0, 6.0, 2.0, 1.0):
        poly = poly * x + 1.0 / term
    return jnp.where(x > -0.5, -x * poly, 1.0 - e)


def gelu_parts(x):
    scale = 0.7978845608028654
    cube = 0.044715
    squared = x * x
    t = jnp.tanh(scale * (x + cube * x * squared))
    half = 0.5 * (1.0 + t)
    slope = half + 0.5 * x * (1.0 - t * t) * scale * (1.0 + 3.0 * cube * squared)
    return half * x, slope


def group_scan(a, b):
    place = lax.broadcasted_iota(jnp.int32, a.shape, 1)
    for k in (1, 2, 4):
        fits = place >= k
        b = jnp.where(fits, a * pltpu.roll(b, k, 1) + b, b)
        a = jnp.where(fits, a * pltpu.roll(a, k, 1), a)
    return a, b


def group_scan_back(a, b):
    place = lax.broadcasted_iota(jnp.int32, a.shape, 1)
    for k in (1, 2, 4):
        fits = place < SUB - k
        b = jnp.where(fits, a * pltpu.roll(b, SUB - k, 1) + b, b)
        a = jnp.where(fits, a * pltpu.roll(a, SUB - k, 1), a)
    return a, b


def forward_kernel(
    inner_ref, halo_ref, valid_ref, row_ref, gate_ref,
    conv_ref, low_ref, rg_ref, ig_ref, alpha_ref, factor_ref, part_ref, span_ref, last_ref,
    ext_ref, pre_ref,
):
    count, width = inner_ref.shape
    ext_ref[pl.ds(0, SUB), :] = halo_ref[...]

    def fill(i, _):
        r = pl.multiple_of(i * ROWS, ROWS)
        ext_ref[pl.ds(r + SUB, ROWS), :] = inner_ref[pl.ds(r, ROWS), :]
        return 0

    lax.fori_loop(0, count // ROWS, fill, 0)

    def convolve(i, _):
        r = pl.multiple_of(i * ROWS, ROWS)
        window = ext_ref[pl.ds(r, ROWS + SUB), :]
        total = row_ref[0:1, :] * window[SUB:]
        for k in range(1, 4):
            valid = wide(valid_ref[k, pl.ds(r, ROWS), :], width)
            total = total + row_ref[k : k + 1, :] * window[SUB - k : SUB - k + ROWS] * valid
        total = total + row_ref[4:5, :]
        conv_ref[pl.ds(r, ROWS), :] = total
        low_ref[pl.ds(r, ROWS), :] = total.astype(bf16)
        return 0

    lax.fori_loop(0, count // ROWS, convolve, 0)
    pre_ref[...] = jnp.dot(low_ref[...], gate_ref[...], preferred_element_type=f32)

    def scan(i, carry):
        r = pl.multiple_of(i * ROWS, ROWS)
        here = pl.ds(r, ROWS)
        rg = jax.nn.sigmoid(pre_ref[here, :width] + row_ref[5:6, :])
        ig = jax.nn.sigmoid(pre_ref[here, width:] + row_ref[6:7, :])
        log_a = row_ref[7:8, :] * rg
        keep = wide(valid_ref[0, here, :], width)
        a = jnp.exp(log_a)
        root = jnp.sqrt(neg_expm1(2.0 * log_a, a * a))
        factor = (1.0 - keep) + keep * root
        alpha = a * keep
        beta = factor * ig * conv_ref[here, :]
        rg_ref[here, :] = rg
        ig_ref[here, :] = ig
        alpha_ref[here, :] = alpha
        factor_ref[here, :] = factor
        groups = (ROWS // SUB, SUB, width)
        a3, b3 = group_scan(alpha.reshape(groups), beta.reshape(groups))
        state, product = carry
        for g in range(ROWS // SUB):
            part = b3[g] + a3[g] * state
            span = a3[g] * product
            part_ref[pl.ds(r + g * SUB, SUB), :] = part
            span_ref[pl.ds(r + g * SUB, SUB), :] = span
            state, product = part[SUB - 1 : SUB, :], span[SUB - 1 : SUB, :]
        return state, product

    zero = jnp.zeros((1, width), f32)
    state, product = lax.fori_loop(0, count // ROWS, scan, (zero, zero + 1.0))
    last_ref[...] = jnp.concatenate([product, state, jnp.zeros((SUB - 2, width), f32)], 0)


def state_kernel(
    mine_ref, ends_ref, part_ref, span_ref, gate_ref, states_ref, mixed_ref, enter_ref
):
    devices = ends_ref.shape[0]
    width = part_ref.shape[1]
    entering = jnp.zeros((1, width), f32)
    for d in range(devices):
        ends = ends_ref[d]
        entering = jnp.where(d < mine_ref[0], ends[0:1, :] * entering + ends[1:2, :], entering)
    states = span_ref[...] * entering + part_ref[...]
    states_ref[...] = states
    mixed_ref[...] = (gelu_parts(gate_ref[...])[0] * states).astype(bf16)
    enter_ref[...] = jnp.broadcast_to(entering, enter_ref.shape)


def turn_kernel(
    dmixed_ref, gate_ref, states_ref, span_ref, dstates_ref, dgate_ref, out_ref
):
    act, slope = gelu_parts(gate_ref[...])
    dmixed = dmixed_ref[...]
    dstates = dmixed * act
    dstates_ref[...] = dstates
    dgate_ref[...] = (dmixed * states_ref[...] * slope).astype(bf16)

    @pl.when(pl.program_id(0) == 0)
    def _():
        out_ref[...] = jnp.zeros_like(out_ref)

    out_ref[...] += jnp.sum(
        (dstates * span_ref[...]).reshape(-1, SUB, dstates.shape[1]), axis=0
    )


def backward_kernel(
    mine_ref, ends_ref, dstates_ref, alpha_ref, states_ref, enter_ref, conv_ref, rg_ref, ig_ref,
    factor_ref, valid_ref, inner_ref, halo_ref, row_ref, gate_ref,
    dinner_ref, tail_ref, head_ref, drec_ref, sums_ref,
    dconv_ref, ext_ref,
):
    devices = ends_ref.shape[0]
    count, width = alpha_ref.shape
    blocks = count // ROWS
    incoming = jnp.zeros((1, width), f32)
    for d in reversed(range(devices)):
        ends = ends_ref[d]
        incoming = jnp.where(d > mine_ref[0], ends[0:1, :] * incoming + ends[1:2, :], incoming)
    dconv_ref[pl.ds(0, SUB), :] = jnp.zeros((SUB, width), f32)
    dconv_ref[pl.ds(count + SUB, SUB), :] = jnp.zeros((SUB, width), f32)
    ext_ref[pl.ds(0, SUB), :] = halo_ref[...]
    groups = (ROWS // SUB, SUB, width)
    place = lax.broadcasted_iota(jnp.int32, (SUB, width), 0)

    def fold(value):
        return jnp.sum(value.reshape(groups), axis=0)

    def back(step, carry):
        flow, decay, bias_r, bias_i = carry
        i = blocks - 1 - step
        r = pl.multiple_of(i * ROWS, ROWS)
        here = pl.ds(r, ROWS)
        ext_ref[pl.ds(r + SUB, ROWS), :] = inner_ref[here, :]
        alpha = alpha_ref[here, :]
        dstates = dstates_ref[here, :]
        a3, b3 = group_scan_back(alpha.reshape(groups), (alpha * dstates).reshape(groups))
        d3 = dstates.reshape(groups)
        totals = [None] * (ROWS // SUB)
        for g in reversed(range(ROWS // SUB)):
            flows = b3[g] + a3[g] * flow
            later = jnp.where(place == SUB - 1, flow, pltpu.roll(flows, SUB - 1, 0))
            totals[g] = d3[g] + later
            flow = flows[0:1, :]
        total = jnp.concatenate(totals, 0)
        before = pl.multiple_of(jnp.maximum(r - SUB, 0), SUB)
        first = jnp.where(i == 0, enter_ref[...], states_ref[pl.ds(before, SUB), :])
        window = jnp.concatenate([first, states_ref[here, :]], 0)
        prior = window[SUB - 1 : SUB - 1 + ROWS]
        rg = rg_ref[here, :]
        ig = ig_ref[here, :]
        factor = factor_ref[here, :]
        conv = conv_ref[here, :]
        gain = total * factor
        dconv_ref[pl.ds(r + SUB, ROWS), :] = gain * ig
        dinput = (gain * conv * ig * (1.0 - ig)).astype(bf16)
        dlog = alpha * (total * prior - total * ig * conv * alpha / factor)
        drecur = (dlog * row_ref[7:8, :] * rg * (1.0 - rg)).astype(bf16)
        drec_ref[here, :width] = drecur
        drec_ref[here, width:] = dinput
        return (
            flow,
            decay + fold(dlog * rg),
            bias_r + fold(drecur.astype(f32)),
            bias_i + fold(dinput.astype(f32)),
        )

    zero = jnp.zeros((SUB, width), f32)
    _, decay, bias_r, bias_i = lax.fori_loop(0, blocks, back, (incoming, zero, zero, zero))
    dconv_ref[pl.ds(SUB, count), :] += lax.dot_general(
        drec_ref[...], gate_ref[...], (((1,), (1,)), ((), ())), preferred_element_type=f32
    )

    def spread_back(window, r, rows):
        total = row_ref[0:1, :] * window[:rows]
        for k in range(1, 4):
            valid = wide(valid_ref[k, pl.ds(r, rows + SUB), :], width)
            total = total + row_ref[k : k + 1, :] * (window * valid)[k : k + rows]
        return total

    head_ref[...] = spread_back(dconv_ref[pl.ds(0, 2 * SUB), :], 0, SUB)

    def finish(i, carry):
        r = pl.multiple_of(i * ROWS, ROWS)
        window = dconv_ref[pl.ds(r + SUB, ROWS + SUB), :]
        total = spread_back(window, r + SUB, ROWS)
        dinner_ref[pl.ds(r, ROWS), :] = total.astype(bf16)

        @pl.when(i == blocks - 1)
        def _():
            tail_ref[...] = total[ROWS - 2 * SUB :]

        dconv = window[:ROWS]
        inputs = ext_ref[pl.ds(r, ROWS + SUB), :]
        sums = [fold(dconv * inputs[SUB:])]
        for k in range(1, 4):
            valid = wide(valid_ref[k, pl.ds(r + SUB, ROWS), :], width)
            sums.append(fold(dconv * valid * inputs[SUB - k : SUB - k + ROWS]))
        sums.append(fold(dconv))
        return tuple(c + s for c, s in zip(carry, sums))

    sums = lax.fori_loop(0, blocks, finish, (zero,) * 5)
    sums_ref[...] = jnp.concatenate(
        [jnp.sum(s, axis=0, keepdims=True) for s in (*sums, bias_r, bias_i, decay)], 0
    )


def vmem(count=1):
    return [pl.BlockSpec(memory_space=pltpu.VMEM)] * count


def shape(dims, kind=f32):
    return jax.ShapeDtypeStruct(dims, kind)


def cost(flops, moved, special=0):
    return pl.CostEstimate(flops=flops, bytes_accessed=moved, transcendentals=special)


def run_forward(inner, halo, valid, rows, gates):
    count, width = inner.shape
    full = shape((count, width))
    return pl.pallas_call(
        forward_kernel,
        out_shape=(full, shape((count, width), bf16)) + (full,) * 6 + (shape((SUB, width)),),
        in_specs=vmem(5),
        out_specs=tuple(vmem(9)),
        scratch_shapes=[
            pltpu.VMEM((count + SUB, width), f32),
            pltpu.VMEM((count, 2 * width), f32),
        ],
        compiler_params=pltpu.CompilerParams(vmem_limit_bytes=VMEM_LIMIT),
        cost_estimate=cost(4 * count * width * width, 36 * count * width, 5 * count * width),
        name="recurrence_forward",
    )(inner, halo, valid, rows, gates)


def run_states(mine, ends, part, span, gate_pre):
    count, width = part.shape
    block = count // 4
    tile = pl.BlockSpec((block, width), lambda i: (i, 0))
    return pl.pallas_call(
        state_kernel,
        grid=(4,),
        out_shape=(
            shape((count, width)), shape((count, width), bf16), shape((SUB, width)),
        ),
        in_specs=[
            pl.BlockSpec(memory_space=pltpu.SMEM),
            pl.BlockSpec(ends.shape, lambda i: (0, 0, 0)),
            tile, tile, tile,
        ],
        out_specs=(tile, tile, pl.BlockSpec((SUB, width), lambda i: (0, 0))),
        compiler_params=pltpu.CompilerParams(vmem_limit_bytes=VMEM_LIMIT),
        cost_estimate=cost(20 * count * width, 18 * count * width, count * width),
        name="recurrence_states",
    )(mine, ends, part, span, gate_pre)


def run_turn(dmixed, gate_pre, states, span):
    count, width = dmixed.shape
    block = count // 4
    tile = pl.BlockSpec((block, width), lambda i: (i, 0))
    return pl.pallas_call(
        turn_kernel,
        grid=(4,),
        out_shape=(
            shape((count, width)), shape((count, width), bf16), shape((SUB, width)),
        ),
        in_specs=[tile] * 4,
        out_specs=(tile, tile, pl.BlockSpec((SUB, width), lambda i: (0, 0))),
        compiler_params=pltpu.CompilerParams(vmem_limit_bytes=VMEM_LIMIT),
        cost_estimate=cost(30 * count * width, 22 * count * width, count * width),
        name="recurrence_turn",
    )(dmixed, gate_pre, states, span)


def run_backward(mine, ends, dstates, saved, enter, valid, inner, halo, rows, gates):
    count, width = dstates.shape
    return pl.pallas_call(
        backward_kernel,
        out_shape=(
            shape((count, width), bf16), shape((2 * SUB, width)), shape((SUB, width)),
            shape((count, 2 * width), bf16), shape((SUB, width)),
        ),
        in_specs=[pl.BlockSpec(memory_space=pltpu.SMEM)] + vmem(14),
        out_specs=tuple(vmem(5)),
        scratch_shapes=[
            pltpu.VMEM((count + 2 * SUB, width), f32),
            pltpu.VMEM((count + SUB, width), f32),
        ],
        compiler_params=pltpu.CompilerParams(vmem_limit_bytes=VMEM_LIMIT),
        cost_estimate=cost(4 * count * width * width, 40 * count * width, count * width),
        name="recurrence_backward",
    )(
        mine, ends, dstates, saved["alpha"], saved["states"], enter, saved["conv"], saved["rg"],
        saved["ig"], saved["factor"], valid, inner, halo, rows, gates,
    )


def block_diagonal(weights):
    groups, width, _ = weights.shape
    rows = [
        jnp.pad(weights[b], ((0, 0), (b * width, (groups - 1 - b) * width))) for b in range(groups)
    ]
    return jnp.concatenate(rows, 0)


def diagonal_blocks(whole, groups):
    width = whole.shape[0] // groups
    return jnp.stack(
        [
            whole[b * width : (b + 1) * width, b * width : (b + 1) * width]
            for b in range(groups)
        ],
        0,
    )


def row_scale(squares, features):
    return lax.rsqrt(squares / features + norm_eps)[:, None]


def body(
    stream, doc_starts, gain_first, proj_inner, proj_gate, conv_weight, conv_bias, gate_recur,
    gate_input, bias_recur, bias_input, decay_param, proj_out, gain_second, mlp_gate, mlp_up,
    mlp_down, cotangent,
):
    count, own_width = stream.shape
    features = gain_first.shape[0]
    inner_width = proj_inner.shape[1]
    ffn_width = mlp_gate.shape[1]
    groups = gate_recur.shape[0]
    devices = lax.axis_size("seq")
    seq_at = lax.axis_index("seq").astype(jnp.int32).reshape(1)
    column = lax.axis_index("mp") * own_width
    own_first = lax.dynamic_slice_in_dim(gain_first, column, own_width)
    own_second = lax.dynamic_slice_in_dim(gain_second, column, own_width)
    onward = [(s, s + 1) for s in range(devices - 1)]
    backward = [(s + 1, s) for s in range(devices - 1)]

    stream_pieces = line_gather(stream)
    first_scale = row_scale(line_sum(jnp.sum(stream * stream, axis=1)), features)
    starts_row = jnp.zeros((own_width,), f32).at[:SUB].set(doc_starts[count - SUB :].astype(f32))
    payload = jnp.concatenate(
        [stream[count - SUB :], jnp.broadcast_to(starts_row, (SUB, own_width))], 0
    )
    payload = lax.ppermute(payload, "seq", onward)
    before = lax.all_gather(payload, "mp", axis=1, tiled=True)
    halo_rows = before[:SUB]
    halo_scale = row_scale(jnp.sum(halo_rows * halo_rows, axis=1), features)
    halo_low = (halo_rows * halo_scale * gain_first).astype(bf16)
    keep_ext = jnp.concatenate([1.0 - before[SUB, :SUB], 1.0 - doc_starts.astype(f32)], 0)
    reach = [keep_ext[SUB:]]
    for k in range(1, 4):
        reach.append(
            (reach[-1] if k > 1 else 1.0) * keep_ext[SUB - k + 1 : SUB - k + 1 + count]
        )
    valid = jnp.broadcast_to(jnp.stack(reach, 0)[:, :, None], (4, count, LANES))
    valid_pad = jnp.pad(valid, ((0, 0), (SUB, SUB), (0, 0)))
    rows = jnp.stack(
        [
            conv_weight[0], conv_weight[1], conv_weight[2], conv_weight[3], conv_bias, bias_recur,
            bias_input, -recur_scale * jax.nn.softplus(-decay_param),
        ],
        0,
    )
    gates = jnp.concatenate([block_diagonal(gate_recur), block_diagonal(gate_input)], 1)

    def first_turn(piece, start):
        return piece * first_scale * lax.dynamic_slice_in_dim(gain_first, start, own_width)

    first_low = assemble(stream_pieces, features, first_turn)
    inner = matmul(first_low, proj_inner)
    halo = matmul(halo_low, proj_inner)
    conv, conv_low, rg, ig, alpha, factor, part, span, last = run_forward(
        inner, halo, valid, rows, gates
    )
    gate_pre = matmul(first_low, proj_gate)
    ends = lax.all_gather(last, "seq")
    states, mixed_low, enter = run_states(seq_at, ends, part, span, gate_pre)

    branch = matmul(mixed_low, proj_out)
    own_resid = stream + line_scatter(
        lambda place: lax.dynamic_slice_in_dim(branch, place * own_width, own_width, 1)
    )
    cot_pieces = line_gather(cotangent)
    cot_low = assemble(cot_pieces, features, lambda piece, start: piece)

    resid_pieces = line_gather(own_resid)
    second_scale = row_scale(line_sum(jnp.sum(own_resid * own_resid, axis=1)), features)

    def second_turn(piece, start):
        return piece * second_scale * lax.dynamic_slice_in_dim(gain_second, start, own_width)

    second_low = assemble(resid_pieces, features, second_turn)
    ffn_weight = jnp.concatenate([mlp_gate, mlp_up], 1)
    ffn = matmul(second_low, ffn_weight)
    act, slope = gelu_parts(ffn[:, :ffn_width])
    ffn_up = ffn[:, ffn_width:]
    hidden_low = (act * ffn_up).astype(bf16)
    d_hidden = matmul_nt(cot_low, mlp_down)
    d_pair_low = jnp.concatenate([d_hidden * ffn_up * slope, d_hidden * act], 1).astype(bf16)
    d_second_part = matmul_nt(d_pair_low, ffn_weight)
    own_d_second = line_scatter(
        lambda place: lax.dynamic_slice_in_dim(d_second_part, place * own_width, own_width, 1)
    )
    second_product = d_second_part * second_low.astype(f32)
    second_mean = line_sum(jnp.sum(second_product, axis=1)) / features
    d_gain_second = jnp.sum(second_product, axis=0) / gain_second
    own_d_resid = (
        cotangent
        + second_scale * (own_second * own_d_second)
        - own_resid * (second_scale * second_scale * second_mean[:, None])
    )
    branch_pieces = line_gather(own_d_resid)
    branch_low = assemble(branch_pieces, features, lambda piece, start: piece)

    mlp_part = matmul(hidden_low, mlp_down)
    output = own_resid + line_scatter(
        lambda place: lax.dynamic_slice_in_dim(mlp_part, place * own_width, own_width, 1)
    )

    d_mixed = matmul_nt(branch_low, proj_out)
    d_states, d_gate_low, outgoing = run_turn(d_mixed, gate_pre, states, span)
    leaving = jnp.stack([last[0], jnp.sum(outgoing, axis=0)], 0)
    back_ends = lax.all_gather(leaving, "seq")
    saved = dict(alpha=alpha, states=states, conv=conv, rg=rg, ig=ig, factor=factor)
    d_inner_low, tail, head, d_rec_low, sums = run_backward(
        seq_at, back_ends, d_states, saved, enter, valid_pad, inner, halo, rows, gates
    )
    returned = lax.ppermute(head, "seq", backward)
    tail = tail + jnp.concatenate([jnp.zeros_like(returned), returned], 0)
    d_inner_low = lax.dynamic_update_slice(d_inner_low, tail.astype(bf16), (count - 2 * SUB, 0))

    d_first_part = matmul_nt(d_inner_low, proj_inner) + matmul_nt(d_gate_low, proj_gate)
    own_d_first = line_scatter(
        lambda place: lax.dynamic_slice_in_dim(d_first_part, place * own_width, own_width, 1)
    )
    first_product = d_first_part * first_low.astype(f32)
    first_mean = line_sum(jnp.sum(first_product, axis=1)) / features
    d_gain_first = jnp.sum(first_product, axis=0) / gain_first
    grad_stream = (
        own_d_resid
        + first_scale * (own_first * own_d_first)
        - stream * (first_scale * first_scale * first_mean[:, None])
    )

    d_gains = lax.psum((d_gain_first, d_gain_second), ("seq", "mp"))
    gate_grads = matmul_tn(conv_low, d_rec_low)
    sums, grad_gate_recur, grad_gate_input = lax.psum(
        (
            sums,
            diagonal_blocks(gate_grads[:, :inner_width], groups),
            diagonal_blocks(gate_grads[:, inner_width:], groups),
        ),
        "seq",
    )
    grad_decay = sums[7] * (recur_scale * jax.nn.sigmoid(-decay_param))

    def over_seq(value):
        return lax.psum_scatter(value, "seq", scatter_dimension=0, tiled=True)

    grad_down = over_seq(matmul_tn(hidden_low, cot_low))
    grad_pair = over_seq(matmul_tn(second_low, d_pair_low))
    grad_out = over_seq(matmul_tn(mixed_low, branch_low))
    grad_gate = over_seq(matmul_tn(first_low, d_gate_low))
    grad_inner = over_seq(matmul_tn(first_low, d_inner_low))
    return (
        output,
        grad_stream,
        d_gains[0],
        grad_inner,
        grad_gate,
        sums[:4],
        sums[4],
        grad_gate_recur,
        grad_gate_input,
        sums[5],
        sums[6],
        grad_decay,
        grad_out,
        d_gains[1],
        grad_pair[:, :ffn_width],
        grad_pair[:, ffn_width:],
        grad_down,
    )


def solution(mesh):
    in_specs = (
        P("seq", "mp"),
        P("seq"),
        P(),
        P(None, "mp"),
        P(None, "mp"),
        P(None, "mp"),
        P("mp"),
        P("mp", None, None),
        P("mp", None, None),
        P("mp"),
        P("mp"),
        P("mp"),
        P("mp", None),
        P(),
        P(None, "mp"),
        P(None, "mp"),
        P("mp", None),
        P("seq", "mp"),
    )
    out_specs = (
        P("seq", "mp"),
        P("seq", "mp"),
        P(),
        P("seq", "mp"),
        P("seq", "mp"),
        P(None, "mp"),
        P("mp"),
        P("mp", None, None),
        P("mp", None, None),
        P("mp"),
        P("mp"),
        P("mp"),
        P(("mp", "seq"), None),
        P(),
        P("seq", "mp"),
        P("seq", "mp"),
        P(("mp", "seq"), None),
    )
    return jax.shard_map(body, mesh=mesh, in_specs=in_specs, out_specs=out_specs, check_vma=False)
```

```python
from functools import partial

import jax
import jax.numpy as jnp
from jax import lax
from jax.experimental import pallas as pl
from jax.experimental.pallas import tpu as pltpu
from jax.sharding import PartitionSpec as P

recur_scale = 8.0
norm_eps = 1e-06
bf16 = jnp.bfloat16
f32 = jnp.float32
LANES = 128
SUB = 8
ROWS = 32
VMEM_LIMIT = 50 * 1024 * 1024


def matmul(left, right):
    return jnp.dot(left, right, preferred_element_type=f32)


def matmul_nt(left, right):
    return lax.dot_general(left, right, (((1,), (1,)), ((), ())), preferred_element_type=f32)


def matmul_tn(left, right):
    return lax.dot_general(left, right, (((0,), (0,)), ((), ())), preferred_element_type=f32)


PAIRS = ((0, 1), (1, 0), (2, 3), (3, 2))
MIDDLE = ((1, 2), (2, 1))
OUTWARD = ((1, 0), (2, 3))
INWARD = ((0, 1), (3, 2))
CROSS = ((0, 2), (2, 0), (1, 3), (3, 1))


def over_mp(value, pairs):
    return lax.ppermute(value, "mp", list(pairs))


def line_places():
    mine = lax.axis_index("mp")
    half = mine >> 1
    return mine, mine ^ 1, 2 - half, 3 - 3 * half


def after(value, *needed):
    return lax.optimization_barrier((value, needed))[0]


class LineGather:
    def __init__(self, own):
        self.own = own

    def first(self, *needed):
        own = after(self.own, *needed)
        self.beside, self.near_in = over_mp(own, PAIRS), over_mp(own, MIDDLE)
        return self.beside, self.near_in

    def second(self, *needed):
        near, beside = after((self.near_in, self.beside), *needed)
        self.near_out, self.far_in = over_mp(near, OUTWARD), over_mp(beside, MIDDLE)
        return self.near_out, self.far_in

    def third(self, *needed):
        far, _ = after((self.far_in, self.near_out), *needed)
        self.far_out = over_mp(far, OUTWARD)
        return self.far_out

    def pieces(self):
        return self.own, self.beside, self.near_in + self.near_out, self.far_in + self.far_out


class LineScatter:
    def __init__(self, whole, width):
        self.whole, self.width = whole, width
        self.mine, self.beside, self.near, self.far = line_places()

    def piece(self, place):
        return lax.dynamic_slice_in_dim(self.whole, place * self.width, self.width, 1)

    def first(self, *needed):
        self.far_one = over_mp(after(self.piece(self.far), *needed), INWARD)
        return self.far_one

    def second(self, *needed):
        far, near = after(
            (self.piece(self.far) + self.far_one, self.piece(self.near)), *needed
        )
        self.far_two, self.near_one = over_mp(far, MIDDLE), over_mp(near, INWARD)
        return self.far_two, self.near_one

    def third(self, *needed):
        near, last = after(
            (self.piece(self.near) + self.near_one, self.piece(self.beside) + self.far_two), *needed
        )
        self.near_two, self.last = over_mp(near, MIDDLE), over_mp(last, PAIRS)
        return self.near_two, self.last

    def result(self):
        return self.piece(self.mine) + self.near_two + self.last


def line_sum(value):
    value = value + over_mp(value, PAIRS)
    return value + over_mp(value, CROSS)


def swapped(value, axis, bit):
    count = lax.axis_size(axis)
    return lax.ppermute(value, axis, [(d, d ^ bit) for d in range(count)])


def sum_over(value, axis):
    bit = 1
    while bit < lax.axis_size(axis):
        value = value + swapped(value, axis, bit)
        bit *= 2
    return value


def assemble(pieces, width, turn):
    rows, own_width = pieces[0].shape
    whole = jnp.zeros((rows, width), bf16)
    for piece, place in zip(pieces, line_places()):
        start = place * own_width
        whole = lax.dynamic_update_slice(whole, turn(piece, start).astype(bf16), (0, start))
    return whole


def wide(value, width):
    return jnp.concatenate([value] * (width // LANES), axis=-1)


def neg_expm1(x, e):
    poly = 1.0 / 40320.0
    for term in (5040.0, 720.0, 120.0, 24.0, 6.0, 2.0, 1.0):
        poly = poly * x + 1.0 / term
    return jnp.where(x > -0.5, -x * poly, 1.0 - e)


def gelu_parts(x):
    scale = 0.7978845608028654
    cube = 0.044715
    squared = x * x
    t = jnp.tanh(scale * (x + cube * x * squared))
    half = 0.5 * (1.0 + t)
    slope = half + 0.5 * x * (1.0 - t * t) * scale * (1.0 + 3.0 * cube * squared)
    return half * x, slope


def group_scan(a, b):
    place = lax.broadcasted_iota(jnp.int32, a.shape, 1)
    for k in (1, 2, 4):
        fits = place >= k
        b = jnp.where(fits, a * pltpu.roll(b, k, 1) + b, b)
        a = jnp.where(fits, a * pltpu.roll(a, k, 1), a)
    return a, b


def group_scan_back(a, b):
    place = lax.broadcasted_iota(jnp.int32, a.shape, 1)
    for k in (1, 2, 4):
        fits = place < SUB - k
        b = jnp.where(fits, a * pltpu.roll(b, SUB - k, 1) + b, b)
        a = jnp.where(fits, a * pltpu.roll(a, SUB - k, 1), a)
    return a, b


def forward_kernel(
    inner_ref, halo_ref, valid_ref, row_ref, gate_ref,
    conv_ref, low_ref, rg_ref, ig_ref, alpha_ref, factor_ref, part_ref, span_ref, last_ref,
    ext_ref, pre_ref,
):
    count, width = inner_ref.shape
    ext_ref[pl.ds(0, SUB), :] = halo_ref[...]

    def fill(i, _):
        r = pl.multiple_of(i * ROWS, ROWS)
        ext_ref[pl.ds(r + SUB, ROWS), :] = inner_ref[pl.ds(r, ROWS), :]
        return 0

    lax.fori_loop(0, count // ROWS, fill, 0)

    def convolve(i, _):
        r = pl.multiple_of(i * ROWS, ROWS)
        window = ext_ref[pl.ds(r, ROWS + SUB), :]
        total = row_ref[0:1, :] * window[SUB:]
        for k in range(1, 4):
            valid = wide(valid_ref[k, pl.ds(r + SUB, ROWS), :], width)
            total = total + row_ref[k : k + 1, :] * window[SUB - k : SUB - k + ROWS] * valid
        total = total + row_ref[4:5, :]
        conv_ref[pl.ds(r, ROWS), :] = total
        low_ref[pl.ds(r, ROWS), :] = total.astype(bf16)
        return 0

    lax.fori_loop(0, count // ROWS, convolve, 0)
    pre_ref[...] = jnp.dot(low_ref[...], gate_ref[...], preferred_element_type=f32)

    def scan(i, carry):
        r = pl.multiple_of(i * ROWS, ROWS)
        here = pl.ds(r, ROWS)
        rg = jax.nn.sigmoid(pre_ref[here, :width] + row_ref[5:6, :])
        ig = jax.nn.sigmoid(pre_ref[here, width:] + row_ref[6:7, :])
        log_a = row_ref[7:8, :] * rg
        keep = wide(valid_ref[0, pl.ds(r + SUB, ROWS), :], width)
        a = jnp.exp(log_a)
        root = jnp.sqrt(neg_expm1(2.0 * log_a, a * a))
        factor = (1.0 - keep) + keep * root
        alpha = a * keep
        beta = factor * ig * conv_ref[here, :]
        rg_ref[here, :] = rg
        ig_ref[here, :] = ig
        alpha_ref[here, :] = alpha
        factor_ref[here, :] = factor
        groups = (ROWS // SUB, SUB, width)
        a3, b3 = group_scan(alpha.reshape(groups), beta.reshape(groups))
        state, product = carry
        for g in range(ROWS // SUB):
            part = b3[g] + a3[g] * state
            span = a3[g] * product
            part_ref[pl.ds(r + g * SUB, SUB), :] = part
            span_ref[pl.ds(r + g * SUB, SUB), :] = span
            state, product = part[SUB - 1 : SUB, :], span[SUB - 1 : SUB, :]
        return state, product

    zero = jnp.zeros((1, width), f32)
    state, product = lax.fori_loop(0, count // ROWS, scan, (zero, zero + 1.0))
    last_ref[...] = jnp.concatenate([product, state, jnp.zeros((SUB - 2, width), f32)], 0)


def state_kernel(
    mine_ref, ends_ref, part_ref, span_ref, gate_ref, states_ref, mixed_ref, enter_ref
):
    devices = ends_ref.shape[0]
    width = part_ref.shape[1]
    entering = jnp.zeros((1, width), f32)
    for d in range(devices):
        ends = ends_ref[d]
        entering = jnp.where(d < mine_ref[0], ends[0:1, :] * entering + ends[1:2, :], entering)
    states = span_ref[...] * entering + part_ref[...]
    states_ref[...] = states
    mixed_ref[...] = (gelu_parts(gate_ref[...])[0] * states).astype(bf16)
    enter_ref[...] = jnp.broadcast_to(entering, enter_ref.shape)


def turn_kernel(
    dmixed_ref, gate_ref, states_ref, span_ref, dstates_ref, dgate_ref, out_ref
):
    act, slope = gelu_parts(gate_ref[...])
    dmixed = dmixed_ref[...]
    dstates = dmixed * act
    dstates_ref[...] = dstates
    dgate_ref[...] = (dmixed * states_ref[...] * slope).astype(bf16)

    @pl.when(pl.program_id(0) == 0)
    def _():
        out_ref[...] = jnp.zeros_like(out_ref)

    out_ref[...] += jnp.sum(
        (dstates * span_ref[...]).reshape(-1, SUB, dstates.shape[1]), axis=0
    )


def backward_kernel(
    mine_ref, ends_ref, dstates_ref, alpha_ref, states_ref, enter_ref, conv_ref, rg_ref, ig_ref,
    factor_ref, valid_ref, inner_ref, halo_ref, row_ref, gate_ref,
    dinner_ref, tail_ref, head_ref, drec_ref, sums_ref,
    dconv_ref, ext_ref,
):
    devices = ends_ref.shape[0]
    count, width = alpha_ref.shape
    blocks = count // ROWS
    incoming = jnp.zeros((1, width), f32)
    for d in reversed(range(devices)):
        ends = ends_ref[d]
        incoming = jnp.where(d > mine_ref[0], ends[0:1, :] * incoming + ends[1:2, :], incoming)
    dconv_ref[pl.ds(0, SUB), :] = jnp.zeros((SUB, width), f32)
    dconv_ref[pl.ds(count + SUB, SUB), :] = jnp.zeros((SUB, width), f32)
    ext_ref[pl.ds(0, SUB), :] = halo_ref[...]
    groups = (ROWS // SUB, SUB, width)
    place = lax.broadcasted_iota(jnp.int32, (SUB, width), 0)

    def fold(value):
        return jnp.sum(value.reshape(groups), axis=0)

    def back(step, carry):
        flow, decay, bias_r, bias_i = carry
        i = blocks - 1 - step
        r = pl.multiple_of(i * ROWS, ROWS)
        here = pl.ds(r, ROWS)
        ext_ref[pl.ds(r + SUB, ROWS), :] = inner_ref[here, :]
        alpha = alpha_ref[here, :]
        dstates = dstates_ref[here, :]
        a3, b3 = group_scan_back(alpha.reshape(groups), (alpha * dstates).reshape(groups))
        d3 = dstates.reshape(groups)
        totals = [None] * (ROWS // SUB)
        for g in reversed(range(ROWS // SUB)):
            flows = b3[g] + a3[g] * flow
            later = jnp.where(place == SUB - 1, flow, pltpu.roll(flows, SUB - 1, 0))
            totals[g] = d3[g] + later
            flow = flows[0:1, :]
        total = jnp.concatenate(totals, 0)
        before = pl.multiple_of(jnp.maximum(r - SUB, 0), SUB)
        first = jnp.where(i == 0, enter_ref[...], states_ref[pl.ds(before, SUB), :])
        window = jnp.concatenate([first, states_ref[here, :]], 0)
        prior = window[SUB - 1 : SUB - 1 + ROWS]
        rg = rg_ref[here, :]
        ig = ig_ref[here, :]
        factor = factor_ref[here, :]
        conv = conv_ref[here, :]
        gain = total * factor
        dconv_ref[pl.ds(r + SUB, ROWS), :] = gain * ig
        dinput = (gain * conv * ig * (1.0 - ig)).astype(bf16)
        dlog = alpha * (total * prior - total * ig * conv * alpha / factor)
        drecur = (dlog * row_ref[7:8, :] * rg * (1.0 - rg)).astype(bf16)
        drec_ref[here, :width] = drecur
        drec_ref[here, width:] = dinput
        return (
            flow,
            decay + fold(dlog * rg),
            bias_r + fold(drecur.astype(f32)),
            bias_i + fold(dinput.astype(f32)),
        )

    zero = jnp.zeros((SUB, width), f32)
    _, decay, bias_r, bias_i = lax.fori_loop(0, blocks, back, (incoming, zero, zero, zero))
    dconv_ref[pl.ds(SUB, count), :] += lax.dot_general(
        drec_ref[...], gate_ref[...], (((1,), (1,)), ((), ())), preferred_element_type=f32
    )

    def spread_back(window, r, rows):
        total = row_ref[0:1, :] * window[:rows]
        for k in range(1, 4):
            valid = wide(valid_ref[k, pl.ds(r, rows + SUB), :], width)
            total = total + row_ref[k : k + 1, :] * (window * valid)[k : k + rows]
        return total

    head_ref[...] = spread_back(dconv_ref[pl.ds(0, 2 * SUB), :], 0, SUB)

    def finish(i, carry):
        r = pl.multiple_of(i * ROWS, ROWS)
        window = dconv_ref[pl.ds(r + SUB, ROWS + SUB), :]
        total = spread_back(window, r + SUB, ROWS)
        dinner_ref[pl.ds(r, ROWS), :] = total.astype(bf16)

        @pl.when(i == blocks - 1)
        def _():
            tail_ref[...] = total[ROWS - 2 * SUB :]

        dconv = window[:ROWS]
        inputs = ext_ref[pl.ds(r, ROWS + SUB), :]
        sums = [fold(dconv * inputs[SUB:])]
        for k in range(1, 4):
            valid = wide(valid_ref[k, pl.ds(r + SUB, ROWS), :], width)
            sums.append(fold(dconv * valid * inputs[SUB - k : SUB - k + ROWS]))
        sums.append(fold(dconv))
        return tuple(c + s for c, s in zip(carry, sums))

    sums = lax.fori_loop(0, blocks, finish, (zero,) * 5)
    sums_ref[...] = jnp.concatenate(
        [jnp.sum(s, axis=0, keepdims=True) for s in (*sums, bias_r, bias_i, decay)], 0
    )


def vmem(count=1):
    return [pl.BlockSpec(memory_space=pltpu.VMEM)] * count


def shape(dims, kind=f32):
    return jax.ShapeDtypeStruct(dims, kind)


def small_cost():
    return pl.CostEstimate(flops=1000, bytes_accessed=1000, transcendentals=0)


def run_forward(inner, halo, valid, rows, gates):
    count, width = inner.shape
    full = shape((count, width))
    return pl.pallas_call(
        forward_kernel,
        out_shape=(full, shape((count, width), bf16)) + (full,) * 6 + (shape((SUB, width)),),
        in_specs=vmem(5),
        out_specs=tuple(vmem(9)),
        scratch_shapes=[
            pltpu.VMEM((count + SUB, width), f32),
            pltpu.VMEM((count, 2 * width), f32),
        ],
        compiler_params=pltpu.CompilerParams(vmem_limit_bytes=VMEM_LIMIT),
        cost_estimate=small_cost(),
        name="recurrence_forward",
    )(inner, halo, valid, rows, gates)


def run_states(mine, ends, part, span, gate_pre):
    count, width = part.shape
    block = count // 4
    tile = pl.BlockSpec((block, width), lambda i: (i, 0))
    return pl.pallas_call(
        state_kernel,
        grid=(4,),
        out_shape=(
            shape((count, width)), shape((count, width), bf16), shape((SUB, width)),
        ),
        in_specs=[
            pl.BlockSpec(memory_space=pltpu.SMEM),
            pl.BlockSpec(ends.shape, lambda i: (0, 0, 0)),
            tile, tile, tile,
        ],
        out_specs=(tile, tile, pl.BlockSpec((SUB, width), lambda i: (0, 0))),
        compiler_params=pltpu.CompilerParams(vmem_limit_bytes=VMEM_LIMIT),
        cost_estimate=small_cost(),
        name="recurrence_states",
    )(mine, ends, part, span, gate_pre)


def run_turn(dmixed, gate_pre, states, span):
    count, width = dmixed.shape
    block = count // 4
    tile = pl.BlockSpec((block, width), lambda i: (i, 0))
    return pl.pallas_call(
        turn_kernel,
        grid=(4,),
        out_shape=(
            shape((count, width)), shape((count, width), bf16), shape((SUB, width)),
        ),
        in_specs=[tile] * 4,
        out_specs=(tile, tile, pl.BlockSpec((SUB, width), lambda i: (0, 0))),
        compiler_params=pltpu.CompilerParams(vmem_limit_bytes=VMEM_LIMIT),
        cost_estimate=small_cost(),
        name="recurrence_turn",
    )(dmixed, gate_pre, states, span)


def run_backward(mine, ends, dstates, saved, enter, valid, inner, halo, rows, gates):
    count, width = dstates.shape
    return pl.pallas_call(
        backward_kernel,
        out_shape=(
            shape((count, width), bf16), shape((2 * SUB, width)), shape((SUB, width)),
            shape((count, 2 * width), bf16), shape((SUB, width)),
        ),
        in_specs=[pl.BlockSpec(memory_space=pltpu.SMEM)] + vmem(14),
        out_specs=tuple(vmem(5)),
        scratch_shapes=[
            pltpu.VMEM((count + 2 * SUB, width), f32),
            pltpu.VMEM((count + SUB, width), f32),
        ],
        compiler_params=pltpu.CompilerParams(vmem_limit_bytes=VMEM_LIMIT),
        cost_estimate=small_cost(),
        name="recurrence_backward",
    )(
        mine, ends, dstates, saved["alpha"], saved["states"], enter, saved["conv"], saved["rg"],
        saved["ig"], saved["factor"], valid, inner, halo, rows, gates,
    )


def columns_product_kernel(ring_ref, left_ref, *refs):
    out_ref = refs[-1]
    left = left_ref[...].T
    start = 0
    for right_ref in refs[:-1]:
        width = right_ref.shape[1]
        out_ref[:, start : start + width] = jnp.dot(
            left, right_ref[...], preferred_element_type=f32
        )
        start += width


def ring_order():
    devices = lax.axis_size("seq")
    return [0, 1, 3, 2, 6, 7, 5, 4] if devices == 8 else list(range(devices))


def ring_scatter(value):
    return lax.psum_scatter(
        value, "seq", scatter_dimension=0, axis_index_groups=[ring_order()], tiled=True
    )


def columns_product(left, rights):
    rows, columns = left.shape
    width = sum(right.shape[1] for right in rights)
    ring = ring_order()
    block = columns // len(ring)
    if block % LANES:
        whole = matmul_tn(left, jnp.concatenate(rights, 1)).reshape(len(ring), block, width)
        return jnp.concatenate([whole[d] for d in ring], 0)
    return pl.pallas_call(
        columns_product_kernel,
        grid_spec=pltpu.PrefetchScalarGridSpec(
            num_scalar_prefetch=1,
            grid=(len(ring),),
            in_specs=[pl.BlockSpec((rows, block), lambda j, ring: (0, ring[j]))]
            + [pl.BlockSpec(right.shape, lambda j, ring: (0, 0)) for right in rights],
            out_specs=pl.BlockSpec((block, width), lambda j, ring: (j, 0)),
        ),
        out_shape=shape((columns, width)),
        compiler_params=pltpu.CompilerParams(vmem_limit_bytes=VMEM_LIMIT),
        cost_estimate=small_cost(),
        name="columns_product",
    )(jnp.array(ring, jnp.int32), left, *rights)


def rows_product_kernel(left_ref, right_ref, out_ref, whole_ref, *, ring):
    whole_ref[...] = jnp.dot(left_ref[...].T, right_ref[...], preferred_element_type=f32)
    block = out_ref.shape[0] // len(ring)
    for j, d in enumerate(ring):
        out_ref[j * block : (j + 1) * block, :] = whole_ref[d * block : (d + 1) * block, :]


def rows_product(left, right, width):
    rows, columns = left.shape
    return pl.pallas_call(
        partial(rows_product_kernel, ring=ring_order()),
        grid=(right.shape[1] // width,),
        in_specs=[
            pl.BlockSpec(left.shape, lambda n: (0, 0)),
            pl.BlockSpec((rows, width), lambda n: (0, n)),
        ],
        out_specs=pl.BlockSpec((columns, width), lambda n: (0, n)),
        scratch_shapes=[pltpu.VMEM((columns, width), f32)],
        out_shape=shape((columns, right.shape[1])),
        compiler_params=pltpu.CompilerParams(vmem_limit_bytes=VMEM_LIMIT),
        cost_estimate=small_cost(),
        name="rows_product",
    )(left, right)


def block_diagonal(weights):
    groups, width, _ = weights.shape
    rows = [
        jnp.pad(weights[b], ((0, 0), (b * width, (groups - 1 - b) * width))) for b in range(groups)
    ]
    return jnp.concatenate(rows, 0)


def diagonal_blocks(whole, groups):
    width = whole.shape[0] // groups
    return jnp.stack(
        [
            whole[b * width : (b + 1) * width, b * width : (b + 1) * width]
            for b in range(groups)
        ],
        0,
    )


def row_scale(squares, features):
    return lax.rsqrt(squares / features + norm_eps)[:, None]


def body(
    stream, doc_starts, gain_first, proj_inner, proj_gate, conv_weight, conv_bias, gate_recur,
    gate_input, bias_recur, bias_input, decay_param, proj_out, gain_second, mlp_gate, mlp_up,
    mlp_down, cotangent,
):
    count, own_width = stream.shape
    features = gain_first.shape[0]
    inner_width = proj_inner.shape[1]
    ffn_width = mlp_gate.shape[1]
    groups = gate_recur.shape[0]
    devices = lax.axis_size("seq")
    seq_at = lax.axis_index("seq").astype(jnp.int32).reshape(1)
    column = lax.axis_index("mp") * own_width
    own_first = lax.dynamic_slice_in_dim(gain_first, column, own_width)
    own_second = lax.dynamic_slice_in_dim(gain_second, column, own_width)
    onward = [(s, s + 1) for s in range(devices - 1)]
    backward = [(s + 1, s) for s in range(devices - 1)]


    first = LineGather(stream)
    first.first()
    first_scale = row_scale(line_sum(jnp.sum(stream * stream, axis=1)), features)
    starts = doc_starts.astype(f32)
    starts_before = lax.ppermute(starts[count - SUB :], "seq", onward)
    keep_ext = 1.0 - jnp.concatenate([starts_before, starts], 0)
    reach = [keep_ext[SUB:]]
    for k in range(1, 4):
        reach.append(
            (reach[-1] if k > 1 else 1.0) * keep_ext[SUB - k + 1 : SUB - k + 1 + count]
        )
    valid = jnp.broadcast_to(jnp.stack(reach, 0)[:, :, None], (4, count, LANES))
    valid = jnp.pad(valid, ((0, 0), (SUB, SUB), (0, 0)))
    rows = jnp.stack(
        [
            conv_weight[0], conv_weight[1], conv_weight[2], conv_weight[3], conv_bias, bias_recur,
            bias_input, -recur_scale * jax.nn.softplus(-decay_param),
        ],
        0,
    )
    gates = jnp.concatenate([block_diagonal(gate_recur), block_diagonal(gate_input)], 1)
    first.second()
    first.third(gates, valid)

    def first_turn(piece, start):
        return piece * first_scale * lax.dynamic_slice_in_dim(gain_first, start, own_width)

    first_low = assemble(first.pieces(), features, first_turn)
    cot = LineGather(cotangent)
    cot.first(first.far_out)
    inner = matmul(first_low, proj_inner)
    halo = lax.ppermute(inner[count - SUB :], "seq", onward)
    gate_pre = matmul(after(first_low, inner), proj_gate)
    halo = after(halo, gate_pre)
    conv, conv_low, rg, ig, alpha, factor, part, span, last = run_forward(
        inner, halo, valid, rows, gates
    )
    ends = after(lax.all_gather(last, "seq"), cot.beside, cot.near_in)
    cot.second()
    states, mixed_low, enter = run_states(seq_at, ends, part, span, gate_pre)

    branch = LineScatter(matmul(mixed_low, proj_out), own_width)
    branch.first()
    branch.second(cot.far_in, cot.near_out)
    cot.third()
    ffn_weight = jnp.concatenate(after((mlp_gate, mlp_up), branch.far_one), 1)
    branch.third(cot.far_out, ffn_weight)
    cot_low = assemble(cot.pieces(), features, lambda piece, start: piece)
    d_hidden = matmul_nt(cot_low, mlp_down)
    own_resid = stream + branch.result()

    second = LineGather(own_resid)
    second.first()
    second_scale = row_scale(line_sum(jnp.sum(own_resid * own_resid, axis=1)), features)
    second.second(d_hidden)
    second.third()

    def second_turn(piece, start):
        return piece * second_scale * lax.dynamic_slice_in_dim(gain_second, start, own_width)

    second_low = assemble(second.pieces(), features, second_turn)
    ffn = matmul(second_low, ffn_weight)
    act, slope = gelu_parts(ffn[:, :ffn_width])
    ffn_up = ffn[:, ffn_width:]
    hidden_low = (act * ffn_up).astype(bf16)
    d_pair_low = jnp.concatenate([d_hidden * ffn_up * slope, d_hidden * act], 1).astype(bf16)
    d_second_part = matmul_nt(d_pair_low, ffn_weight)

    turned = LineScatter(d_second_part, own_width)
    turned.first()
    whole_down = rows_product(after(hidden_low, d_second_part), cot_low, own_width)
    whole_pair = columns_product(after(second_low, d_second_part), [d_pair_low])
    turned.second(whole_down, whole_pair)
    grad_down = ring_scatter(whole_down)
    grad_pair = ring_scatter(whole_pair)
    second_product = after(d_second_part, turned.far_one) * second_low.astype(f32)
    second_mean = line_sum(jnp.sum(second_product, axis=1)) / features
    d_gain_second = jnp.sum(second_product, axis=0) / gain_second
    turned.third(d_gain_second, second_mean)
    mlp_part = matmul(after(hidden_low, turned.far_two, turned.near_one), mlp_down)
    own_d_second = turned.result()
    own_d_resid = (
        cotangent
        + second_scale * (own_second * own_d_second)
        - own_resid * (second_scale * second_scale * second_mean[:, None])
    )
    gathered = LineGather(own_d_resid)
    gathered.first(mlp_part)
    gathered.second()
    sent = LineScatter(mlp_part, own_width)
    sent.first(gathered.near_in, gathered.beside)
    gathered.third(sent.far_one, grad_down)
    sent.second(gathered.near_out)
    branch_low = assemble(gathered.pieces(), features, lambda piece, start: piece)

    d_mixed = matmul_nt(after(branch_low, sent.far_two, sent.near_one), proj_out)
    d_states, d_gate_low, outgoing = run_turn(d_mixed, gate_pre, states, span)
    leaving = jnp.stack([last[0], jnp.sum(outgoing, axis=0)], 0)
    back_ends = lax.all_gather(leaving, "seq")
    sent.third()
    saved = dict(alpha=alpha, states=states, conv=conv, rg=rg, ig=ig, factor=factor)
    d_inner_low, tail, head, d_rec_low, sums = run_backward(
        seq_at, back_ends, d_states, saved, enter, valid, inner, halo, rows, gates
    )
    returned = lax.ppermute(head, "seq", backward)
    d_first_gate = matmul_nt(after(d_gate_low, head), proj_gate)
    returned = after(returned, d_first_gate, sent.last, sent.near_two)
    tail = tail + jnp.concatenate([jnp.zeros_like(returned), returned], 0)
    d_inner_low = lax.dynamic_update_slice(d_inner_low, tail.astype(bf16), (count - 2 * SUB, 0))
    d_first_part = matmul_nt(d_inner_low, proj_inner) + d_first_gate

    final = LineScatter(d_first_part, own_width)
    final.first(grad_pair)
    whole_first = columns_product(
        after(first_low, d_first_part), [d_inner_low, d_gate_low]
    )
    grad_first = ring_scatter(whole_first)
    first_product = after(d_first_part, whole_first) * first_low.astype(f32)
    first_mean = jnp.sum(first_product, axis=1)
    gains = jnp.stack([jnp.sum(first_product, axis=0) / gain_first, d_gain_second], 0)
    gate_grads = matmul_tn(conv_low, after(d_rec_low, whole_first))
    block_width = inner_width // groups
    small = jnp.concatenate(
        [
            jnp.concatenate(
                [
                    diagonal_blocks(gate_grads[:, :inner_width], groups),
                    diagonal_blocks(gate_grads[:, inner_width:], groups),
                ],
                2,
            ).reshape(inner_width, 2 * block_width),
            sums.reshape(-1, 2 * block_width),
        ],
        0,
    )
    whole_out = rows_product(after(mixed_low, whole_first), branch_low, 2 * own_width)
    grad_out = ring_scatter(whole_out)
    final.second(small, gains, first_mean, whole_out)
    small = small + swapped(small, "seq", 1)
    gains = sum_over(gains, "mp")
    first_mean = line_sum(first_mean) / features
    output = own_resid + sent.result()
    final.third(output, first_mean, small, gains)
    bit = 2
    while bit < devices:
        small = small + swapped(small, "seq", bit)
        bit *= 2
    gains = sum_over(gains, "seq")
    own_d_first = final.result()
    grad_stream = (
        own_d_resid
        + first_scale * (own_first * own_d_first)
        - stream * (first_scale * first_scale * first_mean[:, None])
    )
    sums = small[inner_width:].reshape(SUB, inner_width)
    grad_gates = [
        small[:inner_width, g * block_width : (g + 1) * block_width].reshape(
            groups, block_width, block_width
        )
        for g in range(2)
    ]
    grad_decay = sums[7] * (recur_scale * jax.nn.sigmoid(-decay_param))
    return (
        output,
        grad_stream,
        gains[0],
        grad_first[:, :inner_width],
        grad_first[:, inner_width:],
        sums[:4],
        sums[4],
        grad_gates[0],
        grad_gates[1],
        sums[5],
        sums[6],
        grad_decay,
        grad_out,
        gains[1],
        grad_pair[:, :ffn_width],
        grad_pair[:, ffn_width:],
        grad_down,
    )


def solution(mesh):
    in_specs = (
        P("seq", "mp"),
        P("seq"),
        P(),
        P(None, "mp"),
        P(None, "mp"),
        P(None, "mp"),
        P("mp"),
        P("mp", None, None),
        P("mp", None, None),
        P("mp"),
        P("mp"),
        P("mp"),
        P("mp", None),
        P(),
        P(None, "mp"),
        P(None, "mp"),
        P("mp", None),
        P("seq", "mp"),
    )
    out_specs = (
        P("seq", "mp"),
        P("seq", "mp"),
        P(),
        P("seq", "mp"),
        P("seq", "mp"),
        P(None, "mp"),
        P("mp"),
        P("mp", None, None),
        P("mp", None, None),
        P("mp"),
        P("mp"),
        P("mp"),
        P(("mp", "seq"), None),
        P(),
        P("seq", "mp"),
        P("seq", "mp"),
        P(("mp", "seq"), None),
    )
    return jax.shard_map(body, mesh=mesh, in_specs=in_specs, out_specs=out_specs, check_vma=False)
```

```python
from functools import partial

import jax
import jax.numpy as jnp
from jax import lax
from jax.experimental import pallas as pl
from jax.experimental.pallas import tpu as pltpu
from jax.sharding import PartitionSpec as P

recur_scale = 8.0
norm_eps = 1e-06
bf16 = jnp.bfloat16
f32 = jnp.float32
LANES = 128
SUB = 8
ROWS = 32
VMEM_LIMIT = 50 * 1024 * 1024


def matmul(left, right):
    return jnp.dot(left, right, preferred_element_type=f32)


def matmul_nt(left, right):
    return lax.dot_general(left, right, (((1,), (1,)), ((), ())), preferred_element_type=f32)


def matmul_tn(left, right):
    return lax.dot_general(left, right, (((0,), (0,)), ((), ())), preferred_element_type=f32)


PAIRS = ((0, 1), (1, 0), (2, 3), (3, 2))
MIDDLE = ((1, 2), (2, 1))
OUTWARD = ((1, 0), (2, 3))
INWARD = ((0, 1), (3, 2))
CROSS = ((0, 2), (2, 0), (1, 3), (3, 1))


def over_mp(value, pairs):
    return lax.ppermute(value, "mp", list(pairs))


def line_places():
    mine = lax.axis_index("mp")
    half = mine >> 1
    return mine, mine ^ 1, 2 - half, 3 - 3 * half


def after(value, *needed):
    return lax.optimization_barrier((value, needed))[0]


class LineGather:
    def __init__(self, own):
        self.own = own

    def first(self, *needed):
        own = after(self.own, *needed)
        self.beside, self.near_in = over_mp(own, PAIRS), over_mp(own, MIDDLE)
        return self.beside, self.near_in

    def second(self, *needed):
        near, beside = after((self.near_in, self.beside), *needed)
        self.near_out, self.far_in = over_mp(near, OUTWARD), over_mp(beside, MIDDLE)
        return self.near_out, self.far_in

    def third(self, *needed):
        far, _ = after((self.far_in, self.near_out), *needed)
        self.far_out = over_mp(far, OUTWARD)
        return self.far_out

    def pieces(self):
        return self.own, self.beside, self.near_in + self.near_out, self.far_in + self.far_out


class LineScatter:
    def __init__(self, whole, width):
        self.whole, self.width = whole, width
        self.mine, self.beside, self.near, self.far = line_places()

    def piece(self, place):
        return lax.dynamic_slice_in_dim(self.whole, place * self.width, self.width, 1)

    def first(self, *needed):
        self.far_one = over_mp(after(self.piece(self.far), *needed), INWARD)
        return self.far_one

    def second(self, *needed):
        far, near = after(
            (self.piece(self.far) + self.far_one, self.piece(self.near)), *needed
        )
        self.far_two, self.near_one = over_mp(far, MIDDLE), over_mp(near, INWARD)
        return self.far_two, self.near_one

    def third(self, *needed):
        near, last = after(
            (self.piece(self.near) + self.near_one, self.piece(self.beside) + self.far_two), *needed
        )
        self.near_two, self.last = over_mp(near, MIDDLE), over_mp(last, PAIRS)
        return self.near_two, self.last

    def result(self):
        return self.piece(self.mine) + self.near_two + self.last


def line_sum(value):
    value = value + over_mp(value, PAIRS)
    return value + over_mp(value, CROSS)


def swapped(value, axis, bit):
    count = lax.axis_size(axis)
    return lax.ppermute(value, axis, [(d, d ^ bit) for d in range(count)])


def over_chips(value, bit):
    devices = lax.axis_size("seq")
    value = value + swapped(value, "seq", bit)
    while bit > 2 and 2 * bit < devices:
        bit *= 2
        value = value + swapped(value, "seq", bit)
    return value


def sum_over(value, axis):
    bit = 1
    while bit < lax.axis_size(axis):
        value = value + swapped(value, axis, bit)
        bit *= 2
    return value


def assemble(pieces, width, turn):
    rows, own_width = pieces[0].shape
    whole = jnp.zeros((rows, width), bf16)
    for piece, place in zip(pieces, line_places()):
        start = place * own_width
        whole = lax.dynamic_update_slice(whole, turn(piece, start).astype(bf16), (0, start))
    return whole


def wide(value, width):
    return jnp.concatenate([value] * (width // LANES), axis=-1)


def neg_expm1(x, e):
    poly = 1.0 / 40320.0
    for term in (5040.0, 720.0, 120.0, 24.0, 6.0, 2.0, 1.0):
        poly = poly * x + 1.0 / term
    return jnp.where(x > -0.5, -x * poly, 1.0 - e)


def gelu_parts(x):
    scale = 0.7978845608028654
    cube = 0.044715
    squared = x * x
    t = jnp.tanh(scale * (x + cube * x * squared))
    half = 0.5 * (1.0 + t)
    slope = half + 0.5 * x * (1.0 - t * t) * scale * (1.0 + 3.0 * cube * squared)
    return half * x, slope


def group_scan(a, b):
    place = lax.broadcasted_iota(jnp.int32, a.shape, 1)
    for k in (1, 2, 4):
        fits = place >= k
        b = jnp.where(fits, a * pltpu.roll(b, k, 1) + b, b)
        a = jnp.where(fits, a * pltpu.roll(a, k, 1), a)
    return a, b


def group_scan_back(a, b):
    place = lax.broadcasted_iota(jnp.int32, a.shape, 1)
    for k in (1, 2, 4):
        fits = place < SUB - k
        b = jnp.where(fits, a * pltpu.roll(b, SUB - k, 1) + b, b)
        a = jnp.where(fits, a * pltpu.roll(a, SUB - k, 1), a)
    return a, b


def forward_kernel(
    inner_ref, halo_ref, valid_ref, row_ref, gate_ref,
    conv_ref, low_ref, rg_ref, ig_ref, alpha_ref, factor_ref, part_ref, span_ref, last_ref,
    ext_ref, pre_ref,
):
    count, width = inner_ref.shape
    ext_ref[pl.ds(0, SUB), :] = halo_ref[...]

    def fill(i, _):
        r = pl.multiple_of(i * ROWS, ROWS)
        ext_ref[pl.ds(r + SUB, ROWS), :] = inner_ref[pl.ds(r, ROWS), :]
        return 0

    lax.fori_loop(0, count // ROWS, fill, 0)

    def convolve(i, _):
        r = pl.multiple_of(i * ROWS, ROWS)
        window = ext_ref[pl.ds(r, ROWS + SUB), :]
        total = row_ref[0:1, :] * window[SUB:]
        for k in range(1, 4):
            valid = wide(valid_ref[k, pl.ds(r + SUB, ROWS), :], width)
            total = total + row_ref[k : k + 1, :] * window[SUB - k : SUB - k + ROWS] * valid
        total = total + row_ref[4:5, :]
        conv_ref[pl.ds(r, ROWS), :] = total
        low_ref[pl.ds(r, ROWS), :] = total.astype(bf16)
        return 0

    lax.fori_loop(0, count // ROWS, convolve, 0)
    pre_ref[...] = jnp.dot(low_ref[...], gate_ref[...], preferred_element_type=f32)

    def scan(i, carry):
        r = pl.multiple_of(i * ROWS, ROWS)
        here = pl.ds(r, ROWS)
        rg = jax.nn.sigmoid(pre_ref[here, :width] + row_ref[5:6, :])
        ig = jax.nn.sigmoid(pre_ref[here, width:] + row_ref[6:7, :])
        log_a = row_ref[7:8, :] * rg
        keep = wide(valid_ref[0, pl.ds(r + SUB, ROWS), :], width)
        a = jnp.exp(log_a)
        root = jnp.sqrt(neg_expm1(2.0 * log_a, a * a))
        factor = (1.0 - keep) + keep * root
        alpha = a * keep
        beta = factor * ig * conv_ref[here, :]
        rg_ref[here, :] = rg
        ig_ref[here, :] = ig
        alpha_ref[here, :] = alpha
        factor_ref[here, :] = factor
        groups = (ROWS // SUB, SUB, width)
        a3, b3 = group_scan(alpha.reshape(groups), beta.reshape(groups))
        state, product = carry
        for g in range(ROWS // SUB):
            part = b3[g] + a3[g] * state
            span = a3[g] * product
            part_ref[pl.ds(r + g * SUB, SUB), :] = part
            span_ref[pl.ds(r + g * SUB, SUB), :] = span
            state, product = part[SUB - 1 : SUB, :], span[SUB - 1 : SUB, :]
        return state, product

    zero = jnp.zeros((1, width), f32)
    state, product = lax.fori_loop(0, count // ROWS, scan, (zero, zero + 1.0))
    last_ref[...] = jnp.concatenate([product, state, jnp.zeros((SUB - 2, width), f32)], 0)


def state_kernel(
    mine_ref, ends_ref, part_ref, span_ref, gate_ref, states_ref, mixed_ref, enter_ref
):
    devices = ends_ref.shape[0]
    width = part_ref.shape[1]
    entering = jnp.zeros((1, width), f32)
    for d in range(devices):
        ends = ends_ref[d]
        entering = jnp.where(d < mine_ref[0], ends[0:1, :] * entering + ends[1:2, :], entering)
    states = span_ref[...] * entering + part_ref[...]
    states_ref[...] = states
    mixed_ref[...] = (gelu_parts(gate_ref[...])[0] * states).astype(bf16)
    enter_ref[...] = jnp.broadcast_to(entering, enter_ref.shape)


def turn_kernel(
    dmixed_ref, gate_ref, states_ref, span_ref, dstates_ref, dgate_ref, out_ref
):
    act, slope = gelu_parts(gate_ref[...])
    dmixed = dmixed_ref[...]
    dstates = dmixed * act
    dstates_ref[...] = dstates
    dgate_ref[...] = (dmixed * states_ref[...] * slope).astype(bf16)

    @pl.when(pl.program_id(0) == 0)
    def _():
        out_ref[...] = jnp.zeros_like(out_ref)

    out_ref[...] += jnp.sum(
        (dstates * span_ref[...]).reshape(-1, SUB, dstates.shape[1]), axis=0
    )


def backward_kernel(
    mine_ref, ends_ref, dstates_ref, alpha_ref, states_ref, enter_ref, conv_ref, rg_ref, ig_ref,
    factor_ref, valid_ref, inner_ref, halo_ref, row_ref, gate_ref,
    dinner_ref, tail_ref, head_ref, small_ref,
    dconv_ref, ext_ref, drec_ref, whole_ref, *, groups,
):
    devices = ends_ref.shape[0]
    count, width = alpha_ref.shape
    blocks = count // ROWS
    incoming = jnp.zeros((1, width), f32)
    for d in reversed(range(devices)):
        ends = ends_ref[d]
        incoming = jnp.where(d > mine_ref[0], ends[0:1, :] * incoming + ends[1:2, :], incoming)
    dconv_ref[pl.ds(0, SUB), :] = jnp.zeros((SUB, width), f32)
    dconv_ref[pl.ds(count + SUB, SUB), :] = jnp.zeros((SUB, width), f32)
    ext_ref[pl.ds(0, SUB), :] = halo_ref[...]
    parts = (ROWS // SUB, SUB, width)
    place = lax.broadcasted_iota(jnp.int32, (SUB, width), 0)

    def fold(value):
        return jnp.sum(value.reshape(parts), axis=0)

    def back(step, carry):
        flow, decay, bias_r, bias_i = carry
        i = blocks - 1 - step
        r = pl.multiple_of(i * ROWS, ROWS)
        here = pl.ds(r, ROWS)
        ext_ref[pl.ds(r + SUB, ROWS), :] = inner_ref[here, :]
        alpha = alpha_ref[here, :]
        dstates = dstates_ref[here, :]
        a3, b3 = group_scan_back(alpha.reshape(parts), (alpha * dstates).reshape(parts))
        d3 = dstates.reshape(parts)
        totals = [None] * (ROWS // SUB)
        for g in reversed(range(ROWS // SUB)):
            flows = b3[g] + a3[g] * flow
            later = jnp.where(place == SUB - 1, flow, pltpu.roll(flows, SUB - 1, 0))
            totals[g] = d3[g] + later
            flow = flows[0:1, :]
        total = jnp.concatenate(totals, 0)
        before = pl.multiple_of(jnp.maximum(r - SUB, 0), SUB)
        first = jnp.where(i == 0, enter_ref[...], states_ref[pl.ds(before, SUB), :])
        window = jnp.concatenate([first, states_ref[here, :]], 0)
        prior = window[SUB - 1 : SUB - 1 + ROWS]
        rg = rg_ref[here, :]
        ig = ig_ref[here, :]
        factor = factor_ref[here, :]
        conv = conv_ref[here, :]
        gain = total * factor
        dconv_ref[pl.ds(r + SUB, ROWS), :] = gain * ig
        dinput = (gain * conv * ig * (1.0 - ig)).astype(bf16)
        dlog = alpha * (total * prior - total * ig * conv * alpha / factor)
        drecur = (dlog * row_ref[7:8, :] * rg * (1.0 - rg)).astype(bf16)
        drec_ref[here, :width] = drecur
        drec_ref[here, width:] = dinput
        return (
            flow,
            decay + fold(dlog * rg),
            bias_r + fold(drecur.astype(f32)),
            bias_i + fold(dinput.astype(f32)),
        )

    zero = jnp.zeros((SUB, width), f32)
    _, decay, bias_r, bias_i = lax.fori_loop(0, blocks, back, (incoming, zero, zero, zero))
    dconv_ref[pl.ds(SUB, count), :] += lax.dot_general(
        drec_ref[...], gate_ref[...], (((1,), (1,)), ((), ())), preferred_element_type=f32
    )

    def spread_back(window, r, rows):
        total = row_ref[0:1, :] * window[:rows]
        for k in range(1, 4):
            valid = wide(valid_ref[k, pl.ds(r, rows + SUB), :], width)
            total = total + row_ref[k : k + 1, :] * (window * valid)[k : k + rows]
        return total

    head_ref[...] = spread_back(dconv_ref[pl.ds(0, 2 * SUB), :], 0, SUB)

    def finish(i, carry):
        r = pl.multiple_of(i * ROWS, ROWS)
        window = dconv_ref[pl.ds(r + SUB, ROWS + SUB), :]
        total = spread_back(window, r + SUB, ROWS)
        dinner_ref[pl.ds(r, ROWS), :] = total.astype(bf16)

        @pl.when(i == blocks - 1)
        def _():
            tail_ref[...] = total[ROWS - 2 * SUB :]

        dconv = window[:ROWS]
        inputs = ext_ref[pl.ds(r, ROWS + SUB), :]
        sums = [fold(dconv * inputs[SUB:])]
        for k in range(1, 4):
            valid = wide(valid_ref[k, pl.ds(r + SUB, ROWS), :], width)
            sums.append(fold(dconv * valid * inputs[SUB - k : SUB - k + ROWS]))
        sums.append(fold(dconv))
        return tuple(c + s for c, s in zip(carry, sums))

    sums = lax.fori_loop(0, blocks, finish, (zero,) * 5)
    sums = jnp.concatenate(
        [jnp.sum(s, axis=0, keepdims=True) for s in (*sums, bias_r, bias_i, decay)], 0
    )
    whole_ref[...] = lax.dot_general(
        conv_ref[...].astype(bf16), drec_ref[...], (((0,), (0,)), ((), ())),
        preferred_element_type=f32,
    )
    block = width // groups
    left = lax.broadcasted_iota(jnp.int32, (block, width), 1) < block

    def turned(value, shift):
        return pltpu.roll(value, shift % width, 1) if shift % width else value

    for b in range(groups):
        here = slice(b * block, (b + 1) * block)
        recur = turned(whole_ref[here, :width], -b * block)
        entry = turned(whole_ref[here, width:], block - b * block)
        small_ref[here, :] = jnp.where(left, recur, entry)[:, : 2 * block]
    for b in range(groups // 2):
        small_ref[width + b * SUB : width + (b + 1) * SUB, :] = turned(
            sums, -2 * b * block
        )[:, : 2 * block]


def vmem(count=1):
    return [pl.BlockSpec(memory_space=pltpu.VMEM)] * count


def shape(dims, kind=f32):
    return jax.ShapeDtypeStruct(dims, kind)


def small_cost():
    return pl.CostEstimate(flops=1000, bytes_accessed=1000, transcendentals=0)


def run_forward(inner, halo, valid, rows, gates):
    count, width = inner.shape
    full = shape((count, width))
    return pl.pallas_call(
        forward_kernel,
        out_shape=(full, shape((count, width), bf16)) + (full,) * 6 + (shape((SUB, width)),),
        in_specs=vmem(5),
        out_specs=tuple(vmem(9)),
        scratch_shapes=[
            pltpu.VMEM((count + SUB, width), f32),
            pltpu.VMEM((count, 2 * width), f32),
        ],
        compiler_params=pltpu.CompilerParams(vmem_limit_bytes=VMEM_LIMIT),
        cost_estimate=small_cost(),
        name="recurrence_forward",
    )(inner, halo, valid, rows, gates)


def run_states(mine, ends, part, span, gate_pre):
    count, width = part.shape
    block = count // 4
    tile = pl.BlockSpec((block, width), lambda i: (i, 0))
    return pl.pallas_call(
        state_kernel,
        grid=(4,),
        out_shape=(
            shape((count, width)), shape((count, width), bf16), shape((SUB, width)),
        ),
        in_specs=[
            pl.BlockSpec(memory_space=pltpu.SMEM),
            pl.BlockSpec(ends.shape, lambda i: (0, 0, 0)),
            tile, tile, tile,
        ],
        out_specs=(tile, tile, pl.BlockSpec((SUB, width), lambda i: (0, 0))),
        compiler_params=pltpu.CompilerParams(vmem_limit_bytes=VMEM_LIMIT),
        cost_estimate=small_cost(),
        name="recurrence_states",
    )(mine, ends, part, span, gate_pre)


def run_turn(dmixed, gate_pre, states, span):
    count, width = dmixed.shape
    block = count // 4
    tile = pl.BlockSpec((block, width), lambda i: (i, 0))
    return pl.pallas_call(
        turn_kernel,
        grid=(4,),
        out_shape=(
            shape((count, width)), shape((count, width), bf16), shape((SUB, width)),
        ),
        in_specs=[tile] * 4,
        out_specs=(tile, tile, pl.BlockSpec((SUB, width), lambda i: (0, 0))),
        compiler_params=pltpu.CompilerParams(vmem_limit_bytes=VMEM_LIMIT),
        cost_estimate=small_cost(),
        name="recurrence_turn",
    )(dmixed, gate_pre, states, span)


def run_backward(mine, ends, dstates, saved, enter, valid, inner, halo, rows, gates, groups):
    count, width = dstates.shape
    return pl.pallas_call(
        partial(backward_kernel, groups=groups),
        out_shape=(
            shape((count, width), bf16), shape((2 * SUB, width)), shape((SUB, width)),
            shape((width + SUB * groups // 2, 2 * width // groups)),
        ),
        in_specs=[pl.BlockSpec(memory_space=pltpu.SMEM)] + vmem(14),
        out_specs=tuple(vmem(4)),
        scratch_shapes=[
            pltpu.VMEM((count + 2 * SUB, width), f32),
            pltpu.VMEM((count + SUB, width), f32),
            pltpu.VMEM((count, 2 * width), bf16),
            pltpu.VMEM((width, 2 * width), f32),
        ],
        compiler_params=pltpu.CompilerParams(vmem_limit_bytes=VMEM_LIMIT),
        cost_estimate=small_cost(),
        name="recurrence_backward",
    )(
        mine, ends, dstates, saved["alpha"], saved["states"], enter, saved["conv"], saved["rg"],
        saved["ig"], saved["factor"], valid, inner, halo, rows, gates,
    )


def columns_product_kernel(ring_ref, left_ref, *refs):
    out_ref = refs[-1]
    left = left_ref[...].T
    start = 0
    for right_ref in refs[:-1]:
        width = right_ref.shape[1]
        out_ref[:, start : start + width] = jnp.dot(
            left, right_ref[...], preferred_element_type=f32
        )
        start += width


def ring_order():
    devices = lax.axis_size("seq")
    return [0, 1, 3, 2, 6, 7, 5, 4] if devices == 8 else list(range(devices))


def ring_scatter(value):
    return lax.psum_scatter(
        value, "seq", scatter_dimension=0, axis_index_groups=[ring_order()], tiled=True
    )


def columns_product(left, rights):
    rows, columns = left.shape
    width = sum(right.shape[1] for right in rights)
    ring = ring_order()
    block = columns // len(ring)
    if block % LANES:
        whole = matmul_tn(left, jnp.concatenate(rights, 1)).reshape(len(ring), block, width)
        return jnp.concatenate([whole[d] for d in ring], 0)
    return pl.pallas_call(
        columns_product_kernel,
        grid_spec=pltpu.PrefetchScalarGridSpec(
            num_scalar_prefetch=1,
            grid=(len(ring),),
            in_specs=[pl.BlockSpec((rows, block), lambda j, ring: (0, ring[j]))]
            + [pl.BlockSpec(right.shape, lambda j, ring: (0, 0)) for right in rights],
            out_specs=pl.BlockSpec((block, width), lambda j, ring: (j, 0)),
        ),
        out_shape=shape((columns, width)),
        compiler_params=pltpu.CompilerParams(vmem_limit_bytes=VMEM_LIMIT),
        cost_estimate=small_cost(),
        name="columns_product",
    )(jnp.array(ring, jnp.int32), left, *rights)


def rows_product_kernel(left_ref, right_ref, out_ref, whole_ref, *, ring):
    whole_ref[...] = jnp.dot(left_ref[...].T, right_ref[...], preferred_element_type=f32)
    block = out_ref.shape[0] // len(ring)
    for j, d in enumerate(ring):
        out_ref[j * block : (j + 1) * block, :] = whole_ref[d * block : (d + 1) * block, :]


def rows_product(left, right, width):
    rows, columns = left.shape
    return pl.pallas_call(
        partial(rows_product_kernel, ring=ring_order()),
        grid=(right.shape[1] // width,),
        in_specs=[
            pl.BlockSpec(left.shape, lambda n: (0, 0)),
            pl.BlockSpec((rows, width), lambda n: (0, n)),
        ],
        out_specs=pl.BlockSpec((columns, width), lambda n: (0, n)),
        scratch_shapes=[pltpu.VMEM((columns, width), f32)],
        out_shape=shape((columns, right.shape[1])),
        compiler_params=pltpu.CompilerParams(vmem_limit_bytes=VMEM_LIMIT),
        cost_estimate=small_cost(),
        name="rows_product",
    )(left, right)


def block_diagonal(weights):
    groups, width, _ = weights.shape
    rows = [
        jnp.pad(weights[b], ((0, 0), (b * width, (groups - 1 - b) * width))) for b in range(groups)
    ]
    return jnp.concatenate(rows, 0)


def row_scale(squares, features):
    return lax.rsqrt(squares / features + norm_eps)[:, None]


def body(
    stream, doc_starts, gain_first, proj_inner, proj_gate, conv_weight, conv_bias, gate_recur,
    gate_input, bias_recur, bias_input, decay_param, proj_out, gain_second, mlp_gate, mlp_up,
    mlp_down, cotangent,
):
    count, own_width = stream.shape
    features = gain_first.shape[0]
    inner_width = proj_inner.shape[1]
    ffn_width = mlp_gate.shape[1]
    groups = gate_recur.shape[0]
    devices = lax.axis_size("seq")
    seq_at = lax.axis_index("seq").astype(jnp.int32).reshape(1)
    column = lax.axis_index("mp") * own_width
    own_first = lax.dynamic_slice_in_dim(gain_first, column, own_width)
    own_second = lax.dynamic_slice_in_dim(gain_second, column, own_width)
    onward = [(s, s + 1) for s in range(devices - 1)]
    backward = [(s + 1, s) for s in range(devices - 1)]


    first = LineGather(stream)
    first.first()
    first_scale = row_scale(line_sum(jnp.sum(stream * stream, axis=1)), features)
    starts = doc_starts.astype(f32)
    starts_before = lax.ppermute(starts[count - SUB :], "seq", onward)
    keep_ext = 1.0 - jnp.concatenate([starts_before, starts], 0)
    reach = [keep_ext[SUB:]]
    for k in range(1, 4):
        reach.append(
            (reach[-1] if k > 1 else 1.0) * keep_ext[SUB - k + 1 : SUB - k + 1 + count]
        )
    valid = jnp.broadcast_to(jnp.stack(reach, 0)[:, :, None], (4, count, LANES))
    valid = jnp.pad(valid, ((0, 0), (SUB, SUB), (0, 0)))
    rows = jnp.stack(
        [
            conv_weight[0], conv_weight[1], conv_weight[2], conv_weight[3], conv_bias, bias_recur,
            bias_input, -recur_scale * jax.nn.softplus(-decay_param),
        ],
        0,
    )
    gates = jnp.concatenate([block_diagonal(gate_recur), block_diagonal(gate_input)], 1)
    first.second()
    first.third(gates, valid)

    def first_turn(piece, start):
        return piece * first_scale * lax.dynamic_slice_in_dim(gain_first, start, own_width)

    first_low = assemble(first.pieces(), features, first_turn)
    cot = LineGather(cotangent)
    cot.first(first.far_out)
    inner = matmul(first_low, proj_inner)
    halo = lax.ppermute(inner[count - SUB :], "seq", onward)
    gate_pre = matmul(after(first_low, inner), proj_gate)
    halo = after(halo, gate_pre)
    conv, conv_low, rg, ig, alpha, factor, part, span, last = run_forward(
        inner, halo, valid, rows, gates
    )
    ends = after(lax.all_gather(last, "seq"), cot.beside, cot.near_in)
    cot.second()
    states, mixed_low, enter = run_states(seq_at, ends, part, span, gate_pre)

    branch = LineScatter(matmul(mixed_low, proj_out), own_width)
    branch.first()
    branch.second(cot.far_in, cot.near_out)
    cot.third()
    ffn_weight = jnp.concatenate(after((mlp_gate, mlp_up), branch.far_one), 1)
    branch.third(cot.far_out, ffn_weight)
    cot_low = assemble(cot.pieces(), features, lambda piece, start: piece)
    d_hidden = matmul_nt(cot_low, mlp_down)
    own_resid = stream + branch.result()

    second = LineGather(own_resid)
    second.first()
    second_scale = row_scale(line_sum(jnp.sum(own_resid * own_resid, axis=1)), features)
    second.second(d_hidden)
    second.third()

    def second_turn(piece, start):
        return piece * second_scale * lax.dynamic_slice_in_dim(gain_second, start, own_width)

    second_low = assemble(second.pieces(), features, second_turn)
    ffn = matmul(second_low, ffn_weight)
    act, slope = gelu_parts(ffn[:, :ffn_width])
    ffn_up = ffn[:, ffn_width:]
    hidden_low = (act * ffn_up).astype(bf16)
    d_pair_low = jnp.concatenate([d_hidden * ffn_up * slope, d_hidden * act], 1).astype(bf16)
    whole_down = rows_product(hidden_low, cot_low, own_width)
    grad_down = ring_scatter(whole_down)
    d_pair_low = after(d_pair_low, whole_down)
    d_second_part = matmul_nt(d_pair_low, ffn_weight)

    turned = LineScatter(d_second_part, own_width)
    turned.first()
    whole_pair = columns_product(after(second_low, d_second_part), [d_pair_low])
    turned.second(whole_pair)
    whole_pair = after(whole_pair, turned.far_one)
    grad_pair = ring_scatter(whole_pair)
    second_product = after(d_second_part, turned.far_one) * second_low.astype(f32)
    second_mean = line_sum(jnp.sum(second_product, axis=1)) / features
    d_gain_second = jnp.sum(second_product, axis=0) / gain_second
    turned.third(d_gain_second, second_mean)
    mlp_part = matmul(after(hidden_low, turned.far_two, turned.near_one), mlp_down)
    own_d_second = turned.result()
    own_d_resid = (
        cotangent
        + second_scale * (own_second * own_d_second)
        - own_resid * (second_scale * second_scale * second_mean[:, None])
    )
    gathered = LineGather(own_d_resid)
    gathered.first(mlp_part)
    d_gain_second = sum_over(sum_over(after(d_gain_second, own_d_resid), "mp"), "seq")
    gathered.second(d_gain_second)
    sent = LineScatter(mlp_part, own_width)
    sent.first(gathered.near_in, gathered.beside)
    gathered.third(sent.far_one, grad_down)
    sent.second(gathered.near_out)
    branch_low = assemble(gathered.pieces(), features, lambda piece, start: piece)

    d_mixed = matmul_nt(after(branch_low, sent.far_two, sent.near_one), proj_out)
    d_states, d_gate_low, outgoing = run_turn(d_mixed, gate_pre, states, span)
    whole_out = rows_product(after(mixed_low, d_states), branch_low, 2 * own_width)
    grad_out = ring_scatter(whole_out)
    leaving = jnp.stack([last[0], jnp.sum(after(outgoing, whole_out), axis=0)], 0)
    back_ends = lax.all_gather(leaving, "seq")
    sent.third(outgoing)
    saved = dict(alpha=alpha, states=states, conv=conv, rg=rg, ig=ig, factor=factor)
    d_inner_low, tail, head, small = run_backward(
        seq_at, back_ends, d_states, saved, enter, valid, inner, halo, rows, gates, groups
    )
    returned = lax.ppermute(head, "seq", backward)
    d_first_gate = matmul_nt(after(d_gate_low, head), proj_gate)
    returned = after(returned, d_first_gate, sent.last, sent.near_two)
    tail = tail + jnp.concatenate([jnp.zeros_like(returned), returned], 0)
    d_inner_low = lax.dynamic_update_slice(d_inner_low, tail.astype(bf16), (count - 2 * SUB, 0))
    d_first_part = matmul_nt(d_inner_low, proj_inner) + d_first_gate

    final = LineScatter(d_first_part, own_width)
    final.first(grad_pair)
    whole_first = columns_product(
        after(first_low, d_first_part), [d_inner_low, d_gate_low]
    )
    first_product = after(d_first_part, whole_first) * first_low.astype(f32)
    first_mean = jnp.sum(first_product, axis=1)
    d_gain_first = jnp.sum(first_product, axis=0) / gain_first
    output = own_resid + sent.result()
    small = small + swapped(small, "seq", 1)
    half = small.shape[0] // 2
    small = lax.dynamic_slice_in_dim(small, (lax.axis_index("seq") & 1) * half, half, 0)
    final.second(whole_first, first_mean, d_gain_first, output, small, grad_out)
    whole_first, first_mean, d_gain_first = after(
        (whole_first, first_mean, d_gain_first), final.far_one
    )
    grad_first = ring_scatter(whole_first)
    first_sums = line_sum(jnp.concatenate([first_mean, d_gain_first]))
    first_mean, d_gain_first = first_sums[:count] / features, first_sums[count:]
    small = over_chips(after(small, final.far_one), 2)
    final.third(first_mean, d_gain_first, small)
    small = over_chips(small, 4)
    d_gain_first = sum_over(d_gain_first, "seq")
    small, d_gain_first = after((small, d_gain_first), final.last)
    other = swapped(small, "seq", 1)
    lower = lax.axis_index("seq") & 1 == 0
    small = jnp.concatenate([jnp.where(lower, small, other), jnp.where(lower, other, small)], 0)
    own_d_first = final.result()
    grad_stream = (
        own_d_resid
        + first_scale * (own_first * own_d_first)
        - stream * (first_scale * first_scale * first_mean[:, None])
    )
    block_width = inner_width // groups
    sums = small[inner_width:].reshape(groups // 2, SUB, 2 * block_width)
    sums = sums.transpose(1, 0, 2).reshape(SUB, inner_width)
    grad_gates = [
        small[:inner_width, g * block_width : (g + 1) * block_width].reshape(
            groups, block_width, block_width
        )
        for g in range(2)
    ]
    grad_decay = sums[7] * (recur_scale * jax.nn.sigmoid(-decay_param))
    return (
        output,
        grad_stream,
        d_gain_first,
        grad_first[:, :inner_width],
        grad_first[:, inner_width:],
        sums[:4],
        sums[4],
        grad_gates[0],
        grad_gates[1],
        sums[5],
        sums[6],
        grad_decay,
        grad_out,
        d_gain_second,
        grad_pair[:, :ffn_width],
        grad_pair[:, ffn_width:],
        grad_down,
    )


def solution(mesh):
    in_specs = (
        P("seq", "mp"),
        P("seq"),
        P(),
        P(None, "mp"),
        P(None, "mp"),
        P(None, "mp"),
        P("mp"),
        P("mp", None, None),
        P("mp", None, None),
        P("mp"),
        P("mp"),
        P("mp"),
        P("mp", None),
        P(),
        P(None, "mp"),
        P(None, "mp"),
        P("mp", None),
        P("seq", "mp"),
    )
    out_specs = (
        P("seq", "mp"),
        P("seq", "mp"),
        P(),
        P("seq", "mp"),
        P("seq", "mp"),
        P(None, "mp"),
        P("mp"),
        P("mp", None, None),
        P("mp", None, None),
        P("mp"),
        P("mp"),
        P("mp"),
        P(("mp", "seq"), None),
        P(),
        P("seq", "mp"),
        P("seq", "mp"),
        P(("mp", "seq"), None),
    )
    return jax.shard_map(body, mesh=mesh, in_specs=in_specs, out_specs=out_specs, check_vma=False)
```

```python
from functools import partial

import jax
import jax.numpy as jnp
from jax import lax
from jax.experimental import pallas as pl
from jax.experimental.pallas import tpu as pltpu
from jax.sharding import PartitionSpec as P

recur_scale = 8.0
norm_eps = 1e-06
bf16 = jnp.bfloat16
f32 = jnp.float32
LANES = 128
SUB = 8
ROWS = 32
VMEM_LIMIT = 56 * 1024 * 1024


def matmul(left, right):
    return jnp.dot(left, right, preferred_element_type=f32)


def matmul_nt(left, right):
    return lax.dot_general(left, right, (((1,), (1,)), ((), ())), preferred_element_type=f32)


def matmul_tn(left, right):
    return lax.dot_general(left, right, (((0,), (0,)), ((), ())), preferred_element_type=f32)


PAIRS = ((0, 1), (1, 0), (2, 3), (3, 2))
MIDDLE = ((1, 2), (2, 1))
OUTWARD = ((1, 0), (2, 3))
INWARD = ((0, 1), (3, 2))
CROSS = ((0, 2), (2, 0), (1, 3), (3, 1))


def over_mp(value, pairs):
    return lax.ppermute(value, "mp", list(pairs))


def line_places():
    mine = lax.axis_index("mp")
    half = mine >> 1
    return mine, mine ^ 1, 2 - half, 3 - 3 * half


def after(value, *needed):
    return lax.optimization_barrier((value, needed))[0]


class LineGather:
    def __init__(self, own):
        self.own = own

    def first(self, *needed):
        own = after(self.own, *needed)
        self.beside, self.near_in = over_mp(own, PAIRS), over_mp(own, MIDDLE)
        return self.beside, self.near_in

    def second(self, *needed):
        near, beside = after((self.near_in, self.beside), *needed)
        self.near_out, self.far_in = over_mp(near, OUTWARD), over_mp(beside, MIDDLE)
        return self.near_out, self.far_in

    def third(self, *needed):
        far, _ = after((self.far_in, self.near_out), *needed)
        self.far_out = over_mp(far, OUTWARD)
        return self.far_out

    def pieces(self):
        return self.own, self.beside, self.near_in + self.near_out, self.far_in + self.far_out


class LineScatter:
    def __init__(self, blocks):
        self.far, self.near, self.beside, self.own = blocks

    def first(self, *needed):
        self.far_one = over_mp(after(self.far, *needed), INWARD)
        return self.far_one

    def second(self, *needed):
        far, near = after((self.far + self.far_one, self.near), *needed)
        self.far_two, self.near_one = over_mp(far, MIDDLE), over_mp(near, INWARD)
        return self.far_two, self.near_one

    def prepare(self):
        self.parts = (self.near + self.near_one, self.beside + self.far_two)
        return self.parts

    def third(self, *needed):
        near, last = after(self.prepare(), *needed)
        self.near_two, self.last = over_mp(near, MIDDLE), over_mp(last, PAIRS)
        return self.near_two, self.last

    def result(self):
        return self.own + self.near_two + self.last


def block_order():
    mine, beside, near, far = line_places()
    return jnp.stack([far, near, beside, mine]).astype(jnp.int32)


def line_sum(value):
    value = value + over_mp(value, PAIRS)
    return value + over_mp(value, CROSS)


def swapped(value, axis, bit):
    count = lax.axis_size(axis)
    return lax.ppermute(value, axis, [(d, d ^ bit) for d in range(count)])


def over_chips(value, bit):
    devices = lax.axis_size("seq")
    value = value + swapped(value, "seq", bit)
    while bit > 2 and 2 * bit < devices:
        bit *= 2
        value = value + swapped(value, "seq", bit)
    return value


def sum_over(value, axis):
    bit = 1
    while bit < lax.axis_size(axis):
        value = value + swapped(value, axis, bit)
        bit *= 2
    return value


def assemble(pieces, width, turn):
    rows, own_width = pieces[0].shape
    whole = jnp.zeros((rows, width), bf16)
    for piece, place in zip(pieces, line_places()):
        start = place * own_width
        whole = lax.dynamic_update_slice(whole, turn(piece, start).astype(bf16), (0, start))
    return whole


def wide(value, width):
    return jnp.concatenate([value] * (width // LANES), axis=-1)


def neg_expm1(x, e):
    poly = 1.0 / 40320.0
    for term in (5040.0, 720.0, 120.0, 24.0, 6.0, 2.0, 1.0):
        poly = poly * x + 1.0 / term
    return jnp.where(x > -0.5, -x * poly, 1.0 - e)


def gelu_parts(x):
    scale = 0.7978845608028654
    cube = 0.044715
    squared = x * x
    t = jnp.tanh(scale * (x + cube * x * squared))
    half = 0.5 * (1.0 + t)
    slope = half + 0.5 * x * (1.0 - t * t) * scale * (1.0 + 3.0 * cube * squared)
    return half * x, slope


def group_scan(a, b):
    place = lax.broadcasted_iota(jnp.int32, a.shape, 1)
    for k in (1, 2, 4):
        fits = place >= k
        b = jnp.where(fits, a * pltpu.roll(b, k, 1) + b, b)
        a = jnp.where(fits, a * pltpu.roll(a, k, 1), a)
    return a, b


def group_scan_back(a, b):
    place = lax.broadcasted_iota(jnp.int32, a.shape, 1)
    for k in (1, 2, 4):
        fits = place < SUB - k
        b = jnp.where(fits, a * pltpu.roll(b, SUB - k, 1) + b, b)
        a = jnp.where(fits, a * pltpu.roll(a, SUB - k, 1), a)
    return a, b


def forward_kernel(
    inner_ref, halo_ref, valid_ref, row_ref, gate_ref,
    conv_ref, low_ref, rg_ref, ig_ref, alpha_ref, factor_ref, part_ref, span_ref, last_ref,
    ext_ref, pre_ref,
):
    count, width = inner_ref.shape
    ext_ref[pl.ds(0, SUB), :] = halo_ref[...]

    def fill(i, _):
        r = pl.multiple_of(i * ROWS, ROWS)
        ext_ref[pl.ds(r + SUB, ROWS), :] = inner_ref[pl.ds(r, ROWS), :]
        return 0

    lax.fori_loop(0, count // ROWS, fill, 0)

    def convolve(i, _):
        r = pl.multiple_of(i * ROWS, ROWS)
        window = ext_ref[pl.ds(r, ROWS + SUB), :]
        total = row_ref[0:1, :] * window[SUB:]
        for k in range(1, 4):
            valid = wide(valid_ref[k, pl.ds(r + SUB, ROWS), :], width)
            total = total + row_ref[k : k + 1, :] * window[SUB - k : SUB - k + ROWS] * valid
        total = total + row_ref[4:5, :]
        conv_ref[pl.ds(r, ROWS), :] = total
        low_ref[pl.ds(r, ROWS), :] = total.astype(bf16)
        return 0

    lax.fori_loop(0, count // ROWS, convolve, 0)
    pre_ref[...] = jnp.dot(low_ref[...], gate_ref[...], preferred_element_type=f32)

    def scan(i, carry):
        r = pl.multiple_of(i * ROWS, ROWS)
        here = pl.ds(r, ROWS)
        rg = jax.nn.sigmoid(pre_ref[here, :width] + row_ref[5:6, :])
        ig = jax.nn.sigmoid(pre_ref[here, width:] + row_ref[6:7, :])
        log_a = row_ref[7:8, :] * rg
        keep = wide(valid_ref[0, pl.ds(r + SUB, ROWS), :], width)
        a = jnp.exp(log_a)
        root = jnp.sqrt(neg_expm1(2.0 * log_a, a * a))
        factor = (1.0 - keep) + keep * root
        alpha = a * keep
        beta = factor * ig * conv_ref[here, :]
        rg_ref[here, :] = rg
        ig_ref[here, :] = ig
        alpha_ref[here, :] = alpha
        factor_ref[here, :] = factor
        groups = (ROWS // SUB, SUB, width)
        a3, b3 = group_scan(alpha.reshape(groups), beta.reshape(groups))
        state, product = carry
        for g in range(ROWS // SUB):
            part = b3[g] + a3[g] * state
            span = a3[g] * product
            part_ref[pl.ds(r + g * SUB, SUB), :] = part
            span_ref[pl.ds(r + g * SUB, SUB), :] = span
            state, product = part[SUB - 1 : SUB, :], span[SUB - 1 : SUB, :]
        return state, product

    zero = jnp.zeros((1, width), f32)
    state, product = lax.fori_loop(0, count // ROWS, scan, (zero, zero + 1.0))
    last_ref[...] = jnp.concatenate([product, state, jnp.zeros((SUB - 2, width), f32)], 0)


def state_kernel(
    mine_ref, order_ref, ends_ref, part_ref, span_ref, gate_ref, weight_ref,
    states_ref, mixed_ref, enter_ref, *block_refs,
):
    devices = ends_ref.shape[0]
    width = part_ref.shape[1]
    entering = jnp.zeros((1, width), f32)
    for d in range(devices):
        ends = ends_ref[d]
        entering = jnp.where(d < mine_ref[0], ends[0:1, :] * entering + ends[1:2, :], entering)
    states = span_ref[...] * entering + part_ref[...]
    states_ref[...] = states
    mixed = (gelu_parts(gate_ref[...])[0] * states).astype(bf16)
    mixed_ref[...] = mixed
    enter_ref[...] = jnp.broadcast_to(entering, enter_ref.shape)
    for k, block_ref in enumerate(block_refs):
        block = block_ref.shape[1]
        columns = pl.ds(pl.multiple_of(order_ref[k] * block, block), block)
        block_ref[...] = jnp.dot(mixed, weight_ref[:, columns], preferred_element_type=f32)


def turn_kernel(
    branch_ref, weight_ref, gate_ref, states_ref, span_ref, dstates_ref, dgate_ref, out_ref
):
    act, slope = gelu_parts(gate_ref[...])
    dmixed = lax.dot_general(
        branch_ref[...], weight_ref[...], (((1,), (1,)), ((), ())), preferred_element_type=f32
    )
    dstates = dmixed * act
    dstates_ref[...] = dstates
    dgate_ref[...] = (dmixed * states_ref[...] * slope).astype(bf16)

    @pl.when(pl.program_id(0) == 0)
    def _():
        out_ref[...] = jnp.zeros_like(out_ref)

    out_ref[...] += jnp.sum(
        (dstates * span_ref[...]).reshape(-1, SUB, dstates.shape[1]), axis=0
    )


def feed_forward_kernel(
    order_ref, low_ref, gate_ref, up_ref, dhidden_ref, hidden_ref, dgate_ref, dup_ref, *block_refs
):
    step = pl.program_id(0)
    low = low_ref[...]
    gate = jnp.dot(low, gate_ref[...], preferred_element_type=f32)
    up = jnp.dot(low, up_ref[...], preferred_element_type=f32)
    act, slope = gelu_parts(gate)
    dhidden = dhidden_ref[...]
    hidden_ref[...] = (act * up).astype(bf16)
    dgate_ref[...] = (dhidden * up * slope).astype(bf16)
    dup_ref[...] = (dhidden * act).astype(bf16)
    contract = (((1,), (1,)), ((), ()))
    for k, block_ref in enumerate(block_refs):
        block = block_ref.shape[1]
        rows = pl.ds(pl.multiple_of(order_ref[k] * block, block), block)
        part = lax.dot_general(
            dgate_ref[...], gate_ref[rows, :], contract, preferred_element_type=f32
        ) + lax.dot_general(dup_ref[...], up_ref[rows, :], contract, preferred_element_type=f32)

        @pl.when(step == 0)
        def _():
            block_ref[...] = part

        @pl.when(step > 0)
        def _():
            block_ref[...] += part


def blocks_kernel(order_ref, *refs, pairs, transposed):
    for k, block_ref in enumerate(refs[2 * pairs :]):
        block = block_ref.shape[1]
        here = pl.ds(pl.multiple_of(order_ref[k] * block, block), block)
        total = None
        for left_ref, right_ref in zip(refs[:pairs], refs[pairs : 2 * pairs]):
            if transposed:
                part = lax.dot_general(
                    left_ref[...], right_ref[here, :], (((1,), (1,)), ((), ())),
                    preferred_element_type=f32,
                )
            else:
                part = jnp.dot(left_ref[...], right_ref[:, here], preferred_element_type=f32)
            total = part if total is None else total + part
        block_ref[...] = total


def sums_kernel(order_ref, low_ref, *refs):
    row_ref, column_ref = refs[-2:]
    rows = 0.0
    for k, block_ref in enumerate(refs[:-2]):
        block = block_ref.shape[1]
        here = pl.ds(pl.multiple_of(order_ref[k] * block, block), block)
        product = block_ref[...] * low_ref[:, here].astype(f32)
        rows = rows + jnp.sum(product, axis=1, keepdims=True)
        column_ref[:, here] = jnp.sum(product, axis=0, keepdims=True)
    row_ref[...] = rows


def product_kernel(left_ref, right_ref, out_ref, *, transposed):
    contract = (((1,), (1,)), ((), ())) if transposed else (((1,), (0,)), ((), ()))
    out_ref[...] = lax.dot_general(
        left_ref[...], right_ref[...], contract, preferred_element_type=f32
    )


def backward_kernel(
    mine_ref, ends_ref, dstates_ref, alpha_ref, states_ref, enter_ref, conv_ref, rg_ref, ig_ref,
    factor_ref, valid_ref, inner_ref, halo_ref, row_ref, gate_ref,
    dinner_ref, tail_ref, head_ref, small_ref,
    dconv_ref, ext_ref, drec_ref, whole_ref, *, groups,
):
    devices = ends_ref.shape[0]
    count, width = alpha_ref.shape
    blocks = count // ROWS
    incoming = jnp.zeros((1, width), f32)
    for d in reversed(range(devices)):
        ends = ends_ref[d]
        incoming = jnp.where(d > mine_ref[0], ends[0:1, :] * incoming + ends[1:2, :], incoming)
    dconv_ref[pl.ds(0, SUB), :] = jnp.zeros((SUB, width), f32)
    dconv_ref[pl.ds(count + SUB, SUB), :] = jnp.zeros((SUB, width), f32)
    ext_ref[pl.ds(0, SUB), :] = halo_ref[...]
    parts = (ROWS // SUB, SUB, width)
    place = lax.broadcasted_iota(jnp.int32, (SUB, width), 0)

    def fold(value):
        return jnp.sum(value.reshape(parts), axis=0)

    def back(step, carry):
        flow, decay, bias_r, bias_i = carry
        i = blocks - 1 - step
        r = pl.multiple_of(i * ROWS, ROWS)
        here = pl.ds(r, ROWS)
        ext_ref[pl.ds(r + SUB, ROWS), :] = inner_ref[here, :]
        alpha = alpha_ref[here, :]
        dstates = dstates_ref[here, :]
        a3, b3 = group_scan_back(alpha.reshape(parts), (alpha * dstates).reshape(parts))
        d3 = dstates.reshape(parts)
        totals = [None] * (ROWS // SUB)
        for g in reversed(range(ROWS // SUB)):
            flows = b3[g] + a3[g] * flow
            later = jnp.where(place == SUB - 1, flow, pltpu.roll(flows, SUB - 1, 0))
            totals[g] = d3[g] + later
            flow = flows[0:1, :]
        total = jnp.concatenate(totals, 0)
        before = pl.multiple_of(jnp.maximum(r - SUB, 0), SUB)
        first = jnp.where(i == 0, enter_ref[...], states_ref[pl.ds(before, SUB), :])
        window = jnp.concatenate([first, states_ref[here, :]], 0)
        prior = window[SUB - 1 : SUB - 1 + ROWS]
        rg = rg_ref[here, :]
        ig = ig_ref[here, :]
        factor = factor_ref[here, :]
        conv = conv_ref[here, :]
        gain = total * factor
        dconv_ref[pl.ds(r + SUB, ROWS), :] = gain * ig
        dinput = (gain * conv * ig * (1.0 - ig)).astype(bf16)
        dlog = alpha * (total * prior - total * ig * conv * alpha / factor)
        drecur = (dlog * row_ref[7:8, :] * rg * (1.0 - rg)).astype(bf16)
        drec_ref[here, :width] = drecur
        drec_ref[here, width:] = dinput
        return (
            flow,
            decay + fold(dlog * rg),
            bias_r + fold(drecur.astype(f32)),
            bias_i + fold(dinput.astype(f32)),
        )

    zero = jnp.zeros((SUB, width), f32)
    _, decay, bias_r, bias_i = lax.fori_loop(0, blocks, back, (incoming, zero, zero, zero))
    dconv_ref[pl.ds(SUB, count), :] += lax.dot_general(
        drec_ref[...], gate_ref[...], (((1,), (1,)), ((), ())), preferred_element_type=f32
    )

    def spread_back(window, r, rows):
        total = row_ref[0:1, :] * window[:rows]
        for k in range(1, 4):
            valid = wide(valid_ref[k, pl.ds(r, rows + SUB), :], width)
            total = total + row_ref[k : k + 1, :] * (window * valid)[k : k + rows]
        return total

    head_ref[...] = spread_back(dconv_ref[pl.ds(0, 2 * SUB), :], 0, SUB)

    def finish(i, carry):
        r = pl.multiple_of(i * ROWS, ROWS)
        window = dconv_ref[pl.ds(r + SUB, ROWS + SUB), :]
        total = spread_back(window, r + SUB, ROWS)
        dinner_ref[pl.ds(r, ROWS), :] = total.astype(bf16)

        @pl.when(i == blocks - 1)
        def _():
            tail_ref[...] = total[ROWS - 2 * SUB :]

        dconv = window[:ROWS]
        inputs = ext_ref[pl.ds(r, ROWS + SUB), :]
        sums = [fold(dconv * inputs[SUB:])]
        for k in range(1, 4):
            valid = wide(valid_ref[k, pl.ds(r + SUB, ROWS), :], width)
            sums.append(fold(dconv * valid * inputs[SUB - k : SUB - k + ROWS]))
        sums.append(fold(dconv))
        return tuple(c + s for c, s in zip(carry, sums))

    sums = lax.fori_loop(0, blocks, finish, (zero,) * 5)
    sums = jnp.concatenate(
        [jnp.sum(s, axis=0, keepdims=True) for s in (*sums, bias_r, bias_i, decay)], 0
    )
    whole_ref[...] = lax.dot_general(
        conv_ref[...].astype(bf16), drec_ref[...], (((0,), (0,)), ((), ())),
        preferred_element_type=f32,
    )
    block = width // groups
    left = lax.broadcasted_iota(jnp.int32, (block, width), 1) < block

    def turned(value, shift):
        return pltpu.roll(value, shift % width, 1) if shift % width else value

    for b in range(groups):
        here = slice(b * block, (b + 1) * block)
        recur = turned(whole_ref[here, :width], -b * block)
        entry = turned(whole_ref[here, width:], block - b * block)
        small_ref[2 * b // groups, b % (groups // 2) * block : (b % (groups // 2) + 1) * block, :] = (
            jnp.where(left, recur, entry)[:, : 2 * block]
        )
    for h in range(2):
        for b in range(groups // 4):
            small_ref[h, width // 2 + b * SUB : width // 2 + (b + 1) * SUB, :] = turned(
                sums, -2 * (h * (groups // 4) + b) * block
            )[:, : 2 * block]


def vmem(count=1):
    return [pl.BlockSpec(memory_space=pltpu.VMEM)] * count


def shape(dims, kind=f32):
    return jax.ShapeDtypeStruct(dims, kind)


def small_cost():
    return pl.CostEstimate(flops=1000, bytes_accessed=1000, transcendentals=0)


def run_forward(inner, halo, valid, rows, gates):
    count, width = inner.shape
    full = shape((count, width))
    return pl.pallas_call(
        forward_kernel,
        out_shape=(full, shape((count, width), bf16)) + (full,) * 6 + (shape((SUB, width)),),
        in_specs=vmem(5),
        out_specs=tuple(vmem(9)),
        scratch_shapes=[
            pltpu.VMEM((count + SUB, width), f32),
            pltpu.VMEM((count, 2 * width), f32),
        ],
        compiler_params=pltpu.CompilerParams(vmem_limit_bytes=VMEM_LIMIT),
        cost_estimate=small_cost(),
        name="recurrence_forward",
    )(inner, halo, valid, rows, gates)


def run_states(mine, order, ends, part, span, gate_pre, weight):
    count, width = part.shape
    features = weight.shape[1]
    block = count // 4
    tile = pl.BlockSpec((block, width), lambda i, m, o: (i, 0))
    out = pl.BlockSpec((block, features // 4), lambda i, m, o: (i, 0))
    return pl.pallas_call(
        state_kernel,
        grid_spec=pltpu.PrefetchScalarGridSpec(
            num_scalar_prefetch=2,
            grid=(4,),
            in_specs=[
                pl.BlockSpec(ends.shape, lambda i, m, o: (0, 0, 0)),
                tile, tile, tile,
                pl.BlockSpec(weight.shape, lambda i, m, o: (0, 0)),
            ],
            out_specs=(tile, tile, pl.BlockSpec((SUB, width), lambda i, m, o: (0, 0))) + (out,) * 4,
        ),
        out_shape=(
            shape((count, width)), shape((count, width), bf16), shape((SUB, width)),
        ) + (shape((count, features // 4)),) * 4,
        compiler_params=pltpu.CompilerParams(vmem_limit_bytes=VMEM_LIMIT),
        cost_estimate=small_cost(),
        name="recurrence_states",
    )(mine, order, ends, part, span, gate_pre, weight)


def run_turn(branch, weight, gate_pre, states, span):
    count, width = states.shape
    features = branch.shape[1]
    block = count // 4
    tile = pl.BlockSpec((block, width), lambda i: (i, 0))
    return pl.pallas_call(
        turn_kernel,
        grid=(4,),
        out_shape=(
            shape((count, width)), shape((count, width), bf16), shape((SUB, width)),
        ),
        in_specs=[
            pl.BlockSpec((block, features), lambda i: (i, 0)),
            pl.BlockSpec(weight.shape, lambda i: (0, 0)),
        ] + [tile] * 3,
        out_specs=(tile, tile, pl.BlockSpec((SUB, width), lambda i: (0, 0))),
        compiler_params=pltpu.CompilerParams(vmem_limit_bytes=VMEM_LIMIT),
        cost_estimate=small_cost(),
        name="recurrence_turn",
    )(branch, weight, gate_pre, states, span)


def feed_forward(order, low, gate, up, dhidden):
    count, features = low.shape
    hidden = gate.shape[1]
    block = 512
    tile = pl.BlockSpec((count, block), lambda i, o: (0, i))
    weight = pl.BlockSpec((features, block), lambda i, o: (0, i))
    out = pl.BlockSpec((count, features // 4), lambda i, o: (0, 0))
    return pl.pallas_call(
        feed_forward_kernel,
        grid_spec=pltpu.PrefetchScalarGridSpec(
            num_scalar_prefetch=1,
            grid=(hidden // block,),
            in_specs=[
                pl.BlockSpec((count, features), lambda i, o: (0, 0)), weight, weight, tile,
            ],
            out_specs=(tile,) * 3 + (out,) * 4,
        ),
        out_shape=(shape((count, hidden), bf16),) * 3 + (shape((count, features // 4)),) * 4,
        compiler_params=pltpu.CompilerParams(vmem_limit_bytes=VMEM_LIMIT),
        cost_estimate=small_cost(),
        name="feed_forward",
    )(order, low, gate, up, dhidden)


def product_blocks(order, lefts, rights, transposed):
    count = lefts[0].shape[0]
    features = rights[0].shape[0 if transposed else 1]
    return pl.pallas_call(
        partial(blocks_kernel, pairs=len(lefts), transposed=transposed),
        out_shape=(shape((count, features // 4)),) * 4,
        in_specs=[pl.BlockSpec(memory_space=pltpu.SMEM)] + vmem(2 * len(lefts)),
        out_specs=tuple(vmem(4)),
        compiler_params=pltpu.CompilerParams(vmem_limit_bytes=VMEM_LIMIT),
        cost_estimate=small_cost(),
        name="product_blocks",
    )(order, *lefts, *rights)


def product_sums(order, low, blocks):
    count, features = low.shape
    row, column = pl.pallas_call(
        sums_kernel,
        out_shape=(shape((count, 1)), shape((1, features))),
        in_specs=[pl.BlockSpec(memory_space=pltpu.SMEM)] + vmem(5),
        out_specs=tuple(vmem(2)),
        compiler_params=pltpu.CompilerParams(vmem_limit_bytes=VMEM_LIMIT),
        cost_estimate=small_cost(),
        name="product_sums",
    )(order, low, *blocks)
    return row[:, 0], column[0]


def product(left, right, block, transposed=False):
    count, inner = left.shape
    width = right.shape[0 if transposed else 1]
    right_tile = (
        pl.BlockSpec((block, inner), lambda i: (i, 0))
        if transposed
        else pl.BlockSpec((inner, block), lambda i: (0, i))
    )
    return pl.pallas_call(
        partial(product_kernel, transposed=transposed),
        grid=(width // block,),
        in_specs=[pl.BlockSpec(left.shape, lambda i: (0, 0)), right_tile],
        out_specs=pl.BlockSpec((count, block), lambda i: (0, i)),
        out_shape=shape((count, width)),
        compiler_params=pltpu.CompilerParams(vmem_limit_bytes=VMEM_LIMIT),
        cost_estimate=small_cost(),
        name="product",
    )(left, right)


def run_backward(mine, ends, dstates, saved, enter, valid, inner, halo, rows, gates, groups):
    count, width = dstates.shape
    return pl.pallas_call(
        partial(backward_kernel, groups=groups),
        out_shape=(
            shape((count, width), bf16), shape((2 * SUB, width)), shape((SUB, width)),
            shape((2, width // 2 + SUB * groups // 4, 2 * width // groups)),
        ),
        in_specs=[pl.BlockSpec(memory_space=pltpu.SMEM)] + vmem(14),
        out_specs=tuple(vmem(4)),
        scratch_shapes=[
            pltpu.VMEM((count + 2 * SUB, width), f32),
            pltpu.VMEM((count + SUB, width), f32),
            pltpu.VMEM((count, 2 * width), bf16),
            pltpu.VMEM((width, 2 * width), f32),
        ],
        compiler_params=pltpu.CompilerParams(vmem_limit_bytes=VMEM_LIMIT),
        cost_estimate=small_cost(),
        name="recurrence_backward",
    )(
        mine, ends, dstates, saved["alpha"], saved["states"], enter, saved["conv"], saved["rg"],
        saved["ig"], saved["factor"], valid, inner, halo, rows, gates,
    )


def columns_product_kernel(ring_ref, left_ref, *refs):
    out_ref = refs[-1]
    left = left_ref[...].T
    start = 0
    for right_ref in refs[:-1]:
        width = right_ref.shape[1]
        out_ref[:, start : start + width] = jnp.dot(
            left, right_ref[...], preferred_element_type=f32
        )
        start += width


def ring_order():
    devices = lax.axis_size("seq")
    return [0, 1, 3, 2, 6, 7, 5, 4] if devices == 8 else list(range(devices))


def ring_scatter(value):
    return lax.psum_scatter(
        value, "seq", scatter_dimension=0, axis_index_groups=[ring_order()], tiled=True
    )


def columns_product(left, rights):
    rows, columns = left.shape
    width = sum(right.shape[1] for right in rights)
    ring = ring_order()
    block = columns // len(ring)
    if block % LANES:
        whole = matmul_tn(left, jnp.concatenate(rights, 1)).reshape(len(ring), block, width)
        return jnp.concatenate([whole[d] for d in ring], 0)
    return pl.pallas_call(
        columns_product_kernel,
        grid_spec=pltpu.PrefetchScalarGridSpec(
            num_scalar_prefetch=1,
            grid=(len(ring),),
            in_specs=[pl.BlockSpec((rows, block), lambda j, ring: (0, ring[j]))]
            + [pl.BlockSpec(right.shape, lambda j, ring: (0, 0)) for right in rights],
            out_specs=pl.BlockSpec((block, width), lambda j, ring: (j, 0)),
        ),
        out_shape=shape((columns, width)),
        compiler_params=pltpu.CompilerParams(vmem_limit_bytes=VMEM_LIMIT),
        cost_estimate=small_cost(),
        name="columns_product",
    )(jnp.array(ring, jnp.int32), left, *rights)


def rows_product_kernel(left_ref, right_ref, out_ref, whole_ref, *, ring):
    whole_ref[...] = jnp.dot(left_ref[...].T, right_ref[...], preferred_element_type=f32)
    block = out_ref.shape[0] // len(ring)
    for j, d in enumerate(ring):
        out_ref[j * block : (j + 1) * block, :] = whole_ref[d * block : (d + 1) * block, :]


def rows_product(left, right, width):
    rows, columns = left.shape
    return pl.pallas_call(
        partial(rows_product_kernel, ring=ring_order()),
        grid=(right.shape[1] // width,),
        in_specs=[
            pl.BlockSpec(left.shape, lambda n: (0, 0)),
            pl.BlockSpec((rows, width), lambda n: (0, n)),
        ],
        out_specs=pl.BlockSpec((columns, width), lambda n: (0, n)),
        scratch_shapes=[pltpu.VMEM((columns, width), f32)],
        out_shape=shape((columns, right.shape[1])),
        compiler_params=pltpu.CompilerParams(vmem_limit_bytes=VMEM_LIMIT),
        cost_estimate=small_cost(),
        name="rows_product",
    )(left, right)


def block_diagonal(weights):
    groups, width, _ = weights.shape
    rows = [
        jnp.pad(weights[b], ((0, 0), (b * width, (groups - 1 - b) * width))) for b in range(groups)
    ]
    return jnp.concatenate(rows, 0)


def row_scale(squares, features):
    return lax.rsqrt(squares / features + norm_eps)[:, None]


def body(
    stream, doc_starts, gain_first, proj_inner, proj_gate, conv_weight, conv_bias, gate_recur,
    gate_input, bias_recur, bias_input, decay_param, proj_out, gain_second, mlp_gate, mlp_up,
    mlp_down, cotangent,
):
    count, own_width = stream.shape
    features = gain_first.shape[0]
    inner_width = proj_inner.shape[1]
    ffn_width = mlp_gate.shape[1]
    groups = gate_recur.shape[0]
    devices = lax.axis_size("seq")
    seq_at = lax.axis_index("seq").astype(jnp.int32).reshape(1)
    column = lax.axis_index("mp") * own_width
    own_first = lax.dynamic_slice_in_dim(gain_first, column, own_width)
    own_second = lax.dynamic_slice_in_dim(gain_second, column, own_width)
    order = block_order()
    onward = [(s, s + 1) for s in range(devices - 1)]
    backward = [(s + 1, s) for s in range(devices - 1)]


    first = LineGather(stream)
    first.first()
    first_scale = row_scale(line_sum(jnp.sum(stream * stream, axis=1)), features)
    starts = doc_starts.astype(f32)
    starts_before = lax.ppermute(starts[count - SUB :], "seq", onward)
    keep_ext = 1.0 - jnp.concatenate([starts_before, starts], 0)
    reach = [keep_ext[SUB:]]
    for k in range(1, 4):
        reach.append(
            (reach[-1] if k > 1 else 1.0) * keep_ext[SUB - k + 1 : SUB - k + 1 + count]
        )
    valid = jnp.broadcast_to(jnp.stack(reach, 0)[:, :, None], (4, count, LANES))
    valid = jnp.pad(valid, ((0, 0), (SUB, SUB), (0, 0)))
    rows = jnp.stack(
        [
            conv_weight[0], conv_weight[1], conv_weight[2], conv_weight[3], conv_bias, bias_recur,
            bias_input, -recur_scale * jax.nn.softplus(-decay_param),
        ],
        0,
    )
    gates = jnp.concatenate([block_diagonal(gate_recur), block_diagonal(gate_input)], 1)
    first.second()
    first.third(gates, valid)

    def first_turn(piece, start):
        return piece * first_scale * lax.dynamic_slice_in_dim(gain_first, start, own_width)

    first_low = assemble(first.pieces(), features, first_turn)
    cot = LineGather(cotangent)
    cot.first(first.far_out)
    inner = matmul(first_low, proj_inner)
    halo = lax.ppermute(inner[count - SUB :], "seq", onward)
    gate_pre = matmul(after(first_low, inner), proj_gate)
    halo = after(halo, gate_pre)
    conv, conv_low, rg, ig, alpha, factor, part, span, last = run_forward(
        inner, halo, valid, rows, gates
    )
    ends = after(lax.all_gather(last, "seq"), cot.beside, cot.near_in)
    cot.second()
    states, mixed_low, enter, *blocks = run_states(
        seq_at, order, ends, part, span, gate_pre, proj_out
    )

    branch = LineScatter(blocks)
    branch.first()
    branch.second(cot.far_in, cot.near_out)
    cot.third()
    branch.third(cot.far_out)
    cot_low = assemble(cot.pieces(), features, lambda piece, start: piece)
    d_hidden = product(cot_low, mlp_down, 2 * LANES, True)
    own_resid = stream + branch.result()

    second = LineGather(own_resid)
    second.first()
    second_scale = row_scale(line_sum(jnp.sum(own_resid * own_resid, axis=1)), features)
    second.second(d_hidden)
    second.third()

    def second_turn(piece, start):
        return piece * second_scale * lax.dynamic_slice_in_dim(gain_second, start, own_width)

    second_low = assemble(second.pieces(), features, second_turn)
    hidden_low, d_gate_ffn, d_up_ffn, *d_second_blocks = feed_forward(
        order, second_low, mlp_gate, mlp_up, d_hidden
    )
    turned = LineScatter(d_second_blocks)
    whole_down = rows_product(hidden_low, cot_low, own_width)
    grad_down = ring_scatter(whole_down)
    turned.first(whole_down)
    whole_pair = columns_product(after(second_low, turned.own), [d_gate_ffn, d_up_ffn])
    turned.second(whole_pair)
    whole_pair = after(whole_pair, turned.far_one)
    grad_pair = ring_scatter(whole_pair)
    second_sums, gain_sums = product_sums(
        order, second_low, after(d_second_blocks, turned.far_one)
    )
    second_mean = line_sum(second_sums) / features
    d_gain_second = gain_sums / gain_second
    turned.third(d_gain_second, second_mean)
    mlp_blocks = product_blocks(
        order, [after(hidden_low, turned.far_two, turned.near_one)], [mlp_down], False
    )
    own_d_second = turned.result()
    own_d_resid = (
        cotangent
        + second_scale * (own_second * own_d_second)
        - own_resid * (second_scale * second_scale * second_mean[:, None])
    )
    gathered = LineGather(own_d_resid)
    gathered.first(mlp_blocks)
    gathered.second()
    sent = LineScatter(mlp_blocks)
    sent.first(gathered.near_in, gathered.beside)
    gathered.third(sent.far_one, grad_down)
    sent.second(gathered.near_out)
    branch_low = assemble(gathered.pieces(), features, lambda piece, start: piece)

    d_states, d_gate_low, outgoing = run_turn(
        after(branch_low, sent.far_two, sent.near_one), proj_out, gate_pre, states, span
    )
    leaving = jnp.stack([last[0], jnp.sum(outgoing, axis=0)], 0)
    leaving = after(leaving, sent.prepare())
    sent.third()
    back_ends = after(lax.all_gather(leaving, "seq"), sent.last, sent.near_two)
    saved = dict(alpha=alpha, states=states, conv=conv, rg=rg, ig=ig, factor=factor)
    d_inner_low, tail, head, small = run_backward(
        seq_at, back_ends, d_states, saved, enter, valid, inner, halo, rows, gates, groups
    )
    returned = lax.ppermute(head, "seq", backward)
    whole_out = rows_product(after(mixed_low, head), branch_low, 2 * own_width)
    grad_out = ring_scatter(whole_out)
    returned = after(returned, whole_out)
    tail = tail + jnp.concatenate([jnp.zeros_like(returned), returned], 0)
    d_inner_low = lax.dynamic_update_slice(d_inner_low, tail.astype(bf16), (count - 2 * SUB, 0))
    d_first_blocks = product_blocks(
        order, [d_inner_low, d_gate_low], [proj_inner, proj_gate], True
    )

    final = LineScatter(d_first_blocks)
    final.first(grad_pair)
    whole_first = columns_product(
        after(first_low, final.own), [d_inner_low, d_gate_low]
    )
    first_mean, gain_sums = product_sums(
        order, after(first_low, whole_first), d_first_blocks
    )
    d_gain_first = gain_sums / gain_first
    output = after(own_resid, final.own) + sent.result()
    core = lax.axis_index("seq") & 1
    other = swapped(lax.dynamic_index_in_dim(small, 1 - core, 0, False), "seq", 1)
    small = lax.dynamic_index_in_dim(small, core, 0, False) + other
    final.second(whole_first, first_mean, d_gain_first, grad_out, output, small)
    whole_first, first_mean, d_gain_first = after(
        (whole_first, first_mean, d_gain_first), final.far_one
    )
    grad_first = ring_scatter(whole_first)
    small = over_chips(small, 2)
    first_sums = jnp.concatenate([first_mean, d_gain_first, d_gain_second])
    first_sums = first_sums + over_mp(first_sums, PAIRS)
    final.third(first_sums, small)
    first_sums, small = after((first_sums, small), final.far_two, final.near_one)
    first_sums = first_sums + over_mp(first_sums, CROSS)
    first_mean = first_sums[:count] / features
    small = over_chips(small, 4)
    gains = sum_over(first_sums[count:], "seq")
    small, gains = after((small, gains), final.last)
    other = swapped(small, "seq", 1)
    small = [jnp.where(core == 0, small, other), jnp.where(core == 0, other, small)]
    own_d_first = final.result()
    grad_stream = (
        own_d_resid
        + first_scale * (own_first * own_d_first)
        - stream * (first_scale * first_scale * first_mean[:, None])
    )
    block_width = inner_width // groups
    half = inner_width // 2
    sums = [
        part[half + b * SUB : half + (b + 1) * SUB] for part in small for b in range(groups // 4)
    ]
    sums = jnp.concatenate(sums, 1)
    grad_gates = [
        jnp.concatenate(
            [part[:half, g * block_width : (g + 1) * block_width] for part in small], 0
        ).reshape(groups, block_width, block_width)
        for g in range(2)
    ]
    grad_decay = sums[7] * (recur_scale * jax.nn.sigmoid(-decay_param))
    return (
        output,
        grad_stream,
        gains[:features],
        grad_first[:, :inner_width],
        grad_first[:, inner_width:],
        sums[:4],
        sums[4],
        grad_gates[0],
        grad_gates[1],
        sums[5],
        sums[6],
        grad_decay,
        grad_out,
        gains[features:],
        grad_pair[:, :ffn_width],
        grad_pair[:, ffn_width:],
        grad_down,
    )


def solution(mesh):
    in_specs = (
        P("seq", "mp"),
        P("seq"),
        P(),
        P(None, "mp"),
        P(None, "mp"),
        P(None, "mp"),
        P("mp"),
        P("mp", None, None),
        P("mp", None, None),
        P("mp"),
        P("mp"),
        P("mp"),
        P("mp", None),
        P(),
        P(None, "mp"),
        P(None, "mp"),
        P("mp", None),
        P("seq", "mp"),
    )
    out_specs = (
        P("seq", "mp"),
        P("seq", "mp"),
        P(),
        P("seq", "mp"),
        P("seq", "mp"),
        P(None, "mp"),
        P("mp"),
        P("mp", None, None),
        P("mp", None, None),
        P("mp"),
        P("mp"),
        P("mp"),
        P(("mp", "seq"), None),
        P(),
        P("seq", "mp"),
        P("seq", "mp"),
        P(("mp", "seq"), None),
    )
    return jax.shard_map(body, mesh=mesh, in_specs=in_specs, out_specs=out_specs, check_vma=False)
```

```python
from functools import partial

import jax
import jax.numpy as jnp
from jax import lax
from jax.experimental import pallas as pl
from jax.experimental.pallas import tpu as pltpu
from jax.sharding import PartitionSpec as P

recur_scale = 8.0
norm_eps = 1e-06
bf16 = jnp.bfloat16
f32 = jnp.float32
LANES = 128
SUB = 8
ROWS = 32
VMEM_LIMIT = 56 * 1024 * 1024
VMEM_SMALL = 24 * 1024 * 1024


def matmul(left, right):
    return jnp.dot(left, right, preferred_element_type=f32)


def matmul_nt(left, right):
    return lax.dot_general(left, right, (((1,), (1,)), ((), ())), preferred_element_type=f32)


def matmul_tn(left, right):
    return lax.dot_general(left, right, (((0,), (0,)), ((), ())), preferred_element_type=f32)


PAIRS = ((0, 1), (1, 0), (2, 3), (3, 2))
MIDDLE = ((1, 2), (2, 1))
OUTWARD = ((1, 0), (2, 3))
INWARD = ((0, 1), (3, 2))
CROSS = ((0, 2), (2, 0), (1, 3), (3, 1))


def over_mp(value, pairs):
    return lax.ppermute(value, "mp", list(pairs))


def line_places():
    mine = lax.axis_index("mp")
    half = mine >> 1
    return mine, mine ^ 1, 2 - half, 3 - 3 * half


def after(value, *needed):
    return lax.optimization_barrier((value, needed))[0]


class LineGather:
    def __init__(self, own):
        self.own = own

    def first(self, *needed):
        own = after(self.own, *needed)
        self.beside, self.near_in = over_mp(own, PAIRS), over_mp(own, MIDDLE)
        return self.beside, self.near_in

    def second(self, *needed):
        near, beside = after((self.near_in, self.beside), *needed)
        self.near_out, self.far_in = over_mp(near, OUTWARD), over_mp(beside, MIDDLE)
        return self.near_out, self.far_in

    def third(self, *needed):
        far, _ = after((self.far_in, self.near_out), *needed)
        self.far_out = over_mp(far, OUTWARD)
        return self.far_out

    def pieces(self):
        return self.own, self.beside, self.near_in + self.near_out, self.far_in + self.far_out


class LineScatter:
    def __init__(self, blocks):
        self.far, self.near, self.beside, self.own = blocks

    def first(self, *needed):
        self.far_one = over_mp(after(self.far, *needed), INWARD)
        return self.far_one

    def second(self, *needed):
        far, near = after((self.far + self.far_one, self.near), *needed)
        self.far_two, self.near_one = over_mp(far, MIDDLE), over_mp(near, INWARD)
        return self.far_two, self.near_one

    def prepare(self):
        self.parts = (self.near + self.near_one, self.beside + self.far_two)
        return self.parts

    def third(self, *needed):
        near, last = after(self.prepare(), *needed)
        self.near_two, self.last = over_mp(near, MIDDLE), over_mp(last, PAIRS)
        return self.near_two, self.last

    def result(self):
        return self.own + self.near_two + self.last


def block_order():
    mine, beside, near, far = line_places()
    return jnp.stack([far, near, beside, mine]).astype(jnp.int32)


def line_sum(value):
    value = value + over_mp(value, PAIRS)
    return value + over_mp(value, CROSS)


def swapped(value, axis, bit):
    count = lax.axis_size(axis)
    return lax.ppermute(value, axis, [(d, d ^ bit) for d in range(count)])


def over_chips(value, bit):
    devices = lax.axis_size("seq")
    value = value + swapped(value, "seq", bit)
    while bit > 2 and 2 * bit < devices:
        bit *= 2
        value = value + swapped(value, "seq", bit)
    return value


def sum_over(value, axis):
    bit = 1
    while bit < lax.axis_size(axis):
        value = value + swapped(value, axis, bit)
        bit *= 2
    return value


def assemble(pieces, width, turn):
    rows, own_width = pieces[0].shape
    whole = jnp.zeros((rows, width), bf16)
    for piece, place in zip(pieces, line_places()):
        start = place * own_width
        whole = lax.dynamic_update_slice(whole, turn(piece, start).astype(bf16), (0, start))
    return whole


def wide(value, width):
    return jnp.concatenate([value] * (width // LANES), axis=-1)


def neg_expm1(x, e):
    poly = 1.0 / 40320.0
    for term in (5040.0, 720.0, 120.0, 24.0, 6.0, 2.0, 1.0):
        poly = poly * x + 1.0 / term
    return jnp.where(x > -0.5, -x * poly, 1.0 - e)


def gelu_parts(x):
    scale = 0.7978845608028654
    cube = 0.044715
    squared = x * x
    t = jnp.tanh(scale * (x + cube * x * squared))
    half = 0.5 * (1.0 + t)
    slope = half + 0.5 * x * (1.0 - t * t) * scale * (1.0 + 3.0 * cube * squared)
    return half * x, slope


def group_scan(a, b):
    place = lax.broadcasted_iota(jnp.int32, a.shape, 1)
    for k in (1, 2, 4):
        fits = place >= k
        b = jnp.where(fits, a * pltpu.roll(b, k, 1) + b, b)
        a = jnp.where(fits, a * pltpu.roll(a, k, 1), a)
    return a, b


def group_scan_back(a, b):
    place = lax.broadcasted_iota(jnp.int32, a.shape, 1)
    for k in (1, 2, 4):
        fits = place < SUB - k
        b = jnp.where(fits, a * pltpu.roll(b, SUB - k, 1) + b, b)
        a = jnp.where(fits, a * pltpu.roll(a, SUB - k, 1), a)
    return a, b


def forward_kernel(
    inner_ref, halo_ref, valid_ref, row_ref, gate_ref,
    conv_ref, low_ref, rg_ref, ig_ref, alpha_ref, factor_ref, part_ref, span_ref, last_ref,
    ext_ref, pre_ref,
):
    count, width = inner_ref.shape
    ext_ref[pl.ds(0, SUB), :] = halo_ref[...]

    def fill(i, _):
        r = pl.multiple_of(i * ROWS, ROWS)
        ext_ref[pl.ds(r + SUB, ROWS), :] = inner_ref[pl.ds(r, ROWS), :]
        return 0

    lax.fori_loop(0, count // ROWS, fill, 0)

    def convolve(i, _):
        r = pl.multiple_of(i * ROWS, ROWS)
        window = ext_ref[pl.ds(r, ROWS + SUB), :]
        total = row_ref[0:1, :] * window[SUB:]
        for k in range(1, 4):
            valid = wide(valid_ref[k, pl.ds(r + SUB, ROWS), :], width)
            total = total + row_ref[k : k + 1, :] * window[SUB - k : SUB - k + ROWS] * valid
        total = total + row_ref[4:5, :]
        conv_ref[pl.ds(r, ROWS), :] = total
        low_ref[pl.ds(r, ROWS), :] = total.astype(bf16)
        return 0

    lax.fori_loop(0, count // ROWS, convolve, 0)
    pre_ref[...] = jnp.dot(low_ref[...], gate_ref[...], preferred_element_type=f32)

    def scan(i, carry):
        r = pl.multiple_of(i * ROWS, ROWS)
        here = pl.ds(r, ROWS)
        rg = jax.nn.sigmoid(pre_ref[here, :width] + row_ref[5:6, :])
        ig = jax.nn.sigmoid(pre_ref[here, width:] + row_ref[6:7, :])
        log_a = row_ref[7:8, :] * rg
        keep = wide(valid_ref[0, pl.ds(r + SUB, ROWS), :], width)
        a = jnp.exp(log_a)
        root = jnp.sqrt(neg_expm1(2.0 * log_a, a * a))
        factor = (1.0 - keep) + keep * root
        alpha = a * keep
        beta = factor * ig * conv_ref[here, :]
        rg_ref[here, :] = rg
        ig_ref[here, :] = ig
        alpha_ref[here, :] = alpha
        factor_ref[here, :] = factor
        groups = (ROWS // SUB, SUB, width)
        a3, b3 = group_scan(alpha.reshape(groups), beta.reshape(groups))
        state, product = carry
        for g in range(ROWS // SUB):
            part = b3[g] + a3[g] * state
            span = a3[g] * product
            part_ref[pl.ds(r + g * SUB, SUB), :] = part
            span_ref[pl.ds(r + g * SUB, SUB), :] = span
            state, product = part[SUB - 1 : SUB, :], span[SUB - 1 : SUB, :]
        return state, product

    zero = jnp.zeros((1, width), f32)
    state, product = lax.fori_loop(0, count // ROWS, scan, (zero, zero + 1.0))
    last_ref[...] = jnp.concatenate([product, state, jnp.zeros((SUB - 2, width), f32)], 0)


def state_kernel(
    mine_ref, order_ref, ends_ref, part_ref, span_ref, gate_ref, weight_ref,
    states_ref, mixed_ref, enter_ref, *block_refs,
):
    devices = ends_ref.shape[0]
    width = part_ref.shape[1]
    entering = jnp.zeros((1, width), f32)
    for d in range(devices):
        ends = ends_ref[d]
        entering = jnp.where(d < mine_ref[0], ends[0:1, :] * entering + ends[1:2, :], entering)
    states = span_ref[...] * entering + part_ref[...]
    states_ref[...] = states
    mixed = (gelu_parts(gate_ref[...])[0] * states).astype(bf16)
    mixed_ref[...] = mixed
    enter_ref[...] = jnp.broadcast_to(entering, enter_ref.shape)
    for k, block_ref in enumerate(block_refs):
        block = block_ref.shape[1]
        columns = pl.ds(pl.multiple_of(order_ref[k] * block, block), block)
        block_ref[...] = jnp.dot(mixed, weight_ref[:, columns], preferred_element_type=f32)


def turn_kernel(
    branch_ref, weight_ref, gate_ref, states_ref, span_ref, dstates_ref, dgate_ref, out_ref
):
    act, slope = gelu_parts(gate_ref[...])
    dmixed = lax.dot_general(
        branch_ref[...], weight_ref[...], (((1,), (1,)), ((), ())), preferred_element_type=f32
    )
    dstates = dmixed * act
    dstates_ref[...] = dstates
    dgate_ref[...] = (dmixed * states_ref[...] * slope).astype(bf16)

    @pl.when(pl.program_id(0) == 0)
    def _():
        out_ref[...] = jnp.zeros_like(out_ref)

    out_ref[...] += jnp.sum(
        (dstates * span_ref[...]).reshape(-1, SUB, dstates.shape[1]), axis=0
    )


def feed_forward_kernel(
    low_ref, gate_ref, up_ref, dhidden_ref, hidden_ref, dgate_ref, dup_ref
):
    low = low_ref[...]
    gate = jnp.dot(low, gate_ref[...], preferred_element_type=f32)
    up = jnp.dot(low, up_ref[...], preferred_element_type=f32)
    act, slope = gelu_parts(gate)
    dhidden = dhidden_ref[...]
    hidden_ref[...] = (act * up).astype(bf16)
    dgate_ref[...] = (dhidden * up * slope).astype(bf16)
    dup_ref[...] = (dhidden * act).astype(bf16)


def blocks_kernel(order_ref, *refs, pairs, transposed):
    for k, block_ref in enumerate(refs[2 * pairs :]):
        block = block_ref.shape[1]
        here = pl.ds(pl.multiple_of(order_ref[k] * block, block), block)
        total = None
        for left_ref, right_ref in zip(refs[:pairs], refs[pairs : 2 * pairs]):
            if transposed:
                part = lax.dot_general(
                    left_ref[...], right_ref[here, :], (((1,), (1,)), ((), ())),
                    preferred_element_type=f32,
                )
            else:
                part = jnp.dot(left_ref[...], right_ref[:, here], preferred_element_type=f32)
            total = part if total is None else total + part
        block_ref[...] = total


def sums_kernel(order_ref, low_ref, *refs):
    row_ref, column_ref = refs[-2:]
    rows = 0.0
    for k, block_ref in enumerate(refs[:-2]):
        block = block_ref.shape[1]
        here = pl.ds(pl.multiple_of(order_ref[k] * block, block), block)
        product = block_ref[...] * low_ref[:, here].astype(f32)
        rows = rows + jnp.sum(product, axis=1, keepdims=True)
        column_ref[:, here] = jnp.sum(product, axis=0, keepdims=True)
    row_ref[...] = rows


def product_kernel(left_ref, right_ref, out_ref, *, transposed):
    contract = (((1,), (1,)), ((), ())) if transposed else (((1,), (0,)), ((), ()))
    out_ref[...] = lax.dot_general(
        left_ref[...], right_ref[...], contract, preferred_element_type=f32
    )


def backward_kernel(
    mine_ref, ends_ref, dstates_ref, alpha_ref, states_ref, enter_ref, conv_ref, rg_ref, ig_ref,
    factor_ref, valid_ref, inner_ref, halo_ref, row_ref, gate_ref,
    dinner_ref, tail_ref, head_ref, small_ref,
    dconv_ref, ext_ref, drec_ref, whole_ref, *, groups,
):
    devices = ends_ref.shape[0]
    count, width = alpha_ref.shape
    blocks = count // ROWS
    incoming = jnp.zeros((1, width), f32)
    for d in reversed(range(devices)):
        ends = ends_ref[d]
        incoming = jnp.where(d > mine_ref[0], ends[0:1, :] * incoming + ends[1:2, :], incoming)
    dconv_ref[pl.ds(0, SUB), :] = jnp.zeros((SUB, width), f32)
    dconv_ref[pl.ds(count + SUB, SUB), :] = jnp.zeros((SUB, width), f32)
    ext_ref[pl.ds(0, SUB), :] = halo_ref[...]
    parts = (ROWS // SUB, SUB, width)
    place = lax.broadcasted_iota(jnp.int32, (SUB, width), 0)

    def fold(value):
        return jnp.sum(value.reshape(parts), axis=0)

    def back(step, carry):
        flow, decay, bias_r, bias_i = carry
        i = blocks - 1 - step
        r = pl.multiple_of(i * ROWS, ROWS)
        here = pl.ds(r, ROWS)
        ext_ref[pl.ds(r + SUB, ROWS), :] = inner_ref[here, :]
        alpha = alpha_ref[here, :]
        dstates = dstates_ref[here, :]
        a3, b3 = group_scan_back(alpha.reshape(parts), (alpha * dstates).reshape(parts))
        d3 = dstates.reshape(parts)
        totals = [None] * (ROWS // SUB)
        for g in reversed(range(ROWS // SUB)):
            flows = b3[g] + a3[g] * flow
            later = jnp.where(place == SUB - 1, flow, pltpu.roll(flows, SUB - 1, 0))
            totals[g] = d3[g] + later
            flow = flows[0:1, :]
        total = jnp.concatenate(totals, 0)
        before = pl.multiple_of(jnp.maximum(r - SUB, 0), SUB)
        first = jnp.where(i == 0, enter_ref[...], states_ref[pl.ds(before, SUB), :])
        window = jnp.concatenate([first, states_ref[here, :]], 0)
        prior = window[SUB - 1 : SUB - 1 + ROWS]
        rg = rg_ref[here, :]
        ig = ig_ref[here, :]
        factor = factor_ref[here, :]
        conv = conv_ref[here, :]
        gain = total * factor
        dconv_ref[pl.ds(r + SUB, ROWS), :] = gain * ig
        dinput = (gain * conv * ig * (1.0 - ig)).astype(bf16)
        dlog = alpha * (total * prior - total * ig * conv * alpha / factor)
        drecur = (dlog * row_ref[7:8, :] * rg * (1.0 - rg)).astype(bf16)
        drec_ref[here, :width] = drecur
        drec_ref[here, width:] = dinput
        return (
            flow,
            decay + fold(dlog * rg),
            bias_r + fold(drecur.astype(f32)),
            bias_i + fold(dinput.astype(f32)),
        )

    zero = jnp.zeros((SUB, width), f32)
    _, decay, bias_r, bias_i = lax.fori_loop(0, blocks, back, (incoming, zero, zero, zero))
    dconv_ref[pl.ds(SUB, count), :] += lax.dot_general(
        drec_ref[...], gate_ref[...], (((1,), (1,)), ((), ())), preferred_element_type=f32
    )

    def spread_back(window, r, rows):
        total = row_ref[0:1, :] * window[:rows]
        for k in range(1, 4):
            valid = wide(valid_ref[k, pl.ds(r, rows + SUB), :], width)
            total = total + row_ref[k : k + 1, :] * (window * valid)[k : k + rows]
        return total

    head_ref[...] = spread_back(dconv_ref[pl.ds(0, 2 * SUB), :], 0, SUB)

    def finish(i, carry):
        r = pl.multiple_of(i * ROWS, ROWS)
        window = dconv_ref[pl.ds(r + SUB, ROWS + SUB), :]
        total = spread_back(window, r + SUB, ROWS)
        dinner_ref[pl.ds(r, ROWS), :] = total.astype(bf16)

        @pl.when(i == blocks - 1)
        def _():
            tail_ref[...] = total[ROWS - 2 * SUB :]

        dconv = window[:ROWS]
        inputs = ext_ref[pl.ds(r, ROWS + SUB), :]
        sums = [fold(dconv * inputs[SUB:])]
        for k in range(1, 4):
            valid = wide(valid_ref[k, pl.ds(r + SUB, ROWS), :], width)
            sums.append(fold(dconv * valid * inputs[SUB - k : SUB - k + ROWS]))
        sums.append(fold(dconv))
        return tuple(c + s for c, s in zip(carry, sums))

    sums = lax.fori_loop(0, blocks, finish, (zero,) * 5)
    sums = jnp.concatenate(
        [jnp.sum(s, axis=0, keepdims=True) for s in (*sums, bias_r, bias_i, decay)], 0
    )
    whole_ref[...] = lax.dot_general(
        conv_ref[...].astype(bf16), drec_ref[...], (((0,), (0,)), ((), ())),
        preferred_element_type=f32,
    )
    block = width // groups
    left = lax.broadcasted_iota(jnp.int32, (block, width), 1) < block

    def turned(value, shift):
        return pltpu.roll(value, shift % width, 1) if shift % width else value

    for b in range(groups):
        here = slice(b * block, (b + 1) * block)
        recur = turned(whole_ref[here, :width], -b * block)
        entry = turned(whole_ref[here, width:], block - b * block)
        small_ref[2 * b // groups, b % (groups // 2) * block : (b % (groups // 2) + 1) * block, :] = (
            jnp.where(left, recur, entry)[:, : 2 * block]
        )
    for h in range(2):
        for b in range(groups // 4):
            small_ref[h, width // 2 + b * SUB : width // 2 + (b + 1) * SUB, :] = turned(
                sums, -2 * (h * (groups // 4) + b) * block
            )[:, : 2 * block]


def vmem(count=1):
    return [pl.BlockSpec(memory_space=pltpu.VMEM)] * count


def shape(dims, kind=f32):
    return jax.ShapeDtypeStruct(dims, kind)


def small_cost():
    return pl.CostEstimate(flops=1000, bytes_accessed=1000, transcendentals=0)


def run_forward(inner, halo, valid, rows, gates):
    count, width = inner.shape
    full = shape((count, width))
    return pl.pallas_call(
        forward_kernel,
        out_shape=(full, shape((count, width), bf16)) + (full,) * 6 + (shape((SUB, width)),),
        in_specs=vmem(5),
        out_specs=tuple(vmem(9)),
        scratch_shapes=[
            pltpu.VMEM((count + SUB, width), f32),
            pltpu.VMEM((count, 2 * width), f32),
        ],
        compiler_params=pltpu.CompilerParams(vmem_limit_bytes=VMEM_LIMIT),
        cost_estimate=small_cost(),
        name="recurrence_forward",
    )(inner, halo, valid, rows, gates)


def run_states(mine, order, ends, part, span, gate_pre, weight):
    count, width = part.shape
    features = weight.shape[1]
    block = count // 4
    tile = pl.BlockSpec((block, width), lambda i, m, o: (i, 0))
    out = pl.BlockSpec((block, features // 4), lambda i, m, o: (i, 0))
    return pl.pallas_call(
        state_kernel,
        grid_spec=pltpu.PrefetchScalarGridSpec(
            num_scalar_prefetch=2,
            grid=(4,),
            in_specs=[
                pl.BlockSpec(ends.shape, lambda i, m, o: (0, 0, 0)),
                tile, tile, tile,
                pl.BlockSpec(weight.shape, lambda i, m, o: (0, 0)),
            ],
            out_specs=(tile, tile, pl.BlockSpec((SUB, width), lambda i, m, o: (0, 0))) + (out,) * 4,
        ),
        out_shape=(
            shape((count, width)), shape((count, width), bf16), shape((SUB, width)),
        ) + (shape((count, features // 4)),) * 4,
        compiler_params=pltpu.CompilerParams(vmem_limit_bytes=VMEM_SMALL),
        cost_estimate=small_cost(),
        name="recurrence_states",
    )(mine, order, ends, part, span, gate_pre, weight)


def run_turn(branch, weight, gate_pre, states, span):
    count, width = states.shape
    features = branch.shape[1]
    block = count // 4
    tile = pl.BlockSpec((block, width), lambda i: (i, 0))
    return pl.pallas_call(
        turn_kernel,
        grid=(4,),
        out_shape=(
            shape((count, width)), shape((count, width), bf16), shape((SUB, width)),
        ),
        in_specs=[
            pl.BlockSpec((block, features), lambda i: (i, 0)),
            pl.BlockSpec(weight.shape, lambda i: (0, 0)),
        ] + [tile] * 3,
        out_specs=(tile, tile, pl.BlockSpec((SUB, width), lambda i: (0, 0))),
        compiler_params=pltpu.CompilerParams(vmem_limit_bytes=VMEM_SMALL),
        cost_estimate=small_cost(),
        name="recurrence_turn",
    )(branch, weight, gate_pre, states, span)


def feed_forward(low, gate, up, dhidden):
    count, features = low.shape
    hidden = gate.shape[1]
    block = 512
    tile = pl.BlockSpec((count, block), lambda i: (0, i))
    weight = pl.BlockSpec((features, block), lambda i: (0, i))
    return pl.pallas_call(
        feed_forward_kernel,
        grid=(hidden // block,),
        in_specs=[pl.BlockSpec((count, features), lambda i: (0, 0)), weight, weight, tile],
        out_specs=(tile,) * 3,
        out_shape=(shape((count, hidden), bf16),) * 3,
        compiler_params=pltpu.CompilerParams(vmem_limit_bytes=VMEM_LIMIT),
        cost_estimate=small_cost(),
        name="feed_forward",
    )(low, gate, up, dhidden)


def product_blocks(order, lefts, rights, transposed):
    count = lefts[0].shape[0]
    features = rights[0].shape[0 if transposed else 1]
    return pl.pallas_call(
        partial(blocks_kernel, pairs=len(lefts), transposed=transposed),
        out_shape=(shape((count, features // 4)),) * 4,
        in_specs=[pl.BlockSpec(memory_space=pltpu.SMEM)] + vmem(2 * len(lefts)),
        out_specs=tuple(vmem(4)),
        compiler_params=pltpu.CompilerParams(vmem_limit_bytes=VMEM_LIMIT),
        cost_estimate=small_cost(),
        name="product_blocks",
    )(order, *lefts, *rights)


def product_sums(order, low, blocks):
    count, features = low.shape
    row, column = pl.pallas_call(
        sums_kernel,
        out_shape=(shape((count, 1)), shape((1, features))),
        in_specs=[pl.BlockSpec(memory_space=pltpu.SMEM)] + vmem(5),
        out_specs=tuple(vmem(2)),
        compiler_params=pltpu.CompilerParams(vmem_limit_bytes=VMEM_LIMIT),
        cost_estimate=small_cost(),
        name="product_sums",
    )(order, low, *blocks)
    return row[:, 0], column[0]


def product(left, right, block, transposed=False):
    count, inner = left.shape
    width = right.shape[0 if transposed else 1]
    right_tile = (
        pl.BlockSpec((block, inner), lambda i: (i, 0))
        if transposed
        else pl.BlockSpec((inner, block), lambda i: (0, i))
    )
    return pl.pallas_call(
        partial(product_kernel, transposed=transposed),
        grid=(width // block,),
        in_specs=[pl.BlockSpec(left.shape, lambda i: (0, 0)), right_tile],
        out_specs=pl.BlockSpec((count, block), lambda i: (0, i)),
        out_shape=shape((count, width)),
        compiler_params=pltpu.CompilerParams(vmem_limit_bytes=VMEM_LIMIT),
        cost_estimate=small_cost(),
        name="product",
    )(left, right)


def run_backward(mine, ends, dstates, saved, enter, valid, inner, halo, rows, gates, groups):
    count, width = dstates.shape
    return pl.pallas_call(
        partial(backward_kernel, groups=groups),
        out_shape=(
            shape((count, width), bf16), shape((2 * SUB, width)), shape((SUB, width)),
            shape((2, width // 2 + SUB * groups // 4, 2 * width // groups)),
        ),
        in_specs=[pl.BlockSpec(memory_space=pltpu.SMEM)] + vmem(14),
        out_specs=tuple(vmem(4)),
        scratch_shapes=[
            pltpu.VMEM((count + 2 * SUB, width), f32),
            pltpu.VMEM((count + SUB, width), f32),
            pltpu.VMEM((count, 2 * width), bf16),
            pltpu.VMEM((width, 2 * width), f32),
        ],
        compiler_params=pltpu.CompilerParams(vmem_limit_bytes=VMEM_LIMIT),
        cost_estimate=small_cost(),
        name="recurrence_backward",
    )(
        mine, ends, dstates, saved["alpha"], saved["states"], enter, saved["conv"], saved["rg"],
        saved["ig"], saved["factor"], valid, inner, halo, rows, gates,
    )


def columns_product_kernel(ring_ref, left_ref, *refs):
    out_ref = refs[-1]
    left = left_ref[...].T
    start = 0
    for right_ref in refs[:-1]:
        width = right_ref.shape[1]
        out_ref[:, start : start + width] = jnp.dot(
            left, right_ref[...], preferred_element_type=f32
        )
        start += width


def ring_order():
    devices = lax.axis_size("seq")
    return [0, 1, 3, 2, 6, 7, 5, 4] if devices == 8 else list(range(devices))


def ring_scatter(value):
    return lax.psum_scatter(
        value, "seq", scatter_dimension=0, axis_index_groups=[ring_order()], tiled=True
    )


def columns_product(left, rights):
    rows, columns = left.shape
    width = sum(right.shape[1] for right in rights)
    ring = ring_order()
    block = columns // len(ring)
    if block % LANES:
        whole = matmul_tn(left, jnp.concatenate(rights, 1)).reshape(len(ring), block, width)
        return jnp.concatenate([whole[d] for d in ring], 0)
    return pl.pallas_call(
        columns_product_kernel,
        grid_spec=pltpu.PrefetchScalarGridSpec(
            num_scalar_prefetch=1,
            grid=(len(ring),),
            in_specs=[pl.BlockSpec((rows, block), lambda j, ring: (0, ring[j]))]
            + [pl.BlockSpec(right.shape, lambda j, ring: (0, 0)) for right in rights],
            out_specs=pl.BlockSpec((block, width), lambda j, ring: (j, 0)),
        ),
        out_shape=shape((columns, width)),
        compiler_params=pltpu.CompilerParams(vmem_limit_bytes=VMEM_LIMIT),
        cost_estimate=small_cost(),
        name="columns_product",
    )(jnp.array(ring, jnp.int32), left, *rights)


def rows_product_kernel(left_ref, right_ref, out_ref, whole_ref, *, ring):
    whole_ref[...] = jnp.dot(left_ref[...].T, right_ref[...], preferred_element_type=f32)
    block = out_ref.shape[0] // len(ring)
    for j, d in enumerate(ring):
        out_ref[j * block : (j + 1) * block, :] = whole_ref[d * block : (d + 1) * block, :]


def rows_product(left, right, width):
    rows, columns = left.shape
    return pl.pallas_call(
        partial(rows_product_kernel, ring=ring_order()),
        grid=(right.shape[1] // width,),
        in_specs=[
            pl.BlockSpec(left.shape, lambda n: (0, 0)),
            pl.BlockSpec((rows, width), lambda n: (0, n)),
        ],
        out_specs=pl.BlockSpec((columns, width), lambda n: (0, n)),
        scratch_shapes=[pltpu.VMEM((columns, width), f32)],
        out_shape=shape((columns, right.shape[1])),
        compiler_params=pltpu.CompilerParams(vmem_limit_bytes=VMEM_LIMIT),
        cost_estimate=small_cost(),
        name="rows_product",
    )(left, right)


def block_diagonal(weights):
    groups, width, _ = weights.shape
    rows = [
        jnp.pad(weights[b], ((0, 0), (b * width, (groups - 1 - b) * width))) for b in range(groups)
    ]
    return jnp.concatenate(rows, 0)


def row_scale(squares, features):
    return lax.rsqrt(squares / features + norm_eps)[:, None]


def body(
    stream, doc_starts, gain_first, proj_inner, proj_gate, conv_weight, conv_bias, gate_recur,
    gate_input, bias_recur, bias_input, decay_param, proj_out, gain_second, mlp_gate, mlp_up,
    mlp_down, cotangent,
):
    count, own_width = stream.shape
    features = gain_first.shape[0]
    inner_width = proj_inner.shape[1]
    ffn_width = mlp_gate.shape[1]
    groups = gate_recur.shape[0]
    devices = lax.axis_size("seq")
    seq_at = lax.axis_index("seq").astype(jnp.int32).reshape(1)
    column = lax.axis_index("mp") * own_width
    own_first = lax.dynamic_slice_in_dim(gain_first, column, own_width)
    own_second = lax.dynamic_slice_in_dim(gain_second, column, own_width)
    order = block_order()
    onward = [(s, s + 1) for s in range(devices - 1)]
    backward = [(s + 1, s) for s in range(devices - 1)]


    first = LineGather(stream)
    first.first()
    first_scale = row_scale(line_sum(jnp.sum(stream * stream, axis=1)), features)
    starts = doc_starts.astype(f32)
    starts_before = lax.ppermute(starts[count - SUB :], "seq", onward)
    keep_ext = 1.0 - jnp.concatenate([starts_before, starts], 0)
    reach = [keep_ext[SUB:]]
    for k in range(1, 4):
        reach.append(
            (reach[-1] if k > 1 else 1.0) * keep_ext[SUB - k + 1 : SUB - k + 1 + count]
        )
    valid = jnp.broadcast_to(jnp.stack(reach, 0)[:, :, None], (4, count, LANES))
    valid = jnp.pad(valid, ((0, 0), (SUB, SUB), (0, 0)))
    rows = jnp.stack(
        [
            conv_weight[0], conv_weight[1], conv_weight[2], conv_weight[3], conv_bias, bias_recur,
            bias_input, -recur_scale * jax.nn.softplus(-decay_param),
        ],
        0,
    )
    gates = jnp.concatenate([block_diagonal(gate_recur), block_diagonal(gate_input)], 1)
    first.second()
    first.third(gates, valid)

    def first_turn(piece, start):
        return piece * first_scale * lax.dynamic_slice_in_dim(gain_first, start, own_width)

    first_low = assemble(first.pieces(), features, first_turn)
    cot = LineGather(cotangent)
    cot.first(first.far_out)
    inner = matmul(first_low, proj_inner)
    halo = lax.ppermute(inner[count - SUB :], "seq", onward)
    gate_pre = matmul(after(first_low, inner), proj_gate)
    halo = after(halo, gate_pre)
    conv, conv_low, rg, ig, alpha, factor, part, span, last = run_forward(
        inner, halo, valid, rows, gates
    )
    ends = after(lax.all_gather(last, "seq"), cot.beside, cot.near_in)
    cot.second()
    states, mixed_low, enter, *blocks = run_states(
        seq_at, order, ends, part, span, gate_pre, proj_out
    )

    branch = LineScatter(blocks)
    branch.first()
    branch.second(cot.far_in, cot.near_out)
    cot.third()
    branch.third(cot.far_out)
    cot_low = assemble(cot.pieces(), features, lambda piece, start: piece)
    d_hidden = product(cot_low, mlp_down, 2 * LANES, True)
    own_resid = stream + branch.result()

    second = LineGather(own_resid)
    second.first()
    second_scale = row_scale(line_sum(jnp.sum(own_resid * own_resid, axis=1)), features)
    second.second(d_hidden)
    second.third()

    def second_turn(piece, start):
        return piece * second_scale * lax.dynamic_slice_in_dim(gain_second, start, own_width)

    second_low = assemble(second.pieces(), features, second_turn)
    hidden_low, d_gate_ffn, d_up_ffn = feed_forward(second_low, mlp_gate, mlp_up, d_hidden)
    whole_down = rows_product(hidden_low, cot_low, own_width)
    grad_down = ring_scatter(whole_down)
    d_pair = after((d_gate_ffn, d_up_ffn), whole_down)
    d_second_blocks = product_blocks(order, d_pair, [mlp_gate, mlp_up], True)
    turned = LineScatter(d_second_blocks)
    turned.first()
    whole_pair = columns_product(after(second_low, turned.own), [d_gate_ffn, d_up_ffn])
    turned.second(whole_pair)
    whole_pair = after(whole_pair, turned.far_one)
    grad_pair = ring_scatter(whole_pair)
    second_sums, gain_sums = product_sums(
        order, second_low, after(d_second_blocks, turned.far_one)
    )
    second_mean = line_sum(second_sums) / features
    d_gain_second = gain_sums / gain_second
    turned.third(d_gain_second, second_mean)
    mlp_blocks = product_blocks(
        order, [after(hidden_low, turned.far_two, turned.near_one)], [mlp_down], False
    )
    own_d_second = turned.result()
    own_d_resid = (
        cotangent
        + second_scale * (own_second * own_d_second)
        - own_resid * (second_scale * second_scale * second_mean[:, None])
    )
    gathered = LineGather(own_d_resid)
    gathered.first(mlp_blocks)
    gathered.second()
    sent = LineScatter(mlp_blocks)
    sent.first(gathered.near_in, gathered.beside)
    gathered.third(sent.far_one, grad_down)
    sent.second(gathered.near_out)
    branch_low = assemble(gathered.pieces(), features, lambda piece, start: piece)

    d_states, d_gate_low, outgoing = run_turn(
        after(branch_low, sent.far_two, sent.near_one), proj_out, gate_pre, states, span
    )
    leaving = jnp.stack([last[0], jnp.sum(outgoing, axis=0)], 0)
    leaving = after(leaving, sent.prepare())
    sent.third()
    back_ends = after(lax.all_gather(leaving, "seq"), sent.last, sent.near_two)
    saved = dict(alpha=alpha, states=states, conv=conv, rg=rg, ig=ig, factor=factor)
    d_inner_low, tail, head, small = run_backward(
        seq_at, back_ends, d_states, saved, enter, valid, inner, halo, rows, gates, groups
    )
    returned = lax.ppermute(head, "seq", backward)
    whole_out = rows_product(after(mixed_low, head), branch_low, 2 * own_width)
    grad_out = ring_scatter(whole_out)
    returned = after(returned, whole_out)
    tail = tail + jnp.concatenate([jnp.zeros_like(returned), returned], 0)
    d_inner_low = lax.dynamic_update_slice(d_inner_low, tail.astype(bf16), (count - 2 * SUB, 0))
    d_first_blocks = product_blocks(
        order, [d_inner_low, d_gate_low], [proj_inner, proj_gate], True
    )

    final = LineScatter(d_first_blocks)
    final.first(grad_pair)
    whole_first = columns_product(
        after(first_low, final.own), [d_inner_low, d_gate_low]
    )
    first_mean, gain_sums = product_sums(
        order, after(first_low, whole_first), d_first_blocks
    )
    d_gain_first = gain_sums / gain_first
    first_sums = jnp.concatenate([first_mean, d_gain_first, d_gain_second])
    first_sums = first_sums + over_mp(first_sums, PAIRS)
    final.second(whole_first, first_sums, grad_out)
    whole_first = after(whole_first, final.far_one)
    grad_first = ring_scatter(whole_first)
    core = lax.axis_index("seq") & 1
    small = after(small, final.far_one)
    other = swapped(lax.dynamic_index_in_dim(small, 1 - core, 0, False), "seq", 1)
    small = lax.dynamic_index_in_dim(small, core, 0, False) + other
    small = over_chips(small, 2)
    final.third(small)
    first_sums, small = after((first_sums, small), final.far_two, final.near_one)
    first_sums = first_sums + over_mp(first_sums, CROSS)
    first_mean = first_sums[:count] / features
    small = over_chips(small, 4)
    output = after(own_resid, final.far_two) + sent.result()
    gains = sum_over(first_sums[count:], "seq")
    small, gains = after((small, gains), final.last)
    other = swapped(small, "seq", 1)
    small = [jnp.where(core == 0, small, other), jnp.where(core == 0, other, small)]
    own_d_first = final.result()
    grad_stream = (
        own_d_resid
        + first_scale * (own_first * own_d_first)
        - stream * (first_scale * first_scale * first_mean[:, None])
    )
    block_width = inner_width // groups
    half = inner_width // 2
    sums = [
        part[half + b * SUB : half + (b + 1) * SUB] for part in small for b in range(groups // 4)
    ]
    sums = jnp.concatenate(sums, 1)
    grad_gates = [
        jnp.concatenate(
            [part[:half, g * block_width : (g + 1) * block_width] for part in small], 0
        ).reshape(groups, block_width, block_width)
        for g in range(2)
    ]
    grad_decay = sums[7] * (recur_scale * jax.nn.sigmoid(-decay_param))
    return (
        output,
        grad_stream,
        gains[:features],
        grad_first[:, :inner_width],
        grad_first[:, inner_width:],
        sums[:4],
        sums[4],
        grad_gates[0],
        grad_gates[1],
        sums[5],
        sums[6],
        grad_decay,
        grad_out,
        gains[features:],
        grad_pair[:, :ffn_width],
        grad_pair[:, ffn_width:],
        grad_down,
    )


def solution(mesh):
    in_specs = (
        P("seq", "mp"),
        P("seq"),
        P(),
        P(None, "mp"),
        P(None, "mp"),
        P(None, "mp"),
        P("mp"),
        P("mp", None, None),
        P("mp", None, None),
        P("mp"),
        P("mp"),
        P("mp"),
        P("mp", None),
        P(),
        P(None, "mp"),
        P(None, "mp"),
        P("mp", None),
        P("seq", "mp"),
    )
    out_specs = (
        P("seq", "mp"),
        P("seq", "mp"),
        P(),
        P("seq", "mp"),
        P("seq", "mp"),
        P(None, "mp"),
        P("mp"),
        P("mp", None, None),
        P("mp", None, None),
        P("mp"),
        P("mp"),
        P("mp"),
        P(("mp", "seq"), None),
        P(),
        P("seq", "mp"),
        P("seq", "mp"),
        P(("mp", "seq"), None),
    )
    return jax.shard_map(body, mesh=mesh, in_specs=in_specs, out_specs=out_specs, check_vma=False)
```

```python
from functools import partial

import jax
import jax.numpy as jnp
from jax import lax
from jax.experimental import pallas as pl
from jax.experimental.pallas import tpu as pltpu
from jax.sharding import PartitionSpec as P

recur_scale = 8.0
norm_eps = 1e-06
bf16 = jnp.bfloat16
f32 = jnp.float32
LANES = 128
SUB = 8
STEPS = 4
ROWS = 32
VMEM_LIMIT = 56 * 1024 * 1024
VMEM_SMALL = 24 * 1024 * 1024


def matmul(left, right):
    return jnp.dot(left, right, preferred_element_type=f32)


def matmul_nt(left, right):
    return lax.dot_general(left, right, (((1,), (1,)), ((), ())), preferred_element_type=f32)


def matmul_tn(left, right):
    return lax.dot_general(left, right, (((0,), (0,)), ((), ())), preferred_element_type=f32)


PAIRS = ((0, 1), (1, 0), (2, 3), (3, 2))
MIDDLE = ((1, 2), (2, 1))
OUTWARD = ((1, 0), (2, 3))
INWARD = ((0, 1), (3, 2))
CROSS = ((0, 2), (2, 0), (1, 3), (3, 1))


def over_mp(value, pairs):
    return lax.ppermute(value, "mp", list(pairs))


def line_places():
    mine = lax.axis_index("mp")
    half = mine >> 1
    return mine, mine ^ 1, 2 - half, 3 - 3 * half


def after(value, *needed):
    return lax.optimization_barrier((value, needed))[0]


class LineGather:
    def __init__(self, own):
        self.own = own

    def first(self, *needed):
        own = after(self.own, *needed)
        self.beside, self.near_in = over_mp(own, PAIRS), over_mp(own, MIDDLE)
        return self.beside, self.near_in

    def second(self, *needed):
        near, beside = after((self.near_in, self.beside), *needed)
        self.near_out, self.far_in = over_mp(near, OUTWARD), over_mp(beside, MIDDLE)
        return self.near_out, self.far_in

    def third(self, *needed):
        far, _ = after((self.far_in, self.near_out), *needed)
        self.far_out = over_mp(far, OUTWARD)
        return self.far_out

    def pieces(self):
        return self.own, self.beside, self.near_in + self.near_out, self.far_in + self.far_out


class LineScatter:
    def __init__(self, blocks):
        self.far, self.near, self.beside, self.own = blocks

    def first(self, *needed):
        self.far_one = over_mp(after(self.far, *needed), INWARD)
        return self.far_one

    def second(self, *needed):
        far, near = after((self.far + self.far_one, self.near), *needed)
        self.far_two, self.near_one = over_mp(far, MIDDLE), over_mp(near, INWARD)
        return self.far_two, self.near_one

    def prepare(self):
        self.parts = (self.near + self.near_one, self.beside + self.far_two)
        return self.parts

    def third(self, *needed):
        near, last = after(self.prepare(), *needed)
        self.near_two, self.last = over_mp(near, MIDDLE), over_mp(last, PAIRS)
        return self.near_two, self.last

    def result(self):
        return self.own + self.near_two + self.last


def block_order():
    mine, beside, near, far = line_places()
    return jnp.stack([far, near, beside, mine]).astype(jnp.int32)


def line_sum(value):
    value = value + over_mp(value, PAIRS)
    return value + over_mp(value, CROSS)


def swapped(value, axis, bit):
    count = lax.axis_size(axis)
    return lax.ppermute(value, axis, [(d, d ^ bit) for d in range(count)])


def over_chips(value, bit):
    devices = lax.axis_size("seq")
    value = value + swapped(value, "seq", bit)
    while bit > 2 and 2 * bit < devices:
        bit *= 2
        value = value + swapped(value, "seq", bit)
    return value


def sum_over(value, axis):
    bit = 1
    while bit < lax.axis_size(axis):
        value = value + swapped(value, axis, bit)
        bit *= 2
    return value


def assemble(pieces, width, turn):
    rows, own_width = pieces[0].shape
    whole = jnp.zeros((rows, width), bf16)
    for piece, place in zip(pieces, line_places()):
        start = place * own_width
        whole = lax.dynamic_update_slice(whole, turn(piece, start).astype(bf16), (0, start))
    return whole


def wide(value, width):
    return jnp.concatenate([value] * (width // LANES), axis=-1)


def neg_expm1(x, e):
    poly = 1.0 / 40320.0
    for term in (5040.0, 720.0, 120.0, 24.0, 6.0, 2.0, 1.0):
        poly = poly * x + 1.0 / term
    return jnp.where(x > -0.5, -x * poly, 1.0 - e)


def gelu_parts(x):
    scale = 0.7978845608028654
    cube = 0.044715
    squared = x * x
    t = jnp.tanh(scale * (x + cube * x * squared))
    half = 0.5 * (1.0 + t)
    slope = half + 0.5 * x * (1.0 - t * t) * scale * (1.0 + 3.0 * cube * squared)
    return half * x, slope


def group_scan(a, b):
    place = lax.broadcasted_iota(jnp.int32, a.shape, 1)
    for k in (1, 2, 4):
        fits = place >= k
        b = jnp.where(fits, a * pltpu.roll(b, k, 1) + b, b)
        a = jnp.where(fits, a * pltpu.roll(a, k, 1), a)
    return a, b


def group_scan_back(a, b):
    place = lax.broadcasted_iota(jnp.int32, a.shape, 1)
    for k in (1, 2, 4):
        fits = place < SUB - k
        b = jnp.where(fits, a * pltpu.roll(b, SUB - k, 1) + b, b)
        a = jnp.where(fits, a * pltpu.roll(a, SUB - k, 1), a)
    return a, b


def forward_kernel(
    inner_ref, halo_ref, valid_ref, row_ref, gate_ref,
    conv_ref, low_ref, rg_ref, ig_ref, alpha_ref, factor_ref, part_ref, span_ref, last_ref,
    ext_ref, pre_ref,
):
    count, width = inner_ref.shape

    @pl.when(pl.program_id(0) == 0)
    def _():
        ext_ref[pl.ds(0, SUB), :] = halo_ref[...]
        start = lax.broadcasted_iota(jnp.int32, (SUB, width), 0) == 0
        last_ref[...] = jnp.where(start, 1.0, 0.0)

    @pl.when(pl.program_id(0) > 0)
    def _():
        ext_ref[pl.ds(0, SUB), :] = ext_ref[pl.ds(count, SUB), :]

    def fill(i, _):
        r = pl.multiple_of(i * ROWS, ROWS)
        ext_ref[pl.ds(r + SUB, ROWS), :] = inner_ref[pl.ds(r, ROWS), :]
        return 0

    lax.fori_loop(0, count // ROWS, fill, 0)

    def convolve(i, _):
        r = pl.multiple_of(i * ROWS, ROWS)
        window = ext_ref[pl.ds(r, ROWS + SUB), :]
        total = row_ref[0:1, :] * window[SUB:]
        for k in range(1, 4):
            valid = wide(valid_ref[k, pl.ds(r, ROWS), :], width)
            total = total + row_ref[k : k + 1, :] * window[SUB - k : SUB - k + ROWS] * valid
        total = total + row_ref[4:5, :]
        conv_ref[pl.ds(r, ROWS), :] = total
        low_ref[pl.ds(r, ROWS), :] = total.astype(bf16)
        return 0

    lax.fori_loop(0, count // ROWS, convolve, 0)
    pre_ref[...] = jnp.dot(low_ref[...], gate_ref[...], preferred_element_type=f32)

    def scan(i, carry):
        r = pl.multiple_of(i * ROWS, ROWS)
        here = pl.ds(r, ROWS)
        rg = jax.nn.sigmoid(pre_ref[here, :width] + row_ref[5:6, :])
        ig = jax.nn.sigmoid(pre_ref[here, width:] + row_ref[6:7, :])
        log_a = row_ref[7:8, :] * rg
        keep = wide(valid_ref[0, here, :], width)
        a = jnp.exp(log_a)
        root = jnp.sqrt(neg_expm1(2.0 * log_a, a * a))
        factor = (1.0 - keep) + keep * root
        alpha = a * keep
        beta = factor * ig * conv_ref[here, :]
        rg_ref[here, :] = rg
        ig_ref[here, :] = ig
        alpha_ref[here, :] = alpha
        factor_ref[here, :] = factor
        groups = (ROWS // SUB, SUB, width)
        a3, b3 = group_scan(alpha.reshape(groups), beta.reshape(groups))
        state, product = carry
        for g in range(ROWS // SUB):
            part = b3[g] + a3[g] * state
            span = a3[g] * product
            part_ref[pl.ds(r + g * SUB, SUB), :] = part
            span_ref[pl.ds(r + g * SUB, SUB), :] = span
            state, product = part[SUB - 1 : SUB, :], span[SUB - 1 : SUB, :]
        return state, product

    state, product = lax.fori_loop(
        0, count // ROWS, scan, (last_ref[1:2, :], last_ref[0:1, :])
    )
    last_ref[...] = jnp.concatenate([product, state, jnp.zeros((SUB - 2, width), f32)], 0)


def state_kernel(
    mine_ref, order_ref, ends_ref, part_ref, span_ref, gate_ref, weight_ref,
    states_ref, mixed_ref, enter_ref, *block_refs,
):
    devices = ends_ref.shape[0]
    width = part_ref.shape[1]
    entering = jnp.zeros((1, width), f32)
    for d in range(devices):
        ends = ends_ref[d]
        entering = jnp.where(d < mine_ref[0], ends[0:1, :] * entering + ends[1:2, :], entering)
    states = span_ref[...] * entering + part_ref[...]
    states_ref[...] = states
    mixed = (gelu_parts(gate_ref[...])[0] * states).astype(bf16)
    mixed_ref[...] = mixed
    enter_ref[...] = jnp.broadcast_to(entering, enter_ref.shape)
    for k, block_ref in enumerate(block_refs):
        block = block_ref.shape[1]
        columns = pl.ds(pl.multiple_of(order_ref[k] * block, block), block)
        block_ref[...] = jnp.dot(mixed, weight_ref[:, columns], preferred_element_type=f32)


def turn_kernel(
    branch_ref, weight_ref, gate_ref, states_ref, span_ref, dstates_ref, dgate_ref, out_ref
):
    act, slope = gelu_parts(gate_ref[...])
    dmixed = lax.dot_general(
        branch_ref[...], weight_ref[...], (((1,), (1,)), ((), ())), preferred_element_type=f32
    )
    dstates = dmixed * act
    dstates_ref[...] = dstates
    dgate_ref[...] = (dmixed * states_ref[...] * slope).astype(bf16)

    @pl.when(pl.program_id(0) == 0)
    def _():
        out_ref[...] = jnp.zeros_like(out_ref)

    out_ref[...] += jnp.sum(
        (dstates * span_ref[...]).reshape(-1, SUB, dstates.shape[1]), axis=0
    )


def feed_forward_kernel(
    low_ref, gate_ref, up_ref, dhidden_ref, hidden_ref, dgate_ref, dup_ref
):
    low = low_ref[...]
    gate = jnp.dot(low, gate_ref[...], preferred_element_type=f32)
    up = jnp.dot(low, up_ref[...], preferred_element_type=f32)
    act, slope = gelu_parts(gate)
    dhidden = dhidden_ref[...]
    hidden_ref[...] = (act * up).astype(bf16)
    dgate_ref[...] = (dhidden * up * slope).astype(bf16)
    dup_ref[...] = (dhidden * act).astype(bf16)


def blocks_kernel(order_ref, *refs, pairs, transposed):
    for k, block_ref in enumerate(refs[2 * pairs :]):
        block = block_ref.shape[1]
        here = pl.ds(pl.multiple_of(order_ref[k] * block, block), block)
        total = None
        for left_ref, right_ref in zip(refs[:pairs], refs[pairs : 2 * pairs]):
            if transposed:
                part = lax.dot_general(
                    left_ref[...], right_ref[here, :], (((1,), (1,)), ((), ())),
                    preferred_element_type=f32,
                )
            else:
                part = jnp.dot(left_ref[...], right_ref[:, here], preferred_element_type=f32)
            total = part if total is None else total + part
        block_ref[...] = total


def sums_kernel(order_ref, low_ref, *refs):
    row_ref, column_ref = refs[-2:]
    rows = 0.0
    for k, block_ref in enumerate(refs[:-2]):
        block = block_ref.shape[1]
        here = pl.ds(pl.multiple_of(order_ref[k] * block, block), block)
        product = block_ref[...] * low_ref[:, here].astype(f32)
        rows = rows + jnp.sum(product, axis=1, keepdims=True)
        column_ref[:, here] = jnp.sum(product, axis=0, keepdims=True)
    row_ref[...] = rows


def product_kernel(left_ref, right_ref, out_ref, *, transposed):
    contract = (((1,), (1,)), ((), ())) if transposed else (((1,), (0,)), ((), ()))
    out_ref[...] = lax.dot_general(
        left_ref[...], right_ref[...], contract, preferred_element_type=f32
    )


def backward_kernel(
    mine_ref, ends_ref, dstates_ref, alpha_ref, states_ref, before_ref, enter_ref, conv_ref,
    rg_ref, ig_ref, factor_ref, valid_ref, inner_ref, halo_ref, row_ref, gate_ref,
    dinner_ref, tail_ref, head_ref, small_ref,
    dconv_ref, ext_ref, drec_ref, low_ref, whole_ref, flow_ref, sum_ref, *, groups,
):
    devices = ends_ref.shape[0]
    tile, width = alpha_ref.shape
    step = pl.program_id(0)
    base = pl.multiple_of((STEPS - 1 - step) * tile, tile)

    @pl.when(step == 0)
    def _():
        incoming = jnp.zeros((1, width), f32)
        for d in reversed(range(devices)):
            ends = ends_ref[d]
            incoming = jnp.where(d > mine_ref[0], ends[0:1, :] * incoming + ends[1:2, :], incoming)
        flow_ref[...] = jnp.broadcast_to(incoming, (SUB, width))
        sum_ref[...] = jnp.zeros_like(sum_ref)
        dconv_ref[pl.ds(0, SUB), :] = jnp.zeros((SUB, width), f32)
        dconv_ref[pl.ds(STEPS * tile + SUB, SUB), :] = jnp.zeros((SUB, width), f32)
        ext_ref[pl.ds(0, SUB), :] = halo_ref[...]

    parts = (ROWS // SUB, SUB, width)
    place = lax.broadcasted_iota(jnp.int32, (SUB, width), 0)

    def fold(value):
        return jnp.sum(value.reshape(parts), axis=0)

    def back(turn, carry):
        flow, decay, bias_r, bias_i = carry
        i = tile // ROWS - 1 - turn
        r = pl.multiple_of(i * ROWS, ROWS)
        here = pl.ds(r, ROWS)
        there = pl.ds(pl.multiple_of(base + r, ROWS), ROWS)
        padded = pl.ds(pl.multiple_of(base + r + SUB, SUB), ROWS)
        ext_ref[padded, :] = inner_ref[here, :]
        alpha = alpha_ref[here, :]
        dstates = dstates_ref[here, :]
        a3, b3 = group_scan_back(alpha.reshape(parts), (alpha * dstates).reshape(parts))
        d3 = dstates.reshape(parts)
        totals = [None] * (ROWS // SUB)
        for g in reversed(range(ROWS // SUB)):
            flows = b3[g] + a3[g] * flow
            later = jnp.where(place == SUB - 1, flow, pltpu.roll(flows, SUB - 1, 0))
            totals[g] = d3[g] + later
            flow = flows[0:1, :]
        total = jnp.concatenate(totals, 0)
        earlier = jnp.where(step == STEPS - 1, enter_ref[...], before_ref[...])
        inside = states_ref[pl.ds(pl.multiple_of(jnp.maximum(r - SUB, 0), SUB), SUB), :]
        window = jnp.concatenate([jnp.where(i == 0, earlier, inside), states_ref[here, :]], 0)
        prior = window[SUB - 1 : SUB - 1 + ROWS]
        rg = rg_ref[here, :]
        ig = ig_ref[here, :]
        factor = factor_ref[here, :]
        conv = conv_ref[here, :]
        low_ref[there, :] = conv.astype(bf16)
        gain = total * factor
        dconv_ref[padded, :] = gain * ig
        dinput = (gain * conv * ig * (1.0 - ig)).astype(bf16)
        dlog = alpha * (total * prior - total * ig * conv * alpha / factor)
        drecur = (dlog * row_ref[7:8, :] * rg * (1.0 - rg)).astype(bf16)
        drec_ref[there, :width] = drecur
        drec_ref[there, width:] = dinput
        return (
            flow,
            decay + fold(dlog * rg),
            bias_r + fold(drecur.astype(f32)),
            bias_i + fold(dinput.astype(f32)),
        )

    flow, *totals = lax.fori_loop(
        0, tile // ROWS, back, (flow_ref[0:1, :], sum_ref[0], sum_ref[1], sum_ref[2])
    )
    flow_ref[...] = jnp.broadcast_to(flow, (SUB, width))
    for k in range(3):
        sum_ref[k] = totals[k]
    dconv_ref[pl.ds(pl.multiple_of(base + SUB, SUB), tile), :] += lax.dot_general(
        drec_ref[pl.ds(base, tile), :], gate_ref[...], (((1,), (1,)), ((), ())),
        preferred_element_type=f32,
    )

    @pl.when(step == STEPS - 1)
    def _():
        backward_end(
            valid_ref, row_ref, dinner_ref, tail_ref, head_ref, small_ref, dconv_ref, ext_ref,
            drec_ref, low_ref, whole_ref, sum_ref, groups,
        )


def backward_end(
    valid_ref, row_ref, dinner_ref, tail_ref, head_ref, small_ref, dconv_ref, ext_ref,
    drec_ref, low_ref, whole_ref, sum_ref, groups,
):
    count, width = dinner_ref.shape
    blocks = count // ROWS
    zero = jnp.zeros((SUB, width), f32)

    def fold(value):
        return jnp.sum(value.reshape(ROWS // SUB, SUB, width), axis=0)

    def spread_back(window, r, rows):
        total = row_ref[0:1, :] * window[:rows]
        for k in range(1, 4):
            valid = wide(valid_ref[k, pl.ds(r, rows + SUB), :], width)
            total = total + row_ref[k : k + 1, :] * (window * valid)[k : k + rows]
        return total

    head_ref[...] = spread_back(dconv_ref[pl.ds(0, 2 * SUB), :], 0, SUB)

    def finish(i, carry):
        r = pl.multiple_of(i * ROWS, ROWS)
        window = dconv_ref[pl.ds(r + SUB, ROWS + SUB), :]
        total = spread_back(window, r + SUB, ROWS)
        dinner_ref[pl.ds(r, ROWS), :] = total.astype(bf16)

        @pl.when(i == blocks - 1)
        def _():
            tail_ref[...] = total[ROWS - 2 * SUB :]

        dconv = window[:ROWS]
        inputs = ext_ref[pl.ds(r, ROWS + SUB), :]
        sums = [fold(dconv * inputs[SUB:])]
        for k in range(1, 4):
            valid = wide(valid_ref[k, pl.ds(r + SUB, ROWS), :], width)
            sums.append(fold(dconv * valid * inputs[SUB - k : SUB - k + ROWS]))
        sums.append(fold(dconv))
        return tuple(c + s for c, s in zip(carry, sums))

    sums = lax.fori_loop(0, blocks, finish, (zero,) * 5)
    sums = jnp.concatenate(
        [jnp.sum(s, axis=0, keepdims=True) for s in (*sums, sum_ref[1], sum_ref[2], sum_ref[0])], 0
    )
    whole_ref[...] = lax.dot_general(
        low_ref[...], drec_ref[...], (((0,), (0,)), ((), ())),
        preferred_element_type=f32,
    )
    block = width // groups
    left = lax.broadcasted_iota(jnp.int32, (block, width), 1) < block

    def turned(value, shift):
        return pltpu.roll(value, shift % width, 1) if shift % width else value

    for b in range(groups):
        here = slice(b * block, (b + 1) * block)
        recur = turned(whole_ref[here, :width], -b * block)
        entry = turned(whole_ref[here, width:], block - b * block)
        small_ref[2 * b // groups, b % (groups // 2) * block : (b % (groups // 2) + 1) * block, :] = (
            jnp.where(left, recur, entry)[:, : 2 * block]
        )
    for h in range(2):
        for b in range(groups // 4):
            small_ref[h, width // 2 + b * SUB : width // 2 + (b + 1) * SUB, :] = turned(
                sums, -2 * (h * (groups // 4) + b) * block
            )[:, : 2 * block]


def vmem(count=1):
    return [pl.BlockSpec(memory_space=pltpu.VMEM)] * count


def shape(dims, kind=f32):
    return jax.ShapeDtypeStruct(dims, kind)


def small_cost():
    return pl.CostEstimate(flops=1000, bytes_accessed=1000, transcendentals=0)


def run_forward(inner, halo, valid, rows, gates):
    count, width = inner.shape
    block = count // STEPS
    full = shape((count, width))
    tile = pl.BlockSpec((block, width), lambda i: (i, 0))
    small = pl.BlockSpec((SUB, width), lambda i: (0, 0))
    return pl.pallas_call(
        forward_kernel,
        grid=(STEPS,),
        out_shape=(full, shape((count, width), bf16)) + (full,) * 6 + (shape((SUB, width)),),
        in_specs=[
            tile, small,
            pl.BlockSpec((4, block, LANES), lambda i: (0, i, 0)),
            small,
            pl.BlockSpec(gates.shape, lambda i: (0, 0)),
        ],
        out_specs=(tile,) * 8 + (small,),
        scratch_shapes=[
            pltpu.VMEM((block + SUB, width), f32),
            pltpu.VMEM((block, 2 * width), f32),
        ],
        compiler_params=pltpu.CompilerParams(vmem_limit_bytes=VMEM_LIMIT),
        cost_estimate=small_cost(),
        name="recurrence_forward",
    )(inner, halo, valid, rows, gates)


def run_states(mine, order, ends, part, span, gate_pre, weight):
    count, width = part.shape
    features = weight.shape[1]
    block = count // 4
    tile = pl.BlockSpec((block, width), lambda i, m, o: (i, 0))
    out = pl.BlockSpec((block, features // 4), lambda i, m, o: (i, 0))
    return pl.pallas_call(
        state_kernel,
        grid_spec=pltpu.PrefetchScalarGridSpec(
            num_scalar_prefetch=2,
            grid=(4,),
            in_specs=[
                pl.BlockSpec(ends.shape, lambda i, m, o: (0, 0, 0)),
                tile, tile, tile,
                pl.BlockSpec(weight.shape, lambda i, m, o: (0, 0)),
            ],
            out_specs=(tile, tile, pl.BlockSpec((SUB, width), lambda i, m, o: (0, 0))) + (out,) * 4,
        ),
        out_shape=(
            shape((count, width)), shape((count, width), bf16), shape((SUB, width)),
        ) + (shape((count, features // 4)),) * 4,
        compiler_params=pltpu.CompilerParams(vmem_limit_bytes=VMEM_SMALL),
        cost_estimate=small_cost(),
        name="recurrence_states",
    )(mine, order, ends, part, span, gate_pre, weight)


def run_turn(branch, weight, gate_pre, states, span):
    count, width = states.shape
    features = branch.shape[1]
    block = count // 4
    tile = pl.BlockSpec((block, width), lambda i: (i, 0))
    return pl.pallas_call(
        turn_kernel,
        grid=(4,),
        out_shape=(
            shape((count, width)), shape((count, width), bf16), shape((SUB, width)),
        ),
        in_specs=[
            pl.BlockSpec((block, features), lambda i: (i, 0)),
            pl.BlockSpec(weight.shape, lambda i: (0, 0)),
        ] + [tile] * 3,
        out_specs=(tile, tile, pl.BlockSpec((SUB, width), lambda i: (0, 0))),
        compiler_params=pltpu.CompilerParams(vmem_limit_bytes=VMEM_SMALL),
        cost_estimate=small_cost(),
        name="recurrence_turn",
    )(branch, weight, gate_pre, states, span)


def feed_forward(low, gate, up, dhidden):
    count, features = low.shape
    hidden = gate.shape[1]
    block = 512
    tile = pl.BlockSpec((count, block), lambda i: (0, i))
    weight = pl.BlockSpec((features, block), lambda i: (0, i))
    return pl.pallas_call(
        feed_forward_kernel,
        grid=(hidden // block,),
        in_specs=[pl.BlockSpec((count, features), lambda i: (0, 0)), weight, weight, tile],
        out_specs=(tile,) * 3,
        out_shape=(shape((count, hidden), bf16),) * 3,
        compiler_params=pltpu.CompilerParams(vmem_limit_bytes=VMEM_LIMIT),
        cost_estimate=small_cost(),
        name="feed_forward",
    )(low, gate, up, dhidden)


def product_blocks(order, lefts, rights, transposed):
    count = lefts[0].shape[0]
    features = rights[0].shape[0 if transposed else 1]
    return pl.pallas_call(
        partial(blocks_kernel, pairs=len(lefts), transposed=transposed),
        out_shape=(shape((count, features // 4)),) * 4,
        in_specs=[pl.BlockSpec(memory_space=pltpu.SMEM)] + vmem(2 * len(lefts)),
        out_specs=tuple(vmem(4)),
        compiler_params=pltpu.CompilerParams(vmem_limit_bytes=VMEM_LIMIT),
        cost_estimate=small_cost(),
        name="product_blocks",
    )(order, *lefts, *rights)


def product_sums(order, low, blocks):
    count, features = low.shape
    row, column = pl.pallas_call(
        sums_kernel,
        out_shape=(shape((count, 1)), shape((1, features))),
        in_specs=[pl.BlockSpec(memory_space=pltpu.SMEM)] + vmem(5),
        out_specs=tuple(vmem(2)),
        compiler_params=pltpu.CompilerParams(vmem_limit_bytes=VMEM_LIMIT),
        cost_estimate=small_cost(),
        name="product_sums",
    )(order, low, *blocks)
    return row[:, 0], column[0]


def product(left, right, block, transposed=False):
    count, inner = left.shape
    width = right.shape[0 if transposed else 1]
    right_tile = (
        pl.BlockSpec((block, inner), lambda i: (i, 0))
        if transposed
        else pl.BlockSpec((inner, block), lambda i: (0, i))
    )
    return pl.pallas_call(
        partial(product_kernel, transposed=transposed),
        grid=(width // block,),
        in_specs=[pl.BlockSpec(left.shape, lambda i: (0, 0)), right_tile],
        out_specs=pl.BlockSpec((count, block), lambda i: (0, i)),
        out_shape=shape((count, width)),
        compiler_params=pltpu.CompilerParams(vmem_limit_bytes=VMEM_LIMIT),
        cost_estimate=small_cost(),
        name="product",
    )(left, right)


def run_backward(mine, ends, dstates, saved, enter, valid, inner, halo, rows, gates, groups):
    count, width = dstates.shape
    block = count // STEPS
    groups_of_rows = block // SUB
    tile = pl.BlockSpec((block, width), lambda j, m: (STEPS - 1 - j, 0))
    before = pl.BlockSpec(
        (SUB, width), lambda j, m: (jnp.maximum((STEPS - 1 - j) * groups_of_rows - 1, 0), 0)
    )

    def whole(dims):
        return pl.BlockSpec(dims, lambda j, m: (0,) * len(dims))

    small = whole((SUB, width))
    outs = (
        ((count, width), bf16), ((2 * SUB, width), f32), ((SUB, width), f32),
        ((2, width // 2 + SUB * groups // 4, 2 * width // groups), f32),
    )
    return pl.pallas_call(
        partial(backward_kernel, groups=groups),
        grid_spec=pltpu.PrefetchScalarGridSpec(
            num_scalar_prefetch=1,
            grid=(STEPS,),
            in_specs=[
                whole(ends.shape), tile, tile, tile, before, small, tile, tile, tile, tile,
                whole(valid.shape), tile, small, small, whole(gates.shape),
            ],
            out_specs=tuple(whole(dims) for dims, _ in outs),
            scratch_shapes=[
                pltpu.VMEM((count + 2 * SUB, width), f32),
                pltpu.VMEM((count + SUB, width), f32),
                pltpu.VMEM((count, 2 * width), bf16),
                pltpu.VMEM((count, width), bf16),
                pltpu.VMEM((width, 2 * width), f32),
                pltpu.VMEM((SUB, width), f32),
                pltpu.VMEM((3, SUB, width), f32),
            ],
        ),
        out_shape=tuple(shape(*out) for out in outs),
        compiler_params=pltpu.CompilerParams(vmem_limit_bytes=VMEM_LIMIT),
        cost_estimate=small_cost(),
        name="recurrence_backward",
    )(
        mine, ends, dstates, saved["alpha"], saved["states"], saved["states"], enter,
        saved["conv"], saved["rg"], saved["ig"], saved["factor"], valid, inner, halo, rows, gates,
    )


def columns_product_kernel(ring_ref, left_ref, *refs):
    out_ref = refs[-1]
    left = left_ref[...].T
    start = 0
    for right_ref in refs[:-1]:
        width = right_ref.shape[1]
        out_ref[:, start : start + width] = jnp.dot(
            left, right_ref[...], preferred_element_type=f32
        )
        start += width


def ring_order():
    devices = lax.axis_size("seq")
    return [0, 1, 3, 2, 6, 7, 5, 4] if devices == 8 else list(range(devices))


def ring_scatter(value):
    return lax.psum_scatter(
        value, "seq", scatter_dimension=0, axis_index_groups=[ring_order()], tiled=True
    )


def columns_product(left, rights):
    rows, columns = left.shape
    width = sum(right.shape[1] for right in rights)
    ring = ring_order()
    block = columns // len(ring)
    if block % LANES:
        whole = matmul_tn(left, jnp.concatenate(rights, 1)).reshape(len(ring), block, width)
        return jnp.concatenate([whole[d] for d in ring], 0)
    return pl.pallas_call(
        columns_product_kernel,
        grid_spec=pltpu.PrefetchScalarGridSpec(
            num_scalar_prefetch=1,
            grid=(len(ring),),
            in_specs=[pl.BlockSpec((rows, block), lambda j, ring: (0, ring[j]))]
            + [pl.BlockSpec(right.shape, lambda j, ring: (0, 0)) for right in rights],
            out_specs=pl.BlockSpec((block, width), lambda j, ring: (j, 0)),
        ),
        out_shape=shape((columns, width)),
        compiler_params=pltpu.CompilerParams(vmem_limit_bytes=VMEM_LIMIT),
        cost_estimate=small_cost(),
        name="columns_product",
    )(jnp.array(ring, jnp.int32), left, *rights)


def rows_product_kernel(left_ref, right_ref, out_ref, whole_ref, *, ring):
    whole_ref[...] = jnp.dot(left_ref[...].T, right_ref[...], preferred_element_type=f32)
    block = out_ref.shape[0] // len(ring)
    for j, d in enumerate(ring):
        out_ref[j * block : (j + 1) * block, :] = whole_ref[d * block : (d + 1) * block, :]


def rows_product(left, right, width):
    rows, columns = left.shape
    return pl.pallas_call(
        partial(rows_product_kernel, ring=ring_order()),
        grid=(right.shape[1] // width,),
        in_specs=[
            pl.BlockSpec(left.shape, lambda n: (0, 0)),
            pl.BlockSpec((rows, width), lambda n: (0, n)),
        ],
        out_specs=pl.BlockSpec((columns, width), lambda n: (0, n)),
        scratch_shapes=[pltpu.VMEM((columns, width), f32)],
        out_shape=shape((columns, right.shape[1])),
        compiler_params=pltpu.CompilerParams(vmem_limit_bytes=VMEM_LIMIT),
        cost_estimate=small_cost(),
        name="rows_product",
    )(left, right)


def block_diagonal(weights):
    groups, width, _ = weights.shape
    rows = [
        jnp.pad(weights[b], ((0, 0), (b * width, (groups - 1 - b) * width))) for b in range(groups)
    ]
    return jnp.concatenate(rows, 0)


def row_scale(squares, features):
    return lax.rsqrt(squares / features + norm_eps)[:, None]


def body(
    stream, doc_starts, gain_first, proj_inner, proj_gate, conv_weight, conv_bias, gate_recur,
    gate_input, bias_recur, bias_input, decay_param, proj_out, gain_second, mlp_gate, mlp_up,
    mlp_down, cotangent,
):
    count, own_width = stream.shape
    features = gain_first.shape[0]
    inner_width = proj_inner.shape[1]
    ffn_width = mlp_gate.shape[1]
    groups = gate_recur.shape[0]
    devices = lax.axis_size("seq")
    seq_at = lax.axis_index("seq").astype(jnp.int32).reshape(1)
    column = lax.axis_index("mp") * own_width
    own_first = lax.dynamic_slice_in_dim(gain_first, column, own_width)
    own_second = lax.dynamic_slice_in_dim(gain_second, column, own_width)
    order = block_order()
    onward = [(s, s + 1) for s in range(devices - 1)]
    backward = [(s + 1, s) for s in range(devices - 1)]


    first = LineGather(stream)
    first.first()
    first_scale = row_scale(line_sum(jnp.sum(stream * stream, axis=1)), features)
    starts = doc_starts.astype(f32)
    starts_before = lax.ppermute(starts[count - SUB :], "seq", onward)
    keep_ext = 1.0 - jnp.concatenate([starts_before, starts], 0)
    reach = [keep_ext[SUB:]]
    for k in range(1, 4):
        reach.append(
            (reach[-1] if k > 1 else 1.0) * keep_ext[SUB - k + 1 : SUB - k + 1 + count]
        )
    valid = jnp.broadcast_to(jnp.stack(reach, 0)[:, :, None], (4, count, LANES))
    valid_pad = jnp.pad(valid, ((0, 0), (SUB, SUB), (0, 0)))
    rows = jnp.stack(
        [
            conv_weight[0], conv_weight[1], conv_weight[2], conv_weight[3], conv_bias, bias_recur,
            bias_input, -recur_scale * jax.nn.softplus(-decay_param),
        ],
        0,
    )
    gates = jnp.concatenate([block_diagonal(gate_recur), block_diagonal(gate_input)], 1)
    first.second()
    first.third(gates, valid, valid_pad)

    def first_turn(piece, start):
        return piece * first_scale * lax.dynamic_slice_in_dim(gain_first, start, own_width)

    first_low = assemble(first.pieces(), features, first_turn)
    cot = LineGather(cotangent)
    cot.first(first.far_out)
    inner = matmul(first_low, proj_inner)
    halo = lax.ppermute(inner[count - SUB :], "seq", onward)
    gate_pre = matmul(after(first_low, inner), proj_gate)
    halo = after(halo, gate_pre)
    conv, conv_low, rg, ig, alpha, factor, part, span, last = run_forward(
        inner, halo, valid, rows, gates
    )
    ends = after(lax.all_gather(last, "seq"), cot.beside, cot.near_in)
    cot.second()
    states, mixed_low, enter, *blocks = run_states(
        seq_at, order, ends, part, span, gate_pre, proj_out
    )

    branch = LineScatter(blocks)
    branch.first()
    branch.second(cot.far_in, cot.near_out)
    cot.third()
    branch.third(cot.far_out)
    cot_low = assemble(cot.pieces(), features, lambda piece, start: piece)
    d_hidden = product(cot_low, mlp_down, 2 * LANES, True)
    own_resid = stream + branch.result()

    second = LineGather(own_resid)
    second.first()
    second_scale = row_scale(line_sum(jnp.sum(own_resid * own_resid, axis=1)), features)
    second.second(d_hidden)
    second.third()

    def second_turn(piece, start):
        return piece * second_scale * lax.dynamic_slice_in_dim(gain_second, start, own_width)

    second_low = assemble(second.pieces(), features, second_turn)
    hidden_low, d_gate_ffn, d_up_ffn = feed_forward(second_low, mlp_gate, mlp_up, d_hidden)
    whole_down = rows_product(hidden_low, cot_low, own_width)
    grad_down = ring_scatter(whole_down)
    d_pair = after((d_gate_ffn, d_up_ffn), whole_down)
    d_second_blocks = product_blocks(order, d_pair, [mlp_gate, mlp_up], True)
    turned = LineScatter(d_second_blocks)
    turned.first()
    whole_pair = columns_product(after(second_low, turned.own), [d_gate_ffn, d_up_ffn])
    turned.second(whole_pair)
    whole_pair = after(whole_pair, turned.far_one)
    grad_pair = ring_scatter(whole_pair)
    second_sums, gain_sums = product_sums(
        order, second_low, after(d_second_blocks, turned.far_one)
    )
    second_mean = line_sum(second_sums) / features
    d_gain_second = gain_sums / gain_second
    turned.third(d_gain_second, second_mean)
    mlp_blocks = product_blocks(
        order, [after(hidden_low, turned.far_two, turned.near_one)], [mlp_down], False
    )
    own_d_second = turned.result()
    own_d_resid = (
        cotangent
        + second_scale * (own_second * own_d_second)
        - own_resid * (second_scale * second_scale * second_mean[:, None])
    )
    gathered = LineGather(own_d_resid)
    gathered.first(mlp_blocks)
    gathered.second()
    sent = LineScatter(mlp_blocks)
    sent.first(gathered.near_in, gathered.beside)
    gathered.third(sent.far_one, grad_down)
    sent.second(gathered.near_out)
    branch_low = assemble(gathered.pieces(), features, lambda piece, start: piece)

    d_states, d_gate_low, outgoing = run_turn(
        after(branch_low, sent.far_two, sent.near_one), proj_out, gate_pre, states, span
    )
    leaving = jnp.stack([last[0], jnp.sum(outgoing, axis=0)], 0)
    leaving = after(leaving, sent.prepare())
    sent.third()
    back_ends = after(lax.all_gather(leaving, "seq"), sent.last, sent.near_two)
    saved = dict(alpha=alpha, states=states, conv=conv, rg=rg, ig=ig, factor=factor)
    d_inner_low, tail, head, small = run_backward(
        seq_at, back_ends, d_states, saved, enter, valid_pad, inner, halo, rows, gates, groups
    )
    returned = lax.ppermute(head, "seq", backward)
    whole_out = rows_product(after(mixed_low, head), branch_low, 2 * own_width)
    grad_out = ring_scatter(whole_out)
    returned = after(returned, whole_out)
    tail = tail + jnp.concatenate([jnp.zeros_like(returned), returned], 0)
    d_inner_low = lax.dynamic_update_slice(d_inner_low, tail.astype(bf16), (count - 2 * SUB, 0))
    d_first_blocks = product_blocks(
        order, [d_inner_low, d_gate_low], [proj_inner, proj_gate], True
    )

    final = LineScatter(d_first_blocks)
    final.first(grad_pair)
    whole_first = columns_product(
        after(first_low, final.own), [d_inner_low, d_gate_low]
    )
    first_mean, gain_sums = product_sums(
        order, after(first_low, whole_first), d_first_blocks
    )
    d_gain_first = gain_sums / gain_first
    first_sums = jnp.concatenate([first_mean, d_gain_first, d_gain_second])
    core = lax.axis_index("seq") & 1
    other = lax.dynamic_index_in_dim(small, 1 - core, 0, False)
    small = lax.dynamic_index_in_dim(small, core, 0, False)
    whole_first, first_sums, other, small = after(
        (whole_first, first_sums, other, small), final.far_one
    )
    grad_first = ring_scatter(whole_first)
    first_sums = first_sums + over_mp(first_sums, PAIRS)
    final.second(first_sums, grad_out)
    small = small + swapped(other, "seq", 1)
    small = over_chips(small, 2)
    final.third(small)
    first_sums, small = after((first_sums, small), final.far_two, final.near_one)
    first_sums = first_sums + over_mp(first_sums, CROSS)
    first_mean = first_sums[:count] / features
    small = over_chips(small, 4)
    output = after(own_resid, final.far_two) + sent.result()
    gains = sum_over(first_sums[count:], "seq")
    small, gains = after((small, gains), final.last)
    other = swapped(small, "seq", 1)
    small = [jnp.where(core == 0, small, other), jnp.where(core == 0, other, small)]
    own_d_first = final.result()
    grad_stream = (
        own_d_resid
        + first_scale * (own_first * own_d_first)
        - stream * (first_scale * first_scale * first_mean[:, None])
    )
    block_width = inner_width // groups
    half = inner_width // 2
    sums = [
        part[half + b * SUB : half + (b + 1) * SUB] for part in small for b in range(groups // 4)
    ]
    sums = jnp.concatenate(sums, 1)
    grad_gates = [
        jnp.concatenate(
            [part[:half, g * block_width : (g + 1) * block_width] for part in small], 0
        ).reshape(groups, block_width, block_width)
        for g in range(2)
    ]
    grad_decay = sums[7] * (recur_scale * jax.nn.sigmoid(-decay_param))
    return (
        output,
        grad_stream,
        gains[:features],
        grad_first[:, :inner_width],
        grad_first[:, inner_width:],
        sums[:4],
        sums[4],
        grad_gates[0],
        grad_gates[1],
        sums[5],
        sums[6],
        grad_decay,
        grad_out,
        gains[features:],
        grad_pair[:, :ffn_width],
        grad_pair[:, ffn_width:],
        grad_down,
    )


def solution(mesh):
    in_specs = (
        P("seq", "mp"),
        P("seq"),
        P(),
        P(None, "mp"),
        P(None, "mp"),
        P(None, "mp"),
        P("mp"),
        P("mp", None, None),
        P("mp", None, None),
        P("mp"),
        P("mp"),
        P("mp"),
        P("mp", None),
        P(),
        P(None, "mp"),
        P(None, "mp"),
        P("mp", None),
        P("seq", "mp"),
    )
    out_specs = (
        P("seq", "mp"),
        P("seq", "mp"),
        P(),
        P("seq", "mp"),
        P("seq", "mp"),
        P(None, "mp"),
        P("mp"),
        P("mp", None, None),
        P("mp", None, None),
        P("mp"),
        P("mp"),
        P("mp"),
        P(("mp", "seq"), None),
        P(),
        P("seq", "mp"),
        P("seq", "mp"),
        P(("mp", "seq"), None),
    )
    return jax.shard_map(body, mesh=mesh, in_specs=in_specs, out_specs=out_specs, check_vma=False)
```
